32 devices in a mesh: dp: 16 (over z, x, core), tensor: 2 (over y).
Axes of the slice: x: 2, y: 2, z: 4, core: 2. Of those that a mesh axis runs over, the one named last changes fastest.
Arguments:
- src_embed: bfloat16 [512, 16, 768], P('tensor', 'dp'), may hold values from -6 to 6
- tgt_embed: bfloat16 [256, 16, 768], P('tensor', 'dp'), may hold values from -6 to 6
- src_mask: int32 [16, 512], P('dp'), may hold values from 0 to 1, as said below
- tgt_mask: int32 [16, 256], P('dp'), may hold values from 0 to 1, as said below
- objective: int32 [16], P('dp'), may hold values from 0 to 1
- loss_mask: int32 [16, 256], P('dp', 'tensor'), may hold values 0 or 1
- enc_cot: bfloat16 [512, 16, 768], P('tensor', 'dp'), may hold values from -6 to 6
- dec_cot: bfloat16 [256, 16, 768], P('tensor', 'dp'), may hold values from -6 to 6
- norm_gain: float32 [5, 768], replicated, may hold values from 0.1 to 1.9
- norm_bias: float32 [5, 768], replicated, may hold values from -4 to 4
- attn_in: bfloat16 [3, 3, 768, 768], P(None, None, None, 'tensor'), may hold values from -0.21875 to 0.21875
- attn_in_bias: float32 [3, 2, 768], P(None, None, 'tensor'), may hold values from -4 to 4
- attn_out: bfloat16 [3, 768, 768], P(None, 'tensor'), may hold values from -0.625 to 0.625
- attn_out_bias: float32 [3, 768], replicated, may hold values from -4 to 4
- ffn_in: bfloat16 [2, 768, 3072], P(None, None, 'tensor'), may hold values from -0.21875 to 0.21875
- ffn_in_bias: float32 [2, 3072], P(None, 'tensor'), may hold values from -4 to 4
- ffn_out: bfloat16 [2, 3072, 768], P(None, 'tensor'), may hold values from -0.109375 to 0.109375
- ffn_out_bias: float32 [2, 768], replicated, may hold values from -4 to 4
Outputs:
- enc_out: bfloat16 [512, 16, 768], P('tensor', 'dp')
- dec_out: bfloat16 [256, 16, 768], P('tensor', 'dp')
- src_grad: float32 [512, 16, 768], P('tensor', 'dp')
- tgt_grad: float32 [256, 16, 768], P('tensor', 'dp')
- norm_gain_grad: float32 [5, 768], replicated
- norm_bias_grad: float32 [5, 768], replicated
- attn_in_grad: float32 [3, 3, 768, 768], P(None, None, None, 'tensor')
- attn_in_bias_grad: float32 [3, 2, 768], P(None, None, 'tensor')
- attn_out_grad: float32 [3, 768, 768], P(None, 'tensor')
- attn_out_bias_grad: float32 [3, 768], replicated
- ffn_in_grad: float32 [2, 768, 3072], P(None, None, 'tensor')
- ffn_in_bias_grad: float32 [2, 3072], P(None, 'tensor')
- ffn_out_grad: float32 [2, 3072, 768], P(None, 'tensor')
- ffn_out_bias_grad: float32 [2, 768], replicated
The draws below stay inside these ranges and needn't reach their ends.
Inputs may be any that keep to these rules, and one draw needn't show every extreme that they name: `src_mask`: each example's ones form a prefix longer than 256; example 0 has exactly 257 ones and the last example has 512. `tgt_mask`: each example's ones form a prefix longer than 128; example 0 has exactly 129 ones and the last example has 256.
All inputs are finite; a program needn't handle non-finite values. No bound on the sum of `loss_mask` on one device may be relied on, other than what follows from the above.
Results may differ from the reference program's by a relative error of at most 0.025.
Values may be sent and summed in bfloat16 or wider, within the bound.
No kernel may reach another device: no remote copies, remote signals or barrier semaphores. Data moves between devices by JAX's collectives and lax.ppermute only.
A program may use at most 192 MiB of HBM per device.

```python
import jax
import jax.numpy as jnp
from jax import lax

D = 768
HEAD = 64
FF = 3072
SRC = 512
TGT = 256
EXAMPLES = 16


def prefix_mask(key, salt, length):
    lengths = jax.random.randint(jax.random.fold_in(key, salt), (EXAMPLES,), length // 2 + 1, length + 1)
    index = jnp.arange(EXAMPLES)
    lengths = jnp.where(index == 0, length // 2 + 1, lengths)
    lengths = jnp.where(index == EXAMPLES - 1, length, lengths)
    return (jnp.arange(length)[None, :] < lengths[:, None]).astype(jnp.int32)


def draw_src_mask(key, part):
    return prefix_mask(key, 101, SRC)


def draw_tgt_mask(key, part):
    return prefix_mask(key, 202, TGT)


def place_ends(array, stream_key, least, high):
    longest = array.shape.index(max(array.shape))
    spots = []
    for shift in (0, 1):
        where = [jax.random.randint(jax.random.fold_in(stream_key, axis), (), 0, length) for axis, length in enumerate(array.shape)]
        where[longest] = (where[longest] + shift) % array.shape[longest]
        spots.append(tuple(where))
    return array.at[spots[0]].set(least).at[spots[1]].set(high)


def level_of(stream_key, extent, cuts, least, largest):
    loudness = 1.0
    for dim, blocks in cuts:
        steps = jax.random.uniform(jax.random.fold_in(jax.random.fold_in(stream_key, 6), dim), (blocks,), jnp.float32, least / len(cuts), largest / len(cuts))
        loudness = loudness * jnp.repeat(jnp.exp(steps), extent[dim] // blocks).reshape((-1,) + (1,) * (len(extent) - 1 - dim))
    return loudness


def centred(own_key, shape, width, limit, pieces=(), held_as=jnp.bfloat16):
    loudness = level_of(own_key, shape, pieces, -0.22, 0.18) if pieces else 1.0
    drawn = jax.random.normal(own_key, shape, jnp.float32) * width * loudness
    return jnp.minimum(jnp.maximum(drawn, -limit), limit).astype(held_as)


def setup_inputs(seed: int = 0) -> dict:
    key_of = jax.random.split(jax.random.key(seed), 19)
    return {
        "src_embed": centred(key_of[0], (SRC, EXAMPLES, D), 1.0, 6.0, ((0, 2), (1, 16))),
        "tgt_embed": centred(key_of[1], (TGT, EXAMPLES, D), 1.0, 6.0, ((0, 2), (1, 16))),
        "src_mask": draw_src_mask(jax.random.fold_in(key_of[18], 71), 0),
        "tgt_mask": draw_tgt_mask(jax.random.fold_in(key_of[18], 71), 0),
        "objective": place_ends(jax.random.randint(key_of[4], (EXAMPLES,), 0, 2), jax.random.fold_in(key_of[4], 1), 0, 1).astype(jnp.int32),
        "loss_mask": place_ends((jax.random.randint(key_of[5], (EXAMPLES, TGT), 0, 4) < 3).astype(jnp.int32), jax.random.fold_in(key_of[5], 1), 0, 1),
        "enc_cot": centred(key_of[6], (SRC, EXAMPLES, D), 1.0, 6.0, ((0, 2), (1, 16))),
        "dec_cot": centred(key_of[7], (TGT, EXAMPLES, D), 1.0, 6.0, ((0, 2), (1, 16))),
        "norm_gain": jnp.clip(1.0 + 0.18 * jax.random.normal(key_of[8], (5, D), jnp.float32), 0.1, 1.9),
        "norm_bias": centred(key_of[9], (5, D), 0.3, 4.0, (), jnp.float32),
        "attn_in": centred(key_of[10], (3, 3, D, D), D ** -0.5, 0.21875, ((3, 2),)),
        "attn_in_bias": centred(key_of[11], (3, 2, D), 0.3, 4.0, ((2, 2),), jnp.float32),
        "attn_out": centred(key_of[12], (3, D, D), (D // 8) ** -0.5, 0.625, ((1, 2),)),
        "attn_out_bias": centred(key_of[13], (3, D), 0.3, 4.0, (), jnp.float32),
        "ffn_in": centred(key_of[14], (2, D, FF), D ** -0.5, 0.21875, ((2, 2),)),
        "ffn_in_bias": centred(key_of[15], (2, FF), 0.3, 4.0, ((1, 2),), jnp.float32),
        "ffn_out": centred(key_of[16], (2, FF, D), FF ** -0.5, 0.109375, ((1, 2),)),
        "ffn_out_bias": centred(key_of[17], (2, D), 0.3, 4.0, (), jnp.float32),
    }


@jax.custom_vjp
def low(v):
    return lax.optimization_barrier(v.astype(jnp.bfloat16)).astype(jnp.float32)

@jax.custom_vjp
def low_back(v):
    return v

def low_keep(v):
    return (low(v), None)

def low_pass(kept, grad):
    return (grad,)

def back_keep(v):
    return (v, None)

def back_low(kept, grad):
    return (low(grad),)
low.defvjp(low_keep, low_pass)
low_back.defvjp(back_keep, back_low)
EPSILON = 1e-05
MASKED_SCORE = -1000000000.0

def both_ways(values):
    return low(low_back(values))

def dense(left, right):
    return jnp.dot(left, right, precision=lax.Precision.HIGHEST)

def layer_norm(inputs, norm_scale, offset):
    centre = inputs - lax.optimization_barrier(jnp.mean(inputs, axis=-1, keepdims=True))
    variance = lax.optimization_barrier(jnp.mean(centre * centre, axis=-1, keepdims=True))
    return centre * lax.rsqrt(variance + EPSILON) * norm_scale + offset

def attention(query_in, key_in, in_weights, in_biases, out_weights, out_bias, allowed):
    queries = both_ways(dense(query_in, in_weights[0]) + in_biases[0])
    key_rows = both_ways(dense(key_in, in_weights[1]))
    value_rows = both_ways(dense(key_in, in_weights[2]) + in_biases[1])
    head_count = queries.shape[1] // HEAD
    query_heads = queries.reshape(queries.shape[0], head_count, HEAD)
    key_heads = key_rows.reshape(key_rows.shape[0], head_count, HEAD)
    value_heads = value_rows.reshape(value_rows.shape[0], head_count, HEAD)
    scores = jnp.einsum('qhd,khd->hqk', query_heads, key_heads, precision=lax.Precision.HIGHEST) * HEAD ** (-0.5)
    scores = low_back(jnp.where(allowed, scores, MASKED_SCORE))
    probs = low(jax.nn.softmax(scores, axis=-1))
    mixture = jnp.einsum('hqk,khd->qhd', probs, value_heads, precision=lax.Precision.HIGHEST)
    mixture = both_ways(mixture.reshape(queries.shape))
    return low_back(dense(mixture, out_weights) + out_bias)

def feed_forward(inputs, first_weight, first_bias, second_weight, second_bias):
    hidden = low_back(dense(inputs, first_weight) + first_bias)
    active = low(jax.nn.gelu(hidden))
    return low_back(dense(active, second_weight) + second_bias)

def one_example(params, source, target, source_valid, target_valid):
    norm_gain, norm_bias, attn_in, attn_in_bias, attn_out, attn_out_bias, ffn_in, ffn_in_bias, ffn_out, ffn_out_bias = params
    source_allowed = (source_valid == 1)[None, None, :]
    target_len = target.shape[0]
    causal = lax.broadcasted_iota(jnp.int32, (target_len, target_len), 0) >= lax.broadcasted_iota(jnp.int32, (target_len, target_len), 1)
    target_allowed = (target_valid == 1)[None, None, :] & causal[None]
    normed = low(layer_norm(source, norm_gain[0], norm_bias[0]))
    middle = source + attention(normed, normed, attn_in[0], attn_in_bias[0], attn_out[0], attn_out_bias[0], source_allowed)
    encoded = middle + feed_forward(low(layer_norm(middle, norm_gain[1], norm_bias[1])), ffn_in[0], ffn_in_bias[0], ffn_out[0], ffn_out_bias[0])
    memory = low(encoded)
    normed = low(layer_norm(target, norm_gain[2], norm_bias[2]))
    first_out = target + attention(normed, normed, attn_in[1], attn_in_bias[1], attn_out[1], attn_out_bias[1], target_allowed)
    normed = low(layer_norm(first_out, norm_gain[3], norm_bias[3]))
    second = first_out + attention(normed, memory, attn_in[2], attn_in_bias[2], attn_out[2], attn_out_bias[2], source_allowed)
    decoded = second + feed_forward(low(layer_norm(second, norm_gain[4], norm_bias[4])), ffn_in[1], ffn_in_bias[1], ffn_out[1], ffn_out_bias[1])
    return (encoded, decoded)

def reference(src_embed, tgt_embed, src_mask, tgt_mask, objective, loss_mask, enc_cot, dec_cot, norm_gain, norm_bias, attn_in, attn_in_bias, attn_out, attn_out_bias, ffn_in, ffn_in_bias, ffn_out, ffn_out_bias):
    params = (norm_gain.astype(jnp.float32), norm_bias.astype(jnp.float32), attn_in.astype(jnp.float32), attn_in_bias.astype(jnp.float32), attn_out.astype(jnp.float32), attn_out_bias.astype(jnp.float32), ffn_in.astype(jnp.float32), ffn_in_bias.astype(jnp.float32), ffn_out.astype(jnp.float32), ffn_out_bias.astype(jnp.float32))
    source = jnp.transpose(src_embed.astype(jnp.float32), (1, 0, 2))
    target = jnp.transpose(tgt_embed.astype(jnp.float32), (1, 0, 2))

    def forward(weights, source_all, target_all):

        def example_step(example_items):
            return one_example(weights, example_items[0], example_items[1], example_items[2], example_items[3])
        return lax.map(jax.checkpoint(example_step), (source_all, target_all, src_mask, tgt_mask))
    (encoded, decoded), pullback = jax.vjp(forward, params, source, target)
    flag = objective.astype(jnp.float32)
    weight_enc = 1.0 - 0.5 * flag
    weight_dec = 0.5 + 0.5 * flag
    position_weight = 0.25 + 0.75 * loss_mask.astype(jnp.float32)
    enc_cotan = jnp.transpose(enc_cot.astype(jnp.float32), (1, 0, 2)) * weight_enc[:, None, None]
    dec_cotan = jnp.transpose(dec_cot.astype(jnp.float32), (1, 0, 2)) * weight_dec[:, None, None] * position_weight[:, :, None]
    gradients, source_grad, target_grad = pullback((enc_cotan, dec_cotan))
    enc_out = jnp.transpose(encoded, (1, 0, 2)).astype(jnp.bfloat16)
    dec_out = jnp.transpose(decoded, (1, 0, 2)).astype(jnp.bfloat16)
    src_grad = jnp.transpose(source_grad, (1, 0, 2))
    tgt_grad = jnp.transpose(target_grad, (1, 0, 2))
    return (enc_out, dec_out, src_grad, tgt_grad, gradients[0], gradients[1], gradients[2], gradients[3], gradients[4], gradients[5], gradients[6], gradients[7], gradients[8], gradients[9])
```

```python
import functools

import jax
import jax.numpy as jnp
from jax import lax
from jax.experimental import pallas as pl
from jax.experimental.pallas import tpu as pltpu
from jax.sharding import PartitionSpec as P

HEAD = 64
EPSILON = 1e-05
MASKED_SCORE = -1000000000.0
BF16 = jnp.bfloat16
F32 = jnp.float32


def dot(left, right, contract):
    return lax.dot_general(left, right, (contract, ((), ())), preferred_element_type=F32)


def rows_by_cols(left, right):
    return dot(left, right, ((1,), (0,)))


def rows_by_rows(left, right):
    return dot(left, right, ((1,), (1,)))


def cols_by_cols(left, right):
    return dot(left, right, ((0,), (0,)))


def swap(values):
    return lax.ppermute(values, "tensor", [(0, 1), (1, 0)])


def flip(values):
    half = values.shape[0] // 2
    return jnp.concatenate([values[half:], values[:half]], axis=0)


def both_halves(own):
    return jnp.concatenate([own, swap(own)], axis=0)


def pair_sum(partial):
    return partial + flip(swap(partial.astype(BF16))).astype(F32)


def own_sum(partial):
    half = partial.shape[0] // 2
    return partial[:half] + swap(partial[half:].astype(BF16)).astype(F32)


def norm_forward(inputs, gain, offset):
    centre = inputs - jnp.mean(inputs, axis=-1, keepdims=True)
    inverse = lax.rsqrt(jnp.mean(centre * centre, axis=-1, keepdims=True) + EPSILON)
    normed = centre * inverse
    return (normed * gain + offset).astype(BF16), (normed, inverse)


def norm_backward(gradient, kept, gain):
    normed, inverse = kept
    half = (normed.shape[0] // 2)
    gain_grad = jnp.sum(gradient[:half] * normed[:half], axis=0)
    offset_grad = jnp.sum(gradient[:half], axis=0)
    scaled = gradient * gain
    mean_plain = jnp.mean(scaled, axis=-1, keepdims=True)
    mean_normed = jnp.mean(scaled * normed, axis=-1, keepdims=True)
    return inverse * (scaled - mean_plain - normed * mean_normed), gain_grad, offset_grad


def split_heads(values):
    return values.reshape(values.shape[0], values.shape[1] // HEAD, HEAD)


def head_scores(queries, key_rows, allowed):
    scores = jnp.einsum(
        "qhd,khd->hqk", split_heads(queries), split_heads(key_rows), preferred_element_type=F32
    ) * HEAD ** (-0.5)
    return jnp.where(allowed, scores, MASKED_SCORE)


def attend(queries, key_rows, value_rows, allowed):
    scores = head_scores(queries, key_rows, allowed)
    row_max = jnp.max(scores, axis=-1, keepdims=True)
    exponent = jnp.exp(scores - row_max)
    row_total = jnp.sum(exponent, axis=-1, keepdims=True)
    weights = (exponent / row_total).astype(BF16)
    mixture = jnp.einsum(
        "hqk,khd->qhd", weights, split_heads(value_rows), preferred_element_type=F32
    )
    return mixture.reshape(queries.shape).astype(BF16), row_max + jnp.log(row_total)


def attend_backward(mixture_grad, queries, key_rows, value_rows, allowed, log_total):
    scale = HEAD ** (-0.5)
    probs = jnp.exp(head_scores(queries, key_rows, allowed) - log_total)
    grad_heads = split_heads(mixture_grad)
    prob_grad = jnp.einsum(
        "qhd,khd->hqk", grad_heads, split_heads(value_rows), preferred_element_type=F32
    )
    row_inner = jnp.sum(probs * prob_grad, axis=-1, keepdims=True)
    score_grad = (probs * (prob_grad - row_inner)).astype(BF16)
    query_grad = (
        jnp.einsum("hqk,khd->qhd", score_grad, split_heads(key_rows), preferred_element_type=F32)
        * scale
    )
    key_grad = (
        jnp.einsum("hqk,qhd->khd", score_grad, split_heads(queries), preferred_element_type=F32)
        * scale
    )
    value_grad = jnp.einsum(
        "hqk,qhd->khd", probs.astype(BF16), grad_heads, preferred_element_type=F32
    )
    return (
        query_grad.reshape(queries.shape).astype(BF16),
        key_grad.reshape(key_rows.shape).astype(BF16),
        value_grad.reshape(value_rows.shape).astype(BF16),
    )


def bits_of_dp():
    count = lax.axis_size("dp")
    here = lax.axis_index("dp")
    return [(1 << b, (here >> b) & 1) for b in range(count.bit_length() - 1)]


def across(values, stride):
    count = lax.axis_size("dp")
    return lax.ppermute(values, "dp", [(i, i ^ stride) for i in range(count)])


def join_body(bit_ref, own_ref, other_ref, out_ref):
    bit = bit_ref[0]
    out_ref[pl.ds(bit, 1)] = own_ref[...][None]
    out_ref[pl.ds(1 - bit, 1)] = other_ref[...][None]


def join(bit, own, other):
    rows, width = own.shape
    return pl.pallas_call(
        join_body,
        out_shape=jax.ShapeDtypeStruct((2, rows, width), own.dtype),
        in_specs=[
            pl.BlockSpec(memory_space=pltpu.SMEM),
            pl.BlockSpec(memory_space=pltpu.VMEM),
            pl.BlockSpec(memory_space=pltpu.VMEM),
        ],
        out_specs=pl.BlockSpec(memory_space=pltpu.VMEM),
    )(bit.reshape(1), own, other).reshape(2 * rows, width)


def place_body(parts, bit_ref, own_ref, other_ref, *refs):
    out_ref = refs[-1]
    bit = bit_ref[0]
    width = own_ref.shape[1] // parts
    for part in range(parts):
        columns = pl.ds(part * width, width)
        out_ref[0, part, pl.ds(bit, 1)] = own_ref[:, columns].astype(F32)[None]
        out_ref[0, part, pl.ds(1 - bit, 1)] = other_ref[:, columns].astype(F32)[None]


def place(bit, own, other, stacked, layer, layers, parts):
    rows, width = own.shape
    block = rows
    while block * width > 192 * 1024 and block % 32 == 0:
        block //= 2
    shape = (layers, parts, 2, rows, width // parts)
    aliased = stacked is not None
    return pl.pallas_call(
        functools.partial(place_body, parts),
        grid=(rows // block,),
        out_shape=jax.ShapeDtypeStruct(shape, F32),
        in_specs=[
            pl.BlockSpec(memory_space=pltpu.SMEM),
            pl.BlockSpec((block, width), lambda i: (i, 0)),
            pl.BlockSpec((block, width), lambda i: (i, 0)),
        ]
        + ([pl.BlockSpec(memory_space=pl.ANY)] if aliased else []),
        out_specs=pl.BlockSpec(
            (1, parts, 2, block, width // parts), lambda i: (layer, 0, 0, i, 0)
        ),
        input_output_aliases={3: 0} if aliased else {},
    )(bit.reshape(1), own, other, *([stacked] if aliased else []))


def scatter_sum(payload):
    current = payload
    for stride, bit in bits_of_dp():
        halves = current.reshape(2, current.shape[0] // 2, current.shape[1])
        send = lax.dynamic_index_in_dim(halves, 1 - bit, 0, keepdims=False)
        keep = lax.dynamic_index_in_dim(halves, bit, 0, keepdims=False)
        received = across(send.astype(BF16), stride)
        current = keep.astype(F32) + received.astype(F32)
        current = current.astype(BF16)
    return current


def gather_sum(shard, place_last):
    bits = bits_of_dp()
    current = shard
    for stride, bit in bits[:0:-1]:
        current = join(bit, current, across(current, stride))
    stride, bit = bits[0]
    return place_last(bit, current, across(current, stride))


def total_small(values):
    for stride, bit in bits_of_dp():
        values = values + across(values, stride)
    return values


def gelu_parts(hidden):
    cubic = 0.7978845608028654 * (hidden + 0.044715 * hidden * hidden * hidden)
    bent = jnp.tanh(cubic)
    return 0.5 * hidden * (1.0 + bent), bent


def gelu_slope(hidden, bent):
    inner = 0.7978845608028654 * (1.0 + 3 * 0.044715 * hidden * hidden)
    return 0.5 * (1.0 + bent) + 0.5 * hidden * (1.0 - bent * bent) * inner


def on_device(
    src_embed,
    tgt_embed,
    src_mask,
    tgt_mask,
    objective,
    loss_mask,
    enc_cot,
    dec_cot,
    norm_gain,
    norm_bias,
    attn_in,
    attn_in_bias,
    attn_out,
    attn_out_bias,
    ffn_in,
    ffn_in_bias,
    ffn_out,
    ffn_out_bias,
):
    here = lax.axis_index("tensor")
    width = src_embed.shape[2]
    local = attn_in.shape[3]
    source = both_halves(src_embed.reshape(-1, width)).astype(F32)
    target = both_halves(tgt_embed.reshape(-1, width)).astype(F32)
    enc_seed = both_halves(enc_cot.reshape(-1, width))
    dec_seed = both_halves(dec_cot.reshape(-1, width))
    loss_seed = both_halves(loss_mask.reshape(-1, 1).astype(F32))
    source_count = source.shape[0]
    target_count = target.shape[0]

    def positions(count):
        half = count // 2
        index = jnp.arange(count, dtype=jnp.int32)
        return lax.rem(index + here * half, count)

    source_real = src_mask.reshape(2, -1)
    source_real = jnp.where(here == 0, source_real, source_real[::-1]).reshape(-1) == 1
    target_real = tgt_mask.reshape(2, -1)
    target_real = jnp.where(here == 0, target_real, target_real[::-1]).reshape(-1) == 1
    target_position = positions(target_count)
    source_allowed = source_real[None, None, :]
    target_allowed = (
        target_real[None, :] & (target_position[:, None] >= target_position[None, :])
    )[None]

    def project(inputs, layer, which):
        result = rows_by_cols(inputs, attn_in[layer, which])
        if which == 0:
            result = result + attn_in_bias[layer, 0]
        if which == 2:
            result = result + attn_in_bias[layer, 1]
        return result.astype(BF16)

    def attention(inputs, memory, norm, layer, allowed):
        hidden, kept = norm_forward(inputs, norm_gain[norm], norm_bias[norm])
        keys_from = hidden if memory is None else memory
        queries = project(hidden, layer, 0)
        key_rows = project(keys_from, layer, 1)
        value_rows = project(keys_from, layer, 2)
        mixture, log_total = attend(queries, key_rows, value_rows, allowed)
        partial = rows_by_cols(mixture, attn_out[layer])
        result = inputs + (pair_sum(partial) + attn_out_bias[layer])
        return result, (kept, hidden, keys_from, queries, key_rows, value_rows, mixture, log_total)

    def feed(inputs, norm, layer):
        hidden, kept = norm_forward(inputs, norm_gain[norm], norm_bias[norm])
        before = rows_by_cols(hidden, ffn_in[layer]) + ffn_in_bias[layer]
        active, bent = gelu_parts(before)
        active = active.astype(BF16)
        partial = rows_by_cols(active, ffn_out[layer])
        return partial, (kept, hidden, before, active)

    middle, enc_attention = attention(source, None, 0, 0, source_allowed)
    partial, enc_feed = feed(middle, 1, 0)
    encoded = middle + (pair_sum(partial) + ffn_out_bias[0])
    memory = encoded.astype(BF16)
    first, dec_attention = attention(target, None, 2, 1, target_allowed)
    second, dec_cross = attention(first, memory, 3, 2, source_allowed)
    partial, dec_feed = feed(second, 4, 1)
    half = target_count // 2
    decoded = second[:half] + (own_sum(partial) + ffn_out_bias[1])

    flag = objective.astype(F32)[0]
    enc_cotan = enc_seed.astype(F32) * (1.0 - 0.5 * flag)
    dec_cotan = dec_seed.astype(F32) * (0.5 + 0.5 * flag) * (0.25 + 0.75 * loss_seed)

    small = {}

    def feed_backward(gradient, kept_all, norm, layer):
        kept, hidden, before, active = kept_all
        low = gradient.astype(BF16)
        small["ffn_out_bias", layer] = jnp.sum(low[: low.shape[0] // 2].astype(F32), axis=0)
        out_grad = cols_by_cols(active, low).astype(BF16)
        active_grad = rows_by_rows(low, ffn_out[layer])
        unused, bent = gelu_parts(before)
        before_grad = (active_grad * gelu_slope(before, bent)).astype(BF16)
        in_grad = cols_by_cols(hidden, before_grad).astype(BF16)
        small["ffn_in_bias", layer] = jnp.sum(before_grad.astype(F32), axis=0)
        partial = rows_by_rows(before_grad, ffn_in[layer])
        input_grad, gain_grad, offset_grad = norm_backward(
            pair_sum(partial), kept, norm_gain[norm]
        )
        small["gain", norm], small["offset", norm] = gain_grad, offset_grad
        return gradient + input_grad, in_grad, out_grad

    def attention_backward(gradient, kept_all, norm, layer, allowed, cross, last):
        kept, hidden, keys_from, queries, key_rows, value_rows, mixture, log_total = kept_all
        low = gradient.astype(BF16)
        small["attn_out_bias", layer] = jnp.sum(low[: low.shape[0] // 2].astype(F32), axis=0)
        out_grad = cols_by_cols(mixture, low).astype(BF16)
        mixture_grad = rows_by_rows(low, attn_out[layer]).astype(BF16)
        query_grad, key_grad, value_grad = attend_backward(
            mixture_grad, queries, key_rows, value_rows, allowed, log_total
        )
        in_grad = jnp.concatenate(
            [
                cols_by_cols(hidden, query_grad).astype(BF16),
                cols_by_cols(keys_from, key_grad).astype(BF16),
                cols_by_cols(keys_from, value_grad).astype(BF16),
            ],
            axis=1,
        )
        small["attn_in_bias", layer] = jnp.concatenate(
            [jnp.sum(query_grad.astype(F32), axis=0), jnp.sum(value_grad.astype(F32), axis=0)]
        )
        query_part = rows_by_rows(query_grad, attn_in[layer, 0])
        key_part = rows_by_rows(key_grad, attn_in[layer, 1]) + rows_by_rows(
            value_grad, attn_in[layer, 2]
        )
        memory_grad = None
        if cross:
            memory_grad = pair_sum(key_part)
        else:
            query_part = query_part + key_part
        if last:
            total = own_sum(query_part)
            rows = total.shape[0]
            kept = (kept[0][:rows], kept[1][:rows])
            gradient = gradient[:rows]
            normed, inverse = kept
            small["gain", norm] = jnp.sum(total * normed, axis=0)
            small["offset", norm] = jnp.sum(total, axis=0)
            scaled = total * norm_gain[norm]
            mean_plain = jnp.mean(scaled, axis=-1, keepdims=True)
            mean_normed = jnp.mean(scaled * normed, axis=-1, keepdims=True)
            input_grad = inverse * (scaled - mean_plain - normed * mean_normed)
        else:
            input_grad, gain_grad, offset_grad = norm_backward(
                pair_sum(query_part), kept, norm_gain[norm]
            )
            small["gain", norm], small["offset", norm] = gain_grad, offset_grad
        return gradient + input_grad, memory_grad, in_grad, out_grad

    shards = {}
    gradient, in_grad, out_grad = feed_backward(dec_cotan, dec_feed, 4, 1)
    shards["ffn_out", 1] = scatter_sum(out_grad)
    shards["ffn_in", 1] = scatter_sum(in_grad)
    gradient, memory_grad, in_grad, out_grad = attention_backward(
        gradient, dec_cross, 3, 2, source_allowed, True, False
    )
    shards["attn_out", 2] = scatter_sum(out_grad)
    shards["attn_in", 2] = scatter_sum(in_grad)
    target_grad, unused, in_grad, out_grad = attention_backward(
        gradient, dec_attention, 2, 1, target_allowed, False, True
    )
    shards["attn_out", 1] = scatter_sum(out_grad)
    shards["attn_in", 1] = scatter_sum(in_grad)
    gradient, in_grad, out_grad = feed_backward(enc_cotan + memory_grad, enc_feed, 1, 0)
    shards["ffn_out", 0] = scatter_sum(out_grad)
    shards["ffn_in", 0] = scatter_sum(in_grad)
    source_grad, unused, in_grad, out_grad = attention_backward(
        gradient, enc_attention, 0, 0, source_allowed, False, True
    )
    shards["attn_out", 0] = scatter_sum(out_grad)
    shards["attn_in", 0] = scatter_sum(in_grad)

    stacks = {}
    counts = {"ffn_out": (2, 1), "ffn_in": (2, 1), "attn_out": (3, 1), "attn_in": (3, 3)}
    for (name, layer), shard in shards.items():
        layers, parts = counts[name]
        stacks[name] = gather_sum(
            shard,
            lambda bit, own, other: place(
                bit, own, other, stacks.get(name), layer, layers, parts
            ),
        )

    shared = jnp.stack(
        [small["gain", i] for i in range(5)]
        + [small["offset", i] for i in range(5)]
        + [small["attn_out_bias", i] for i in range(3)]
        + [small["ffn_out_bias", i] for i in range(2)]
    )
    apart = jnp.concatenate(
        [small["attn_in_bias", i] for i in range(3)] + [small["ffn_in_bias", i] for i in range(2)]
    ).reshape(-1, width)
    shared = shared + swap(shared)
    summed = total_small(jnp.concatenate([shared, apart], axis=0))
    shared, apart = summed[:15], summed[15:].reshape(-1)
    bias_rows = apart[: 6 * local].reshape(3, 2, local)
    hidden_rows = apart[6 * local :].reshape(2, -1)
    half = source_count // 2
    return (
        memory[:half][:, None],
        decoded.astype(BF16)[:, None],
        source_grad[:, None],
        target_grad[:, None],
        shared[0:5],
        shared[5:10],
        stacks["attn_in"].reshape(attn_in.shape),
        bias_rows,
        stacks["attn_out"].reshape(attn_out.shape),
        shared[10:13],
        stacks["ffn_in"].reshape(ffn_in.shape),
        hidden_rows,
        stacks["ffn_out"].reshape(ffn_out.shape),
        shared[13:15],
    )


def solution(mesh):
    return jax.shard_map(
        on_device,
        mesh=mesh,
        in_specs=(
            P("tensor", "dp", None),
            P("tensor", "dp", None),
            P("dp", None),
            P("dp", None),
            P("dp"),
            P("dp", "tensor"),
            P("tensor", "dp", None),
            P("tensor", "dp", None),
            P(),
            P(),
            P(None, None, None, "tensor"),
            P(None, None, "tensor"),
            P(None, "tensor", None),
            P(),
            P(None, None, "tensor"),
            P(None, "tensor"),
            P(None, "tensor", None),
            P(),
        ),
        out_specs=(
            P("tensor", "dp", None),
            P("tensor", "dp", None),
            P("tensor", "dp", None),
            P("tensor", "dp", None),
            P(),
            P(),
            P(None, None, None, "tensor"),
            P(None, None, "tensor"),
            P(None, "tensor", None),
            P(),
            P(None, None, "tensor"),
            P(None, "tensor"),
            P(None, "tensor", None),
            P(),
        ),
        check_vma=False,
    )
```

```python
import functools

import jax
import jax.numpy as jnp
from jax import lax
from jax.experimental import pallas as pl
from jax.experimental.pallas import tpu as pltpu
from jax.sharding import PartitionSpec as P

HEAD = 64
PAIR = 2 * HEAD
EPSILON = 1e-05
MASKED_SCORE = -1000000000.0
FAR = 1e9
BF16 = jnp.bfloat16
F32 = jnp.float32
VMEM_LIMIT = 24 * 1024 * 1024
NN = ((1,), (0,))
NT = ((1,), (1,))
TN = ((0,), (0,))


def dot(left, right, contract):
    return lax.dot_general(left, right, (contract, ((), ())), preferred_element_type=F32)


def shape(rows, columns, dtype):
    return jax.ShapeDtypeStruct((rows, columns), dtype)


def run(body, outs, *args, scalars=0, scratch=(), flops=0):
    spaces = [pltpu.SMEM] * scalars + [pltpu.VMEM] * (len(args) - scalars)
    moved = sum(a.size * a.dtype.itemsize for a in (*args, *outs))
    return pl.pallas_call(
        body,
        out_shape=list(outs),
        in_specs=[pl.BlockSpec(memory_space=space) for space in spaces],
        out_specs=[pl.BlockSpec(memory_space=pltpu.VMEM)] * len(outs),
        scratch_shapes=list(scratch),
        compiler_params=pltpu.CompilerParams(vmem_limit_bytes=VMEM_LIMIT),
        cost_estimate=pl.CostEstimate(flops=flops, transcendentals=0, bytes_accessed=moved),
    )(*args)


def norm_parts(inputs):
    centre = inputs - jnp.mean(inputs, axis=-1, keepdims=True)
    inverse = lax.rsqrt(jnp.mean(centre * centre, axis=-1, keepdims=True) + EPSILON)
    return centre * inverse, inverse


def halves(count):
    half = count // 2
    return ((0, half), (half, 0))


def lane_half(which, rows):
    lanes = lax.broadcasted_iota(jnp.int32, (rows, PAIR), 1)
    return (lanes >= HEAD) if which else (lanes < HEAD)


def only_head(which, values):
    return jnp.where(lane_half(which, values.shape[0]), values, jnp.zeros_like(values))


def key_scores(key_pair, query_pair, which, key_at, query_at):
    scores = dot(only_head(which, key_pair), query_pair, NT)
    return jnp.where(key_at <= query_at, scores, MASKED_SCORE)


def attend(q_ref, k_ref, v_ref, key_at_ref, query_at_ref, turned_ref, o_ref, log_ref):
    queries, local = q_ref.shape
    block = min(queries, 256)
    key_at = key_at_ref[...]
    for pair in range(local // PAIR):
        columns = pl.ds(pair * PAIR, PAIR)
        key_pair = k_ref[:, columns]
        value_turned = v_ref[:, columns].astype(F32).T.astype(BF16)
        for start in range(0, queries, block):
            rows = pl.ds(start, block)
            query_pair = q_ref[rows, columns]
            query_at = query_at_ref[:, rows]
            for which in range(2):
                head = 2 * pair + which
                scores = key_scores(key_pair, query_pair, which, key_at, query_at)
                top = jnp.max(scores, axis=0, keepdims=True)
                exponent = jnp.exp(scores - top)
                total = jnp.sum(exponent, axis=0, keepdims=True)
                weights = (exponent * (1.0 / total)).astype(BF16)
                log_ref[pl.ds(head, 1), rows] = top + jnp.log(total)
                mixed = dot(value_turned[which * HEAD : (which + 1) * HEAD], weights, NN)
                turned_ref[pl.ds(head * HEAD, HEAD), rows] = mixed.astype(BF16)
    o_ref[...] = turned_ref[...].astype(F32).T.astype(BF16)


def project(hidden, w_ref, which, bias):
    result = dot(hidden, w_ref[which], NN)
    return result if bias is None else result + bias


def finish(base_ref, send_ref, rows, base, partial):
    base_ref[rows] = base + partial
    send_ref[rows] = partial.astype(BF16)


def first_attention_body(
    own_ref, other_ref, gain_ref, offset_ref, w_in_ref, b_in_ref, w_out_ref, b_out_ref,
    key_at_ref, query_at_ref,
    h_ref, q_ref, k_ref, v_ref, turned_ref, log_ref, base_ref, send_ref, o_ref,
):
    half = own_ref.shape[0]
    for part, source in enumerate((own_ref, other_ref)):
        rows = pl.ds(part * half, half)
        normed, unused = norm_parts(source[...].astype(F32))
        hidden = (normed * gain_ref[...] + offset_ref[...]).astype(BF16)
        h_ref[rows] = hidden
        q_ref[rows] = (project(hidden, w_in_ref, 0, b_in_ref[0:1]).astype(BF16) * HEAD ** (-0.5)).astype(BF16)
        k_ref[rows] = project(hidden, w_in_ref, 1, None).astype(BF16)
        v_ref[rows] = project(hidden, w_in_ref, 2, b_in_ref[1:2]).astype(BF16)
    attend(q_ref, k_ref, v_ref, key_at_ref, query_at_ref, turned_ref, o_ref, log_ref)
    for part, source in enumerate((own_ref, other_ref)):
        rows = pl.ds(part * half, half)
        partial = dot(o_ref[rows], w_out_ref[...], NN)
        finish(base_ref, send_ref, rows, source[...].astype(F32) + b_out_ref[...], partial)


def cross_attention_body(
    before_ref, recv_ref, gain_ref, offset_ref, w_in_ref, b_in_ref, w_out_ref, b_out_ref,
    k_ref, v_ref, key_at_ref, query_at_ref,
    x_ref, h_ref, q_ref, turned_ref, log_ref, base_ref, send_ref, o_ref,
):
    count = before_ref.shape[0]
    half = count // 2
    for mine, theirs in halves(count):
        rows = pl.ds(mine, half)
        value = before_ref[rows] + recv_ref[pl.ds(theirs, half)].astype(F32)
        x_ref[rows] = value
        normed, unused = norm_parts(value)
        hidden = (normed * gain_ref[...] + offset_ref[...]).astype(BF16)
        h_ref[rows] = hidden
        q_ref[rows] = (project(hidden, w_in_ref, 0, b_in_ref[0:1]).astype(BF16) * HEAD ** (-0.5)).astype(BF16)
    attend(q_ref, k_ref, v_ref, key_at_ref, query_at_ref, turned_ref, o_ref, log_ref)
    partial = dot(o_ref[...], w_out_ref[...], NN)
    finish(base_ref, send_ref, slice(None), x_ref[...] + b_out_ref[...], partial)


def memory_body(before_ref, recv_ref, w_in_ref, b_in_ref, mem_ref, k_ref, v_ref):
    count = before_ref.shape[0]
    half = count // 2
    for mine, theirs in halves(count):
        rows = pl.ds(mine, half)
        memory = (before_ref[rows] + recv_ref[pl.ds(theirs, half)].astype(F32)).astype(BF16)
        mem_ref[rows] = memory
        k_ref[rows] = project(memory, w_in_ref, 1, None).astype(BF16)
        v_ref[rows] = project(memory, w_in_ref, 2, b_in_ref[1:2]).astype(BF16)


ROOT = 0.7978845608028654
CUBIC = 0.044715


def feed_body(
    before_ref, recv_ref, gain_ref, offset_ref, w1_ref, b1_ref, w2_ref, b2_ref,
    x_ref, h_ref, f_ref, slope_ref, base_ref, send_ref,
):
    count = before_ref.shape[0]
    half = count // 2
    for mine, theirs in halves(count):
        rows = pl.ds(mine, half)
        value = before_ref[rows] + recv_ref[pl.ds(theirs, half)].astype(F32)
        x_ref[rows] = value
        normed, unused = norm_parts(value)
        hidden = (normed * gain_ref[...] + offset_ref[...]).astype(BF16)
        h_ref[rows] = hidden
        u = dot(hidden, w1_ref[...], NN) + b1_ref[...]
        square = u * u
        bent = jnp.tanh(u * (ROOT + (ROOT * CUBIC) * square))
        upper = 0.5 + 0.5 * bent
        active = (u * upper).astype(BF16)
        f_ref[rows] = active
        slope = upper + (0.5 * u) * (1.0 - bent * bent) * (ROOT + (3 * ROOT * CUBIC) * square)
        slope_ref[rows] = slope.astype(BF16)
        finish(base_ref, send_ref, rows, value + b2_ref[...], dot(active, w2_ref[...], NN))


def norm_back(gradient, normed, inverse, gain):
    scaled = gradient * gain
    mean_plain = jnp.mean(scaled, axis=-1, keepdims=True)
    mean_normed = jnp.mean(scaled * normed, axis=-1, keepdims=True)
    return inverse * (scaled - mean_plain - normed * mean_normed)


def column_sum(values):
    return jnp.sum(values.astype(F32), axis=0, keepdims=True)


def feed_back_body(kind, *refs):
    if kind == "dec":
        (cot_ref, cot_other_ref, weight_ref, w1_ref, w2_ref, slope_ref,
         g_ref, low_ref, du_ref, base_ref, send_ref, sums_ref, hidden_sums_ref) = refs
    else:
        (cot_ref, cot_other_ref, weight_ref, mem_base_ref, mem_recv_ref, w1_ref, w2_ref, slope_ref,
         g_ref, low_ref, du_ref, base_ref, send_ref, sums_ref, hidden_sums_ref) = refs
    count = g_ref.shape[0]
    half = count // 2
    hidden_sum = None
    for part, (mine, theirs) in enumerate(halves(count)):
        rows = pl.ds(mine, half)
        cot = (cot_ref if part == 0 else cot_other_ref)[...].astype(F32)
        gradient = cot * weight_ref[rows]
        if kind == "enc":
            gradient = gradient + (
                mem_base_ref[rows] + mem_recv_ref[pl.ds(theirs, half)].astype(F32)
            )
        g_ref[rows] = gradient
        low = gradient.astype(BF16)
        low_ref[rows] = low
        if part == 0:
            sums_ref[...] = column_sum(low)
        du = (dot(low, w2_ref[...], NT) * slope_ref[rows].astype(F32)).astype(BF16)
        du_ref[rows] = du
        partial_sum = column_sum(du)
        hidden_sum = partial_sum if hidden_sum is None else hidden_sum + partial_sum
        partial = dot(du, w1_ref[...], NT)
        base_ref[rows] = partial
        send_ref[rows] = partial.astype(BF16)
    hidden_sums_ref[...] = hidden_sum


def attention_back_body(kind, *refs):
    if kind == "cross":
        (g_in_ref, dh_ref, dh_recv_ref, x_ref, gain_ref, w_in_ref, w_out_ref, q_ref, k_ref, v_ref,
         log_ref, key_at_ref, query_at_ref,
         g_ref, low_ref, dq_ref, dk_ref, dv_ref, base_ref, send_ref, mem_base_ref, mem_send_ref,
         norm_sums_ref, sums_ref, bias_sums_ref, do_ref, turned_ref) = refs
    else:
        (g_in_ref, dh_ref, dh_recv_ref, x_ref, gain_ref, w_in_ref, w_out_ref, q_ref, k_ref, v_ref,
         log_ref, key_at_ref, query_at_ref,
         g_ref, low_ref, dq_ref, dk_ref, dv_ref, base_ref, send_ref,
         norm_sums_ref, sums_ref, bias_sums_ref, do_ref, turned_ref) = refs
    count, local = q_ref.shape
    half = count // 2
    for part, (mine, theirs) in enumerate(halves(count)):
        rows = pl.ds(mine, half)
        normed, inverse = norm_parts(x_ref[rows])
        dh = dh_ref[rows] + dh_recv_ref[pl.ds(theirs, half)].astype(F32)
        gradient = g_in_ref[rows] + norm_back(dh, normed, inverse, gain_ref[...])
        g_ref[rows] = gradient
        low = gradient.astype(BF16)
        low_ref[rows] = low
        if part == 0:
            norm_sums_ref[0:1] = column_sum(dh * normed)
            norm_sums_ref[1:2] = column_sum(dh)
            sums_ref[...] = column_sum(low)
        do_ref[rows] = dot(low, w_out_ref[...], NT).astype(BF16)
    block = min(count, 256)
    key_at = key_at_ref[...]
    keys = k_ref.shape[0]
    for pair in range(local // PAIR):
        columns = pl.ds(pair * PAIR, PAIR)
        key_pair = k_ref[:, columns]
        key_turned = key_pair.astype(F32).T.astype(BF16)
        value_pair = v_ref[:, columns]
        dk = [None, None]
        dv = [None, None]
        for start in range(0, count, block):
            rows = pl.ds(start, block)
            query_pair = q_ref[rows, columns]
            do_pair = do_ref[rows, columns]
            query_at = query_at_ref[:, rows]
            for which in range(2):
                head = 2 * pair + which
                scores = key_scores(key_pair, query_pair, which, key_at, query_at)
                probs = jnp.exp(scores - log_ref[pl.ds(head, 1), rows])
                prob_grad = dot(only_head(which, value_pair), do_pair, NT)
                product = probs * prob_grad
                inner = jnp.sum(product, axis=0, keepdims=True)
                score_grad = (product - probs * inner).astype(BF16)
                dv_part = dot(probs.astype(BF16), do_pair, NN)
                dk_part = dot(score_grad, query_pair, NN)
                dq_part = dot(key_turned[which * HEAD : (which + 1) * HEAD], score_grad, NN)
                turned_ref[pl.ds(head * HEAD, HEAD), rows] = dq_part * HEAD ** (-0.5)
                dk[which] = dk_part if dk[which] is None else dk[which] + dk_part
                dv[which] = dv_part if dv[which] is None else dv[which] + dv_part
        first = lane_half(0, keys)
        dk_ref[:, columns] = jnp.where(first, dk[0], dk[1]).astype(BF16)
        dv_ref[:, columns] = jnp.where(first, dv[0], dv[1]).astype(BF16)
    dq_ref[...] = turned_ref[...].T.astype(BF16)
    bias_sums_ref[0:1] = column_sum(dq_ref[...])
    bias_sums_ref[1:2] = column_sum(dv_ref[...])
    if kind == "cross":
        partial = dot(dq_ref[...], w_in_ref[0], NT)
        base_ref[...] = partial
        send_ref[...] = partial.astype(BF16)
        partial = dot(dk_ref[...], w_in_ref[1], NT) + dot(dv_ref[...], w_in_ref[2], NT)
        mem_base_ref[...] = partial
        mem_send_ref[...] = partial.astype(BF16)
    else:
        rest = pl.ds(half, half)
        own = pl.ds(0, half)
        for rows in (rest, own):
            partial = (
                dot(dq_ref[rows], w_in_ref[0], NT)
                + dot(dk_ref[rows], w_in_ref[1], NT)
                + dot(dv_ref[rows], w_in_ref[2], NT)
            )
            if rows is rest:
                send_ref[...] = partial.astype(BF16)
            else:
                base_ref[...] = partial


def last_norm_body(g_ref, dh_ref, recv_ref, x_ref, gain_ref, out_ref, norm_sums_ref):
    half = dh_ref.shape[0]
    normed, inverse = norm_parts(x_ref[...].astype(F32))
    dh = dh_ref[...] + recv_ref[...].astype(F32)
    norm_sums_ref[0:1] = column_sum(dh * normed)
    norm_sums_ref[1:2] = column_sum(dh)
    out_ref[...] = g_ref[0:half] + norm_back(dh, normed, inverse, gain_ref[...])


def feed_weights_body(bit_ref, h_ref, du_ref, f_ref, low_ref, send_ref, keep_ref):
    bit = bit_ref[0]
    width = h_ref.shape[1]
    part = width // 2
    for which, out_ref in ((1 - bit, send_ref), (bit, keep_ref)):
        left = h_ref[:, pl.ds(pl.multiple_of(which * part, 128), part)]
        for side in range(2):
            out_ref[pl.ds(side * part, part)] = dot(
                left, du_ref[:, pl.ds(side * width, width)], TN
            ).astype(BF16)
        left = f_ref[:, pl.ds(pl.multiple_of(which * width, 128), width)]
        out_ref[pl.ds(width, width)] = dot(left, low_ref[...], TN).astype(BF16)


def attention_weights_body(
    bit_ref, h_ref, mem_ref, dq_ref, dk_ref, dv_ref, turned_ref, low_ref, send_ref, keep_ref
):
    bit = bit_ref[0]
    width = h_ref.shape[1]
    part = width // 2
    quarter = width // 4
    left_side = pl.ds(0, part)
    right_side = pl.ds(part, part)
    for which, out_ref in ((1 - bit, send_ref), (bit, keep_ref)):
        columns = pl.ds(pl.multiple_of(which * part, 128), part)
        out_ref[pl.ds(0, part), left_side] = dot(h_ref[:, columns], dq_ref[...], TN).astype(BF16)
        memory = mem_ref[:, columns]
        out_ref[pl.ds(0, part), right_side] = dot(memory, dk_ref[...], TN).astype(BF16)
        values = dot(memory, dv_ref[...], TN).astype(BF16)
        out_ref[pl.ds(part, quarter), left_side] = values[:quarter]
        out_ref[pl.ds(part, quarter), right_side] = values[quarter:]
        rows = pl.ds(pl.multiple_of(which * quarter, 64), quarter)
        out_ref[pl.ds(part + quarter, quarter)] = dot(turned_ref[rows], low_ref[...], NN).astype(BF16)


def add_split_body(bit_ref, keep_ref, recv_ref, send_ref, next_ref):
    bit = bit_ref[0]
    rows = send_ref.shape[0]
    for which, out_ref in ((1 - bit, send_ref), (bit, next_ref)):
        part = pl.ds(pl.multiple_of(which * rows, 8), rows)
        out_ref[...] = (keep_ref[part].astype(F32) + recv_ref[part].astype(F32)).astype(BF16)


def swap(values):
    return lax.ppermute(values, "tensor", [(0, 1), (1, 0)])


def bits_of_dp():
    count = lax.axis_size("dp")
    here = lax.axis_index("dp")
    return [(1 << b, ((here >> b) & 1).reshape(1)) for b in range(count.bit_length() - 1)]


def across(values, stride):
    count = lax.axis_size("dp")
    return lax.ppermute(values, "dp", [(i, i ^ stride) for i in range(count)])


def scatter_sum(send, keep):
    bits = bits_of_dp()
    for step, (stride, unused) in enumerate(bits):
        received = across(send, stride)
        if step + 1 == len(bits):
            return (keep.astype(F32) + received.astype(F32)).astype(BF16)
        rows, width = keep.shape
        out = shape(rows // 2, width, BF16)
        send, keep = run(
            add_split_body, (out, out), bits[step + 1][1], keep, received, scalars=1
        )


def turned_index(index, count):
    bits = count.bit_length() - 1
    return sum(((index >> b) & 1) << (bits - 1 - b) for b in range(bits))


def place_body(in_ref, *refs):
    out_ref = refs[-1]
    out_ref[...] = in_ref[...].astype(F32).reshape(out_ref.shape)


def place(gathered, stacked, out_shape, grid, in_block, in_map, out_block, out_map):
    aliased = stacked is not None
    return pl.pallas_call(
        place_body,
        grid=grid,
        out_shape=jax.ShapeDtypeStruct(out_shape, F32),
        in_specs=[pl.BlockSpec(in_block, in_map)]
        + ([pl.BlockSpec(memory_space=pl.ANY)] if aliased else []),
        out_specs=pl.BlockSpec(out_block, out_map),
        input_output_aliases={1: 0} if aliased else {},
        compiler_params=pltpu.CompilerParams(vmem_limit_bytes=VMEM_LIMIT),
    )(gathered, *([stacked] if aliased else []))


def place_feed(gathered, at, layer, stacks, shapes):
    count = gathered.shape[0]
    width = gathered.shape[2]
    rows = 4 * width // count
    per_half = count // 2
    part = width // 2
    narrow = part // rows
    stacks["ffn_in"] = place(
        gathered, stacks.get("ffn_in"), shapes["ffn_in"], (2, 2, narrow),
        (1, rows, width),
        lambda h, c, j: (turned_index(h * per_half + c * narrow + j, count), at // rows, 0),
        (1, rows, width),
        lambda h, c, j: (layer, h * narrow + j, c),
    )
    wide = width // rows
    stacks["ffn_out"] = place(
        gathered, stacks.get("ffn_out"), shapes["ffn_out"], (2, wide),
        (1, rows, width),
        lambda h, j: (turned_index(h * per_half + wide + j, count), at // rows, 0),
        (1, rows, width),
        lambda h, j: (layer, h * wide + j, 0),
    )


def place_attention(gathered, at, layer, stacks, shapes):
    count = gathered.shape[0]
    width = gathered.shape[2]
    rows = 2 * width // count
    per_half = count // 2
    part = width // 2
    narrow = part // rows
    quarter = narrow // 2

    def in_map(c, h, j):
        value = c == 2
        shard = jnp.where(value, narrow + lax.rem(j, quarter), j)
        side = jnp.where(value, lax.div(j, quarter), c)
        return turned_index(h * per_half + shard, count), at // rows, side

    stacks["attn_in"] = place(
        gathered, stacks.get("attn_in"), shapes["attn_in"], (3, 2, narrow),
        (1, rows, part), in_map,
        (1, 1, rows, part),
        lambda c, h, j: (layer, c, h * narrow + j, 0),
    )
    stacks["attn_out"] = place(
        gathered, stacks.get("attn_out"), shapes["attn_out"], (2, quarter),
        (1, rows, width),
        lambda h, j: (turned_index(h * per_half + narrow + quarter + j, count), at // rows, 0),
        (1, rows, width),
        lambda h, j: (layer, h * quarter + j, 0),
    )


def total_small(values):
    for stride, unused in bits_of_dp():
        values = values + across(values, stride)
    return values


def on_device(
    src_embed, tgt_embed, src_mask, tgt_mask, objective, loss_mask, enc_cot, dec_cot,
    norm_gain, norm_bias, attn_in, attn_in_bias, attn_out, attn_out_bias,
    ffn_in, ffn_in_bias, ffn_out, ffn_out_bias,
):
    here = lax.axis_index("tensor")
    width = src_embed.shape[2]
    local = attn_in.shape[3]
    hidden_width = ffn_in.shape[2]
    source_own = src_embed.reshape(-1, width)
    target_own = tgt_embed.reshape(-1, width)
    enc_own = enc_cot.reshape(-1, width)
    dec_own = dec_cot.reshape(-1, width)
    source_other = swap(source_own)
    target_other = swap(target_own)
    enc_other = swap(enc_own)
    dec_other = swap(dec_own)
    loss_own = loss_mask.reshape(-1, 1).astype(F32)
    loss_all = jnp.concatenate([loss_own, swap(loss_own)], axis=0)
    sources = 2 * source_own.shape[0]
    targets = 2 * target_own.shape[0]

    def ordered(mask):
        pieces = mask.reshape(2, -1)
        return jnp.where(here == 0, pieces, pieces[::-1]).reshape(-1)

    position = lax.rem(
        jnp.arange(targets, dtype=jnp.int32) + here * (targets // 2), targets
    ).astype(F32)
    source_keys = jnp.where(ordered(src_mask) == 1, 0.0, FAR)[:, None]
    target_keys = jnp.where(ordered(tgt_mask) == 1, position, FAR)[:, None]
    nowhere_source = jnp.zeros((1, sources), F32)
    nowhere_target = jnp.zeros((1, targets), F32)
    target_queries = position[None, :]
    flag = objective.astype(F32)[0]
    enc_weight = jnp.broadcast_to(1.0 - 0.5 * flag, (sources, 1))
    dec_weight = (0.5 + 0.5 * flag) * (0.25 + 0.75 * loss_all)

    gains = [norm_gain[i : i + 1] for i in range(5)]
    offsets = [norm_bias[i : i + 1] for i in range(5)]
    b_out = [attn_out_bias[i : i + 1] for i in range(3)]
    b_two = [ffn_out_bias[i : i + 1] for i in range(2)]
    b_one = [ffn_in_bias[i : i + 1] for i in range(2)]

    def first_attention(own, other, norm, layer, key_at, query_at):
        count = 2 * own.shape[0]
        narrow = shape(count, local, BF16)
        return run(
            first_attention_body,
            (
                shape(count, width, BF16), narrow, narrow, narrow,
                shape(local, count, BF16), shape(8, count, F32),
                shape(count, width, F32), shape(count, width, BF16),
            ),
            own, other, gains[norm], offsets[norm], attn_in[layer], attn_in_bias[layer],
            attn_out[layer], b_out[layer], key_at, query_at,
            scratch=[pltpu.VMEM((count, local), BF16)],
            flops=8 * count * width * local + 4 * count * count * local,
        )

    def feed(before, recv, norm, layer):
        count = before.shape[0]
        return run(
            feed_body,
            (
                shape(count, width, F32), shape(count, width, BF16),
                shape(count, hidden_width, BF16), shape(count, hidden_width, BF16),
                shape(count, width, F32), shape(count, width, BF16),
            ),
            before, recv, gains[norm], offsets[norm], ffn_in[layer], b_one[layer],
            ffn_out[layer], b_two[layer],
            flops=4 * count * width * hidden_width,
        )

    h0, q0, k0, v0, turned0, log0, base0, send0 = first_attention(
        source_own, source_other, 0, 0, source_keys, nowhere_source
    )
    recv0 = swap(send0)
    h2, q1, k1, v1, turned1, log1, base1, send1 = first_attention(
        target_own, target_other, 2, 1, target_keys, target_queries
    )
    x1, h1, f0, slope0, base2, send2 = feed(base0, recv0, 1, 0)
    recv2 = swap(send2)
    recv1 = swap(send1)
    narrow = shape(sources, local, BF16)
    memory, k2, v2 = run(
        memory_body, (shape(sources, width, BF16), narrow, narrow),
        base2, recv2, attn_in[2], attn_in_bias[2],
        flops=4 * sources * width * local,
    )
    x3, h3, q2, turned2, log2, base3, send3 = run(
        cross_attention_body,
        (
            shape(targets, width, F32), shape(targets, width, BF16),
            shape(targets, local, BF16), shape(local, targets, BF16), shape(8, targets, F32),
            shape(targets, width, F32), shape(targets, width, BF16),
        ),
        base1, recv1, gains[3], offsets[3], attn_in[2], attn_in_bias[2], attn_out[2], b_out[2],
        k2, v2, source_keys, nowhere_target,
        scratch=[pltpu.VMEM((targets, local), BF16)],
        flops=4 * targets * width * local + 4 * targets * sources * local,
    )
    recv3 = swap(send3)
    x4, h4, f1, slope1, base4, send4 = feed(base3, recv3, 4, 1)
    half = targets // 2
    decoded = (base4[:half] + swap(send4[half:]).astype(F32)).astype(BF16)

    def feed_back(kind, cot, other, weight, extra, layer, slope):
        count = 2 * cot.shape[0]
        return run(
            functools.partial(feed_back_body, kind),
            (
                shape(count, width, F32), shape(count, width, BF16),
                shape(count, hidden_width, BF16),
                shape(count, width, F32), shape(count, width, BF16),
                shape(1, width, F32), shape(1, hidden_width, F32),
            ),
            cot, other, weight, *extra, ffn_in[layer], ffn_out[layer], slope,
            flops=4 * count * width * hidden_width,
        )

    def attention_back(kind, g, dh, recv, x, norm, layer, q, k, v, log, key_at, query_at):
        count = q.shape[0]
        keys = k.shape[0]
        outs = [
            shape(count, width, F32), shape(count, width, BF16),
            shape(count, local, BF16), shape(keys, local, BF16), shape(keys, local, BF16),
        ]
        if kind == "cross":
            outs += [
                shape(count, width, F32), shape(count, width, BF16),
                shape(keys, width, F32), shape(keys, width, BF16),
            ]
        else:
            outs += [shape(count // 2, width, F32), shape(count // 2, width, BF16)]
        outs += [shape(2, width, F32), shape(1, width, F32), shape(2, local, F32)]
        return run(
            functools.partial(attention_back_body, kind), outs,
            g, dh, recv, x, gains[norm], attn_in[layer], attn_out[layer], q, k, v, log,
            key_at, query_at,
            scratch=[pltpu.VMEM((count, local), BF16), pltpu.VMEM((local, count), F32)],
            flops=8 * count * width * local + 10 * count * keys * local,
        )

    core = bits_of_dp()[0][1]

    def feed_weights(h, du, f, low):
        out = shape(2 * width, width, BF16)
        return run(
            feed_weights_body, (out, out), core, h, du, f, low, scalars=1,
            flops=4 * h.shape[0] * width * hidden_width,
        )

    def attention_weights(h, mem, dq, dk, dv, turned, low):
        out = shape(width, width, BF16)
        return run(
            attention_weights_body, (out, out), core, h, mem, dq, dk, dv, turned, low, scalars=1,
            flops=8 * h.shape[0] * width * local,
        )

    def last_norm(g, dh, recv, own, norm):
        rows = own.shape[0]
        return run(
            last_norm_body, (shape(rows, width, F32), shape(2, width, F32)),
            g, dh, recv, own, gains[norm],
        )

    g4, low4, du1, dh4, dh4_send, two1, one1 = feed_back(
        "dec", dec_own, dec_other, dec_weight, (), 1, slope1
    )
    dh4_recv = swap(dh4_send)
    sum_feed1 = scatter_sum(*feed_weights(h4, du1, f1, low4))
    (
        g3, low3, dq2, dk2, dv2, dh3, dh3_send, mem_grad, mem_send, norm4, out2, in2,
    ) = attention_back(
        "cross", g4, dh4, dh4_recv, x4, 4, 2, q2, k2, v2, log2, source_keys, nowhere_target
    )
    mem_recv = swap(mem_send)
    dh3_recv = swap(dh3_send)
    sum_cross = scatter_sum(*attention_weights(h3, memory, dq2, dk2, dv2, turned2, low3))
    g1, low1, du0, dh1, dh1_send, two0, one0 = feed_back(
        "enc", enc_own, enc_other, enc_weight, (mem_grad, mem_recv), 0, slope0
    )
    dh1_recv = swap(dh1_send)
    sum_feed0 = scatter_sum(*feed_weights(h1, du0, f0, low1))
    g0, low0, dq0, dk0, dv0, dh0, dh0_send, norm1, out0, in0 = attention_back(
        "self", g1, dh1, dh1_recv, x1, 1, 0, q0, k0, v0, log0, source_keys, nowhere_source
    )
    dh0_recv = swap(dh0_send)
    sum_first = scatter_sum(*attention_weights(h0, h0, dq0, dk0, dv0, turned0, low0))
    g2, low2, dq1, dk1, dv1, dh2, dh2_send, norm3, out1, in1 = attention_back(
        "self", g3, dh3, dh3_recv, x3, 3, 1, q1, k1, v1, log1, target_keys, target_queries
    )
    dh2_recv = swap(dh2_send)
    sum_self = scatter_sum(*attention_weights(h2, h2, dq1, dk1, dv1, turned1, low2))
    source_grad, norm0 = last_norm(g0, dh0, dh0_recv, source_own, 0)
    target_grad, norm2 = last_norm(g2, dh2, dh2_recv, target_own, 2)

    shapes = {
        "attn_in": attn_in.shape, "attn_out": attn_out.shape,
        "ffn_in": ffn_in.shape, "ffn_out": ffn_out.shape,
    }
    stacks = {}
    early = lax.all_gather(jnp.concatenate([sum_feed1, sum_cross], axis=0), "dp")
    place_feed(early, 0, 1, stacks, shapes)
    place_attention(early, sum_feed1.shape[0], 2, stacks, shapes)
    late = lax.all_gather(jnp.concatenate([sum_feed0, sum_first, sum_self], axis=0), "dp")
    place_feed(late, 0, 0, stacks, shapes)
    place_attention(late, sum_feed0.shape[0], 0, stacks, shapes)
    place_attention(late, sum_feed0.shape[0] + sum_first.shape[0], 1, stacks, shapes)

    norms = [norm0, norm1, norm2, norm3, norm4]
    shared = jnp.concatenate(
        [n[0:1] for n in norms] + [n[1:2] for n in norms] + [out0, out1, out2, two0, two1], axis=0
    )
    apart = jnp.concatenate(
        [v.reshape(-1) for v in (in0, in1, in2, one0, one1)]
    ).reshape(-1, width)
    shared = shared + swap(shared)
    summed = total_small(jnp.concatenate([shared, apart], axis=0))
    shared, apart = summed[:15], summed[15:].reshape(-1)
    bias_rows = apart[: 6 * local].reshape(3, 2, local)
    hidden_rows = apart[6 * local :].reshape(2, -1)
    return (
        memory[: sources // 2][:, None],
        decoded[:, None],
        source_grad[:, None],
        target_grad[:, None],
        shared[0:5],
        shared[5:10],
        stacks["attn_in"],
        bias_rows,
        stacks["attn_out"],
        shared[10:13],
        stacks["ffn_in"],
        hidden_rows,
        stacks["ffn_out"],
        shared[13:15],
    )


def solution(mesh):
    tokens = P("tensor", "dp", None)
    return jax.shard_map(
        on_device,
        mesh=mesh,
        in_specs=(
            tokens, tokens, P("dp", None), P("dp", None), P("dp"), P("dp", "tensor"),
            tokens, tokens, P(), P(),
            P(None, None, None, "tensor"), P(None, None, "tensor"), P(None, "tensor", None), P(),
            P(None, None, "tensor"), P(None, "tensor"), P(None, "tensor", None), P(),
        ),
        out_specs=(
            tokens, tokens, tokens, tokens, P(), P(),
            P(None, None, None, "tensor"), P(None, None, "tensor"), P(None, "tensor", None), P(),
            P(None, None, "tensor"), P(None, "tensor"), P(None, "tensor", None), P(),
        ),
        check_vma=False,
    )
```

```python
import functools

import jax
import jax.numpy as jnp
from jax import lax
from jax.experimental import pallas as pl
from jax.experimental.pallas import tpu as pltpu
from jax.sharding import PartitionSpec as P

HEAD = 64
PAIR = 2 * HEAD
EPSILON = 1e-05
MASKED_SCORE = -1000000000.0
FAR = 1e9
ROOT = 0.7978845608028654
CUBIC = 0.044715
BF16 = jnp.bfloat16
F32 = jnp.float32
VMEM_LIMIT = 18 * 1024 * 1024
BYTES = 3690000
NN = ((1,), (0,))
NT = ((1,), (1,))
TN = ((0,), (0,))
TOKEN = jax.ShapeDtypeStruct((8, 128), F32)


def dot(left, right, contract):
    return lax.dot_general(left, right, (contract, ((), ())), preferred_element_type=F32)


def shape(rows, columns, dtype):
    return jax.ShapeDtypeStruct((rows, columns), dtype)


NEAR = pl.BlockSpec(memory_space=pltpu.VMEM)
AWAY = pl.BlockSpec(memory_space=pl.ANY)
NUMBER = pl.BlockSpec(memory_space=pltpu.SMEM)


class Weight:
    def __init__(self, stack, layer):
        self.stack = stack
        self.layer = layer


class Params:
    def __init__(self, *arrays):
        self.arrays = arrays


class Fetch:
    def __init__(self, source, buffer, semaphore):
        self.copy = pltpu.make_async_copy(source, buffer, semaphore)
        self.copy.start()
        self.buffer = buffer
        self.arrived = False

    def here(self):
        if not self.arrived:
            self.copy.wait()
            self.arrived = True
        return self.buffer


class Order:
    def __init__(self):
        self.token = None

    def call(self, body, outs, ins, microseconds=1, scratch=(), leave=(), limit=VMEM_LIMIT):
        tokens = [] if self.token is None else [self.token]
        specs, args, weights, groups = [], [], [], []
        for value in ins:
            if isinstance(value, Params):
                groups.append(len(args))
                for array in value.arrays:
                    specs.append(NEAR)
                    args.append(pltpu.with_memory_space_constraint(array, pltpu.VMEM))
            elif isinstance(value, Weight):
                weights.append((len(args), value))
                specs.append(AWAY)
                args.append(pltpu.with_memory_space_constraint(value.stack, pltpu.HBM))
            elif value.dtype == jnp.int32 and value.shape == (1,):
                specs.append(NUMBER)
                args.append(value)
            else:
                specs.append(NEAR)
                args.append(pltpu.with_memory_space_constraint(value, pltpu.VMEM))

        def wrapped(*refs):
            in_refs = list(refs[: len(args)])
            refs = refs[len(args) + len(tokens) :]
            out_refs = refs[: len(outs)]
            refs = refs[len(outs) + 1 :]
            if weights:
                semaphores = refs[-1]
                for i, (at, weight) in enumerate(weights):
                    in_refs[at] = Fetch(in_refs[at].at[weight.layer], refs[i], semaphores.at[i])
            for at in reversed(groups):
                in_refs[at : at + 6] = [in_refs[at : at + 6]]
            body(*in_refs, *out_refs, *refs[len(weights) : len(weights) + len(scratch)])

        buffers = [pltpu.VMEM(w.stack.shape[1:], w.stack.dtype) for unused, w in weights]
        semaphores = [pltpu.SemaphoreType.DMA((len(weights),))] if weights else []
        results = pl.pallas_call(
            wrapped,
            out_shape=[
                *[o if i in leave else pltpu.VMEM(o.shape, o.dtype) for i, o in enumerate(outs)],
                TOKEN,
            ],
            in_specs=specs + [AWAY] * len(tokens),
            out_specs=[NEAR] * len(outs) + [AWAY],
            scratch_shapes=[*buffers, *scratch, *semaphores],
            compiler_params=pltpu.CompilerParams(vmem_limit_bytes=limit),
            cost_estimate=pl.CostEstimate(
                flops=0, transcendentals=0, bytes_accessed=int(microseconds * BYTES)
            ),
        )(*args, *tokens)
        self.token = results[-1]
        return results[:-1]


def norm_parts(inputs):
    centre = inputs - jnp.mean(inputs, axis=-1, keepdims=True)
    inverse = lax.rsqrt(jnp.mean(centre * centre, axis=-1, keepdims=True) + EPSILON)
    return centre * inverse, inverse


def norm_back(gradient, normed, inverse, gain):
    scaled = gradient * gain
    mean_plain = jnp.mean(scaled, axis=-1, keepdims=True)
    mean_normed = jnp.mean(scaled * normed, axis=-1, keepdims=True)
    return inverse * (scaled - mean_plain - normed * mean_normed)


def column_sum(values):
    return jnp.sum(values.astype(F32), axis=0, keepdims=True)


def halves(count):
    half = count // 2
    return ((0, half), (half, 0))


def lane_half(which, rows):
    lanes = lax.broadcasted_iota(jnp.int32, (rows, PAIR), 1)
    return (lanes >= HEAD) if which else (lanes < HEAD)


def only_head(which, values):
    return jnp.where(lane_half(which, values.shape[0]), values, jnp.zeros_like(values))


def key_scores(key_pair, query_pair, which, key_at, query_at):
    scores = dot(only_head(which, key_pair), query_pair, NT)
    return jnp.where(key_at <= query_at, scores, MASKED_SCORE)


def attend(q_ref, k_ref, v_ref, key_at, query_at_ref, turned_ref, o_ref, log_ref):
    queries, local = q_ref.shape
    block = min(queries, 256)
    for pair in range(local // PAIR):
        columns = pl.ds(pair * PAIR, PAIR)
        key_pair = k_ref[:, columns]
        value_turned = v_ref[:, columns].astype(F32).T.astype(BF16)
        for start in range(0, queries, block):
            rows = pl.ds(start, block)
            query_pair = q_ref[rows, columns]
            query_at = 0.0 if query_at_ref is None else query_at_ref[:, rows]
            for which in range(2):
                head = 2 * pair + which
                scores = key_scores(key_pair, query_pair, which, key_at, query_at)
                top = jnp.max(scores, axis=0, keepdims=True)
                exponent = jnp.exp(scores - top)
                total = jnp.sum(exponent, axis=0, keepdims=True)
                weights = (exponent * (1.0 / total)).astype(BF16)
                log_ref[pl.ds(head, 1), rows] = top + jnp.log(total)
                mixed = dot(value_turned[which * HEAD : (which + 1) * HEAD], weights, NN)
                turned_ref[pl.ds(head * HEAD, HEAD), rows] = mixed.astype(BF16)
    o_ref[...] = turned_ref[...].astype(F32).T.astype(BF16)


def in_bias_rows(params, layer):
    return params[4][layer, 0:1], params[4][layer, 1:2]


def row_of(ref, index):
    return ref[index : index + 1]


def normalised(value, params, norm):
    normed, unused = norm_parts(value)
    return (normed * row_of(params[0], norm) + row_of(params[1], norm)).astype(BF16)


def column(row):
    return jnp.broadcast_to(row, (8, row.shape[1])).T[:, 0:1]


def own_first(row, here):
    half = row.shape[1] // 2
    return jnp.where(here == 0, row, jnp.concatenate([row[:, half:], row[:, :half]], axis=1))


def scaled_queries(hidden, w_in, bias):
    return ((dot(hidden, w_in[0], NN) + bias).astype(BF16) * HEAD ** (-0.5)).astype(BF16)


def first_attention(norm, layer, own_ref, other_ref, params, w_in, w_out, key_at, query_at_ref, *refs):
    h_ref, q_ref, k_ref, v_ref, turned_ref, log_ref, base_ref, send_ref, o_ref = refs
    half = own_ref.shape[0]
    query_bias, value_bias = in_bias_rows(params, layer)
    for part, source in enumerate((own_ref, other_ref)):
        rows = pl.ds(part * half, half)
        hidden = normalised(source[...].astype(F32), params, norm)
        h_ref[rows] = hidden
        w = w_in.here()
        q_ref[rows] = scaled_queries(hidden, w, query_bias)
        k_ref[rows] = dot(hidden, w[1], NN).astype(BF16)
        v_ref[rows] = (dot(hidden, w[2], NN) + value_bias).astype(BF16)
    attend(q_ref, k_ref, v_ref, key_at, query_at_ref, turned_ref, o_ref, log_ref)
    w = w_out.here()
    for part, source in enumerate((own_ref, other_ref)):
        rows = pl.ds(part * half, half)
        partial = dot(o_ref[rows], w[...], NN)
        send_ref[rows] = partial.astype(BF16)
        base_ref[rows] = source[...].astype(F32) + row_of(params[2], layer) + partial


def enc_first_body(norm, layer, own_ref, other_ref, params, w_in, w_out, mask_ref, here_ref, *refs):
    outs, key_at_ref, o_ref = refs[:-2], refs[-2], refs[-1]
    row = own_first(jnp.where(mask_ref[...] == 1, 0.0, FAR), here_ref[0])
    key_at = column(row)
    key_at_ref[...] = key_at
    first_attention(norm, layer, own_ref, other_ref, params, w_in, w_out, key_at, None, *outs, o_ref)


def dec_first_body(
    norm, layer, own_ref, other_ref, params, w_in, w_out, mask_ref, here_ref,
    cot_ref, loss_ref, objective_ref, place_ref, *refs
):
    outs, (key_at_ref, query_at_ref, gradient_ref, gradient_send_ref, o_ref) = refs[:-5], refs[-5:]
    count = mask_ref.shape[1]
    position = own_first(
        lax.broadcasted_iota(jnp.int32, (1, count), 1).astype(F32), here_ref[0]
    )
    row = jnp.where(own_first(mask_ref[...].astype(F32), here_ref[0]) == 1.0, position, FAR)
    key_at = column(row)
    key_at_ref[...] = key_at
    query_at_ref[...] = position
    flag = objective_ref[0].astype(F32)
    weight = column(0.25 + 0.75 * loss_ref[...].astype(F32)) * (0.5 + 0.5 * flag)
    gradient = cot_ref[...].astype(F32) * weight
    gradient_ref[...] = gradient
    gradient_send_ref[...] = gradient.astype(BF16)
    first_attention(
        norm, layer, own_ref, other_ref, params, w_in, w_out, key_at, query_at_ref, *outs, o_ref
    )


def cross_attention_body(
    norm, layer, before_ref, recv_ref, params, w_in, w_out, k_ref, v_ref, key_at_ref,
    x_ref, h_ref, q_ref, turned_ref, log_ref, base_ref, send_ref, o_ref,
):
    count = x_ref.shape[0]
    half = count // 2
    query_bias, unused = in_bias_rows(params, layer)
    for mine, theirs in halves(count):
        rows = pl.ds(mine, half)
        value = before_ref[rows] + recv_ref[pl.ds(theirs, half)].astype(F32)
        x_ref[rows] = value
        hidden = normalised(value, params, norm)
        h_ref[rows] = hidden
        q_ref[rows] = scaled_queries(hidden, w_in.here(), query_bias)
    attend(q_ref, k_ref, v_ref, key_at_ref[...], None, turned_ref, o_ref, log_ref)
    partial = dot(o_ref[...], w_out.here()[...], NN)
    send_ref[...] = partial.astype(BF16)
    base_ref[...] = x_ref[...] + row_of(params[2], layer) + partial


def memory_body(layer, before_ref, recv_ref, params, w_in, mem_ref, k_ref, v_ref):
    count = mem_ref.shape[0]
    half = count // 2
    unused, value_bias = in_bias_rows(params, layer)
    for mine, theirs in halves(count):
        rows = pl.ds(mine, half)
        memory = (before_ref[rows] + recv_ref[pl.ds(theirs, half)].astype(F32)).astype(BF16)
        mem_ref[rows] = memory
        w = w_in.here()
        k_ref[rows] = dot(memory, w[1], NN).astype(BF16)
        v_ref[rows] = (dot(memory, w[2], NN) + value_bias).astype(BF16)


def feed_body(
    norm, layer, before_ref, recv_ref, params, w_one, w_two,
    x_ref, h_ref, f_ref, slope_ref, base_ref, send_ref,
):
    count = x_ref.shape[0]
    half = count // 2
    for mine, theirs in halves(count):
        rows = pl.ds(mine, half)
        value = before_ref[rows] + recv_ref[pl.ds(theirs, half)].astype(F32)
        x_ref[rows] = value
        hidden = normalised(value, params, norm)
        h_ref[rows] = hidden
        u = dot(hidden, w_one.here()[...], NN) + row_of(params[5], layer)
        square = u * u
        bent = jnp.tanh(u * (ROOT + (ROOT * CUBIC) * square))
        upper = 0.5 + 0.5 * bent
        active = (u * upper).astype(BF16)
        f_ref[rows] = active
        slope = upper + (0.5 * u) * (1.0 - bent * bent) * (ROOT + (3 * ROOT * CUBIC) * square)
        slope_ref[rows] = slope.astype(BF16)
        partial = dot(active, w_two.here()[...], NN)
        send_ref[rows] = partial.astype(BF16)
        base_ref[rows] = value + row_of(params[3], layer) + partial


def feed_back_rows(
    gradient, rows, w_one, w_two, slope_ref, g_ref, low_ref, du_ref, base_ref, send_ref
):
    g_ref[rows] = gradient
    low = gradient.astype(BF16)
    low_ref[rows] = low
    du = (dot(low, w_two.here()[...], NT) * slope_ref[rows].astype(F32)).astype(BF16)
    du_ref[rows] = du
    partial = dot(du, w_one.here()[...], NT)
    send_ref[rows] = partial.astype(BF16)
    base_ref[rows] = partial


def dec_feed_back_body(own_ref, other_ref, w_one, w_two, slope_ref, *outs):
    half = own_ref.shape[0]
    for part, source in enumerate((own_ref, other_ref)):
        feed_back_rows(
            source[...].astype(F32), pl.ds(part * half, half), w_one, w_two, slope_ref, *outs
        )


def source_seed(cot_ref, objective_ref):
    return cot_ref[...].astype(F32) * (1.0 - 0.5 * objective_ref[0].astype(F32))


def enc_feed_back_body(seed_ref, objective_ref, mem_base_ref, recv_ref, w_one, w_two, slope_ref, *outs):
    half = seed_ref.shape[0]
    own, other = pl.ds(0, half), pl.ds(half, half)
    for rows, theirs in ((own, other), (other, own)):
        gradient = mem_base_ref[rows] + recv_ref[theirs].astype(F32)
        if rows is own:
            gradient = gradient + source_seed(seed_ref, objective_ref)
        feed_back_rows(gradient, rows, w_one, w_two, slope_ref, *outs)


def attention_back_body(norm, cross, causal, *refs):
    (g_in_ref, dh_ref, dh_recv_ref, x_ref, params, w_in, w_out, q_ref, k_ref, v_ref, log_ref,
     key_at_ref), refs = refs[:12], refs[12:]
    query_at_ref = seed_ref = mem_base_ref = mem_send_ref = None
    if causal:
        query_at_ref, refs = refs[0], refs[1:]
    if cross:
        (seed_ref, objective_ref), refs = refs[:2], refs[2:]
    (g_ref, low_ref, dq_ref, dk_ref, dv_ref, base_ref, send_ref), refs = refs[:7], refs[7:]
    if cross:
        (mem_base_ref, mem_send_ref), refs = refs[:2], refs[2:]
    sums_ref, do_ref, turned_ref = refs
    gain = row_of(params[0], norm)
    count, local = dq_ref.shape
    half = count // 2
    for part, (mine, theirs) in enumerate(halves(count)):
        rows = pl.ds(mine, half)
        normed, inverse = norm_parts(x_ref[rows])
        dh = dh_ref[rows] + dh_recv_ref[pl.ds(theirs, half)].astype(F32)
        gradient = g_in_ref[rows] + norm_back(dh, normed, inverse, gain)
        g_ref[rows] = gradient
        low = gradient.astype(BF16)
        low_ref[rows] = low
        if part == 0:
            sums_ref[0:1] = column_sum(dh * normed)
            sums_ref[1:2] = column_sum(dh)
            sums_ref[2:3] = column_sum(low)
        do_ref[rows] = dot(low, w_out.here()[...], NT).astype(BF16)
    key_at = key_at_ref[...]
    block = min(count, 256)
    keys = k_ref.shape[0]
    for pair in range(local // PAIR):
        columns = pl.ds(pair * PAIR, PAIR)
        key_pair = k_ref[:, columns]
        key_turned = key_pair.astype(F32).T.astype(BF16)
        value_pair = v_ref[:, columns]
        dk = [None, None]
        dv = [None, None]
        for start in range(0, count, block):
            rows = pl.ds(start, block)
            query_pair = q_ref[rows, columns]
            do_pair = do_ref[rows, columns]
            query_at = 0.0 if query_at_ref is None else query_at_ref[:, rows]
            for which in range(2):
                head = 2 * pair + which
                scores = key_scores(key_pair, query_pair, which, key_at, query_at)
                probs = jnp.exp(scores - log_ref[pl.ds(head, 1), rows])
                prob_grad = dot(only_head(which, value_pair), do_pair, NT)
                product = probs * prob_grad
                inner = jnp.sum(product, axis=0, keepdims=True)
                score_grad = (product - probs * inner).astype(BF16)
                dv_part = dot(probs.astype(BF16), do_pair, NN)
                dk_part = dot(score_grad, query_pair, NN)
                dq_part = dot(key_turned[which * HEAD : (which + 1) * HEAD], score_grad, NN)
                turned_ref[pl.ds(head * HEAD, HEAD), rows] = dq_part * HEAD ** (-0.5)
                dk[which] = dk_part if dk[which] is None else dk[which] + dk_part
                dv[which] = dv_part if dv[which] is None else dv[which] + dv_part
        first = lane_half(0, keys)
        dk_ref[:, columns] = jnp.where(first, dk[0], dk[1]).astype(BF16)
        dv_ref[:, columns] = jnp.where(first, dv[0], dv[1]).astype(BF16)
    dq_ref[...] = turned_ref[...].T.astype(BF16)
    w = w_in.here()
    if cross:
        partial = dot(dk_ref[...], w[1], NT) + dot(dv_ref[...], w[2], NT)
        mem_base_ref[...] = partial
        mem_half = keys // 2
        mem_send_ref[0:mem_half] = (
            partial[0:mem_half] + source_seed(seed_ref, objective_ref)
        ).astype(BF16)
        mem_send_ref[mem_half:] = partial[mem_half:].astype(BF16)
        partial = dot(dq_ref[...], w[0], NT)
        send_ref[...] = partial.astype(BF16)
        base_ref[...] = partial
    else:
        for part in (1, 0):
            rows = pl.ds(part * half, half)
            partial = (
                dot(dq_ref[rows], w[0], NT)
                + dot(dk_ref[rows], w[1], NT)
                + dot(dv_ref[rows], w[2], NT)
            )
            if part == 1:
                send_ref[...] = partial.astype(BF16)
            else:
                base_ref[...] = partial


def last_norm_body(norm, g_ref, dh_ref, recv_ref, x_ref, params, out_ref, sums_ref):
    normed, inverse = norm_parts(x_ref[...].astype(F32))
    dh = dh_ref[...] + recv_ref[...].astype(F32)
    sums_ref[0:1] = column_sum(dh * normed)
    sums_ref[1:2] = column_sum(dh)
    half = out_ref.shape[0]
    out_ref[...] = g_ref[0:half] + norm_back(dh, normed, inverse, row_of(params[0], norm))


def feed_weights_body(h_ref, du_ref, f_ref, low_ref, place_ref, send_ref, keep_ref, sums_ref, hidden_sums_ref):
    bit = bit_of(place_ref, 0)
    width = h_ref.shape[1]
    part = width // 2
    for which, out_ref in ((1 - bit, send_ref), (bit, keep_ref)):
        left = h_ref[:, pl.ds(pl.multiple_of(which * part, 128), part)]
        for side in range(2):
            out_ref[pl.ds(side * part, part)] = dot(
                left, du_ref[:, pl.ds(side * width, width)], TN
            ).astype(BF16)
        left = f_ref[:, pl.ds(pl.multiple_of(which * width, 128), width)]
        out_ref[pl.ds(width, width)] = dot(left, low_ref[...], TN).astype(BF16)
    half = low_ref.shape[0] // 2
    sums_ref[...] = column_sum(low_ref[0:half])
    hidden_sums_ref[...] = column_sum(du_ref[...])


def attention_weights_body(
    h_ref, mem_ref, dq_ref, dk_ref, dv_ref, turned_ref, low_ref, place_ref, send_ref, keep_ref, sums_ref
):
    bit = bit_of(place_ref, 0)
    width = h_ref.shape[1]
    part = width // 2
    quarter = width // 4
    left_side = pl.ds(0, part)
    right_side = pl.ds(part, part)
    for which, out_ref in ((1 - bit, send_ref), (bit, keep_ref)):
        columns = pl.ds(pl.multiple_of(which * part, 128), part)
        out_ref[pl.ds(0, part), left_side] = dot(h_ref[:, columns], dq_ref[...], TN).astype(BF16)
        memory = mem_ref[:, columns]
        out_ref[pl.ds(0, part), right_side] = dot(memory, dk_ref[...], TN).astype(BF16)
        values = dot(memory, dv_ref[...], TN).astype(BF16)
        out_ref[pl.ds(part, quarter), left_side] = values[:quarter]
        out_ref[pl.ds(part, quarter), right_side] = values[quarter:]
        rows = pl.ds(pl.multiple_of(which * quarter, 64), quarter)
        out_ref[pl.ds(part + quarter, quarter)] = dot(turned_ref[rows], low_ref[...], NN).astype(BF16)
    sums_ref[:, left_side] = column_sum(dq_ref[...])
    sums_ref[:, right_side] = column_sum(dv_ref[...])


def bit_of(place_ref, step):
    return (place_ref[0] >> step) & 1


def add_body(step, keep_ref, received_ref, place_ref, send_ref, next_ref):
    bit = bit_of(place_ref, step)
    rows = send_ref.shape[0]
    block = rows
    while block % 32 == 0 and block > 128:
        block //= 2
    for out_ref, which in ((send_ref, 1 - bit), (next_ref, bit)):
        for start in range(0, rows, block):
            part = pl.ds(pl.multiple_of(which * rows + start, 8), block)
            out_ref[pl.ds(start, block)] = (
                keep_ref[part].astype(F32) + received_ref[part].astype(F32)
            ).astype(BF16)


def last_sums_body(*refs):
    out_ref = refs[-1]
    first = 0
    for keep_ref, received_ref in zip(refs[:-1:2], refs[1:-1:2]):
        rows = keep_ref.shape[0]
        total = keep_ref[...].astype(F32) + received_ref[...].astype(F32)
        out_ref[pl.ds(first, rows)] = total.astype(BF16)
        first += rows


def pass_body(value_ref, unused_ref, out_ref):
    out_ref[...] = value_ref[...]


def swap(values):
    return lax.ppermute(values, "tensor", [(0, 1), (1, 0)])


def strides_of_dp():
    return [1 << b for b in range(lax.axis_size("dp").bit_length() - 1)]


def across(values, stride):
    count = lax.axis_size("dp")
    return lax.ppermute(values, "dp", [(i, i ^ stride) for i in range(count)])


class Halving:
    def __init__(self, send, keep, place):
        self.strides = strides_of_dp()
        self.place = place
        self.at = 0
        self.keep = keep
        self.received = across(send, self.strides[0])

    def pending(self):
        return self.at + 1 < len(self.strides)

    def step(self, order):
        self.at += 1
        rows, width = self.keep.shape
        send, self.keep = order.call(
            functools.partial(add_body, self.at), [shape(rows // 2, width, BF16)] * 2,
            [self.keep, self.received, self.place],
        )
        self.received = across(send, self.strides[self.at])


def last_sums(order, halvings):
    rows = [part.keep.shape[0] for part in halvings]
    ins = [value for part in halvings for value in (part.keep, part.received)]
    (result,) = order.call(
        last_sums_body, [shape(sum(rows), halvings[0].keep.shape[1], BF16)], ins, leave=[0]
    )
    return result


def turned_index(index, count):
    bits = count.bit_length() - 1
    return sum(((index >> b) & 1) << (bits - 1 - b) for b in range(bits))


def place_body(count, width, groups, in_ref, *refs):
    wide_ref, semaphores = refs[-2:]
    outs = dict(zip(("ffn_in", "ffn_out", "attn_in", "attn_out"), refs[-7:-3]))
    step = pl.program_id(0)
    shard = turned_index(step, count)
    per_half = count // 2
    upper = lax.div(shard, per_half)
    index = lax.rem(shard, per_half)
    part = width // 2
    quarter = width // 4
    slot = lax.rem(step, 2)

    def copies(at):
        made = []
        for i, (kind, layer, first, rows) in enumerate(groups):
            for side in range(2):
                source = wide_ref.at[at, pl.ds(first, rows), pl.ds(side * part, part)]
                made.append((source, semaphores.at[at, 2 * i + side]))
        return made

    def wait(at):
        for i, (source, semaphore) in enumerate(copies(at)):
            rows = groups[i // 2][3]
            target = outs["ffn_out"].at[0, pl.ds(0, rows), pl.ds(0, part)]
            pltpu.make_async_copy(source, target, semaphore).wait()

    @pl.when(step >= 2)
    def free():
        wait(slot)

    wide_ref[slot] = in_ref[0].astype(F32)
    pairs = copies(slot)
    for i, (kind, layer, first, rows) in enumerate(groups):
        narrow = part // rows
        sources = pairs[2 * i : 2 * i + 2]

        def send(side, target):
            source, semaphore = sources[side]
            pltpu.make_async_copy(source, target, semaphore).start()

        if kind == "feed":
            column = lax.div(index, narrow)

            @pl.when(index < 2 * narrow)
            def first_matrix():
                row = pl.multiple_of(upper * part + lax.rem(index, narrow) * rows, 8)
                for side in range(2):
                    columns = pl.multiple_of(column * width + side * part, 128)
                    send(side, outs["ffn_in"].at[layer, pl.ds(row, rows), pl.ds(columns, part)])

            @pl.when(index >= 2 * narrow)
            def second_matrix():
                row = pl.multiple_of(upper * width + (index - 2 * narrow) * rows, 8)
                for side in range(2):
                    send(
                        side,
                        outs["ffn_out"].at[layer, pl.ds(row, rows), pl.ds(side * part, part)],
                    )
        else:
            few = quarter // rows

            @pl.when(index < narrow)
            def query_and_key():
                row = pl.multiple_of(upper * part + index * rows, 8)
                for side in range(2):
                    send(side, outs["attn_in"].at[layer, side, pl.ds(row, rows)])

            @pl.when((index >= narrow) & (index < narrow + few))
            def value():
                row = pl.multiple_of(upper * part + (index - narrow) * rows, 8)
                for side in range(2):
                    send(side, outs["attn_in"].at[layer, 2, pl.ds(row + side * quarter, rows)])

            @pl.when(index >= narrow + few)
            def output():
                row = pl.multiple_of(upper * quarter + (index - narrow - few) * rows, 8)
                for side in range(2):
                    send(
                        side,
                        outs["attn_out"].at[layer, pl.ds(row, rows), pl.ds(side * part, part)],
                    )

    @pl.when(step == count - 1)
    def drain():
        wait(1 - slot)
        wait(slot)


def place(order, gathered, groups, stacks, shapes):
    count, rows, width = gathered.shape
    previous = [] if stacks is None else stacks
    results = pl.pallas_call(
        functools.partial(place_body, count, width, groups),
        grid=(count,),
        out_shape=[*[jax.ShapeDtypeStruct(dims, F32) for dims in shapes], TOKEN],
        in_specs=[pl.BlockSpec((1, rows, width), lambda i: (i, 0, 0))]
        + [AWAY] * (len(previous) + 1),
        out_specs=[AWAY] * 5,
        scratch_shapes=[
            pltpu.VMEM((2, rows, width), F32),
            pltpu.SemaphoreType.DMA((2, 2 * len(groups))),
        ],
        input_output_aliases={1 + i: i for i in range(len(previous))},
        compiler_params=pltpu.CompilerParams(vmem_limit_bytes=VMEM_LIMIT),
        cost_estimate=pl.CostEstimate(flops=0, transcendentals=0, bytes_accessed=10 * BYTES),
    )(gathered, *previous, order.token)
    order.token = results[-1]
    return results[:-1]


def total_small(values):
    for stride in strides_of_dp():
        values = values + across(values, stride)
    return values


def on_device(
    src_embed, tgt_embed, src_mask, tgt_mask, objective, loss_mask, enc_cot, dec_cot,
    norm_gain, norm_bias, attn_in, attn_in_bias, attn_out, attn_out_bias,
    ffn_in, ffn_in_bias, ffn_out, ffn_out_bias,
):
    order = Order()
    here = lax.axis_index("tensor")
    width = src_embed.shape[2]
    local = attn_in.shape[3]
    hidden_width = ffn_in.shape[2]
    source_own = src_embed.reshape(-1, width)
    target_own = tgt_embed.reshape(-1, width)
    sources = 2 * source_own.shape[0]
    targets = 2 * target_own.shape[0]
    enc_own = enc_cot.reshape(-1, width)
    target_other = swap(target_own)
    source_other = swap(source_own)
    params = Params(norm_gain, norm_bias, attn_out_bias, ffn_out_bias, attn_in_bias, ffn_in_bias)
    core = lax.axis_index("dp").astype(jnp.int32).reshape(1)
    here = here.astype(jnp.int32).reshape(1)

    def first(body, own, other, norm, layer, mask, more_ins, more_outs):
        count = 2 * own.shape[0]
        narrow = shape(count, local, BF16)
        return order.call(
            functools.partial(body, norm, layer),
            [
                shape(count, width, BF16), narrow, narrow, narrow,
                shape(local, count, BF16), shape(8, count, F32),
                shape(count, width, F32), shape(count, width, BF16), shape(count, 1, F32),
                *more_outs,
            ],
            [own, other, params, Weight(attn_in, layer), Weight(attn_out, layer), mask, here, *more_ins],
            microseconds=count / 50,
            scratch=[pltpu.VMEM((count, local), BF16)],
        )

    def feed(before, recv, norm, layer):
        count = before.shape[0]
        return order.call(
            functools.partial(feed_body, norm, layer),
            [
                shape(count, width, F32), shape(count, width, BF16),
                shape(count, hidden_width, BF16), shape(count, hidden_width, BF16),
                shape(count, width, F32), shape(count, width, BF16),
            ],
            [before, recv, params, Weight(ffn_in, layer), Weight(ffn_out, layer)],
            microseconds=count / 90,
        )

    (
        h2, q1, k1, v1, turned1, log1, base1, send1, target_keys,
        target_queries, dec_own, dec_send,
    ) = first(
        dec_first_body, target_own, target_other, 2, 1, tgt_mask,
        [dec_cot.reshape(-1, width), loss_mask, objective, core],
        [shape(1, targets, F32), shape(targets // 2, width, F32), shape(targets // 2, width, BF16)],
    )
    recv1 = swap(send1)
    dec_other = swap(dec_send)
    h0, q0, k0, v0, turned0, log0, base0, send0, source_keys = first(
        enc_first_body, source_own, source_other, 0, 0, src_mask, [], []
    )
    recv0 = swap(send0)
    x1, h1, f0, slope0, base2, send2 = feed(base0, recv0, 1, 0)
    recv2 = swap(send2)
    narrow = shape(sources, local, BF16)
    memory, k2, v2 = order.call(
        functools.partial(memory_body, 2), [shape(sources, width, BF16), narrow, narrow],
        [base2, recv2, params, Weight(attn_in, 2)], microseconds=3,
    )
    x3, h3, q2, turned2, log2, base3, send3 = order.call(
        functools.partial(cross_attention_body, 3, 2),
        [
            shape(targets, width, F32), shape(targets, width, BF16),
            shape(targets, local, BF16), shape(local, targets, BF16), shape(8, targets, F32),
            shape(targets, width, F32), shape(targets, width, BF16),
        ],
        [
            base1, recv1, params, Weight(attn_in, 2), Weight(attn_out, 2), k2, v2, source_keys,
        ],
        microseconds=5,
        scratch=[pltpu.VMEM((targets, local), BF16)],
    )
    recv3 = swap(send3)
    x4, h4, f1, slope1, base4, send4 = feed(base3, recv3, 4, 1)

    def feed_back(body, layer, *ins):
        count = ins[-1].shape[0]
        return order.call(
            body,
            [
                shape(count, width, F32), shape(count, width, BF16),
                shape(count, hidden_width, BF16),
                shape(count, width, F32), shape(count, width, BF16),
            ],
            [*ins[:-1], Weight(ffn_in, layer), Weight(ffn_out, layer), ins[-1]],
            microseconds=count / 90,
        )

    def attention_back(cross, causal, g, dh, recv, x, norm, layer, q, k, v, log, key_at, *more):
        count = q.shape[0]
        keys = k.shape[0]
        outs = [
            shape(count, width, F32), shape(count, width, BF16),
            shape(count, local, BF16), shape(keys, local, BF16), shape(keys, local, BF16),
        ]
        if cross:
            outs += [
                shape(count, width, F32), shape(count, width, BF16),
                shape(keys, width, F32), shape(keys, width, BF16),
            ]
        else:
            outs += [shape(count // 2, width, F32), shape(count // 2, width, BF16)]
        outs += [shape(3, width, F32)]
        return order.call(
            functools.partial(attention_back_body, norm, cross, causal), outs,
            [
                g, dh, recv, x, params, Weight(attn_in, layer), Weight(attn_out, layer),
                q, k, v, log, key_at, *more,
            ],
            microseconds=count * keys / 28000,
            scratch=[pltpu.VMEM((count, local), BF16), pltpu.VMEM((local, count), F32)],
        )

    def feed_weights(h, du, f, low):
        out = shape(2 * width, width, BF16)
        send, keep, sums, hidden_sums = order.call(
            feed_weights_body, [out, out, shape(1, width, F32), shape(1, hidden_width, F32)],
            [h, du, f, low, core], microseconds=3,
        )
        return Halving(send, keep, core), sums, hidden_sums

    def attention_weights(h, mem, dq, dk, dv, turned, low):
        out = shape(width, width, BF16)
        send, keep, sums = order.call(
            attention_weights_body, [out, out, shape(1, width, F32)],
            [h, mem, dq, dk, dv, turned, low, core], microseconds=2,
        )
        return Halving(send, keep, core), sums

    def last_norm(g, dh, recv, own, norm):
        rows = own.shape[0]
        return order.call(
            functools.partial(last_norm_body, norm),
            [shape(rows, width, F32), shape(2, width, F32)],
            [g, dh, recv, own, params], leave=[0],
        )

    g4, low4, du1, dh4, dh4_send = feed_back(
        dec_feed_back_body, 1, dec_own, dec_other, slope1
    )
    dh4_recv = swap(dh4_send)
    sum_feed1, two1, one1 = feed_weights(h4, du1, f1, low4)
    g3, low3, dq2, dk2, dv2, dh3, dh3_send, mem_grad, mem_send, sums4 = attention_back(
        True, False, g4, dh4, dh4_recv, x4, 4, 2, q2, k2, v2, log2, source_keys, enc_own, objective
    )
    mem_recv = swap(mem_send)
    sum_feed1.step(order)
    sum_cross, in2 = attention_weights(h3, memory, dq2, dk2, dv2, turned2, low3)
    g1, low1, du0, dh1, dh1_send = feed_back(
        enc_feed_back_body, 0, enc_own, objective, mem_grad, mem_recv, slope0
    )
    dh1_recv = swap(dh1_send)
    sum_feed1.step(order)
    sum_cross.step(order)
    sum_feed0, two0, one0 = feed_weights(h1, du0, f0, low1)
    (dh3_late,) = order.call(
        pass_body, [shape(targets, width, BF16)], [dh3_send, dh1_recv], microseconds=0.5
    )
    dh3_recv = swap(dh3_late)
    g0, low0, dq0, dk0, dv0, dh0, dh0_send, sums1 = attention_back(
        False, False, g1, dh1, dh1_recv, x1, 1, 0, q0, k0, v0, log0, source_keys
    )
    dh0_recv = swap(dh0_send)
    sum_feed1.step(order)
    sum_cross.step(order)
    sum_feed0.step(order)
    sum_first, in0 = attention_weights(h0, h0, dq0, dk0, dv0, turned0, low0)
    g2, low2, dq1, dk1, dv1, dh2, dh2_send, sums3 = attention_back(
        False, True, g3, dh3, dh3_recv, x3, 3, 1, q1, k1, v1, log1, target_keys, target_queries
    )
    dh2_recv = swap(dh2_send)
    sum_self, in1 = attention_weights(h2, h2, dq1, dk1, dv1, turned1, low2)
    sum_first.step(order)
    source_grad, sums0 = last_norm(g0, dh0, dh0_recv, source_own, 0)
    sum_cross.step(order)
    sum_self.step(order)
    target_grad, sums2 = last_norm(g2, dh2, dh2_recv, target_own, 2)
    sum_feed0.step(order)
    early_parts, late_parts = [sum_feed1, sum_cross], [sum_feed0, sum_first, sum_self]
    for parts in (early_parts, late_parts):
        while any(part.pending() for part in parts):
            for part in parts:
                if part.pending():
                    part.step(order)
    early = lax.all_gather(last_sums(order, early_parts), "dp")
    late = lax.all_gather(last_sums(order, late_parts), "dp")
    half = targets // 2
    decoded = (base4[:half] + swap(send4[half:]).astype(F32)).astype(BF16)

    shapes = [ffn_in.shape, ffn_out.shape, attn_in.shape, attn_out.shape]
    wide, thin = sum_feed1.keep.shape[0], sum_cross.keep.shape[0]
    stacks = place(
        order, early, [("feed", 1, 0, wide), ("attention", 2, wide, thin)], None, shapes
    )
    stacks = place(
        order, late,
        [
            ("feed", 0, 0, wide), ("attention", 0, wide, thin),
            ("attention", 1, wide + thin, thin),
        ],
        stacks, shapes,
    )

    sums = [sums0, sums1, sums2, sums3, sums4]
    shared = jnp.concatenate(
        [v[0:1] for v in sums] + [v[1:2] for v in sums]
        + [sums1[2:3], sums3[2:3], sums4[2:3], two0, two1],
        axis=0,
    )
    apart = jnp.concatenate(
        [in0, in1, in2, one0.reshape(-1, width), one1.reshape(-1, width)], axis=0
    )
    shared = shared + swap(shared)
    summed = total_small(jnp.concatenate([shared, apart], axis=0))
    return (
        memory[: sources // 2][:, None],
        decoded[:, None],
        source_grad[:, None],
        target_grad[:, None],
        summed[0:5],
        summed[5:10],
        stacks[2],
        summed[15:18].reshape(3, 2, local),
        stacks[3],
        summed[10:13],
        stacks[0],
        summed[18:22].reshape(2, hidden_width),
        stacks[1],
        summed[13:15],
    )


def solution(mesh):
    tokens = P("tensor", "dp", None)
    return jax.shard_map(
        on_device,
        mesh=mesh,
        in_specs=(
            tokens, tokens, P("dp", None), P("dp", None), P("dp"), P("dp", "tensor"),
            tokens, tokens, P(), P(),
            P(None, None, None, "tensor"), P(None, None, "tensor"), P(None, "tensor", None), P(),
            P(None, None, "tensor"), P(None, "tensor"), P(None, "tensor", None), P(),
        ),
        out_specs=(
            tokens, tokens, tokens, tokens, P(), P(),
            P(None, None, None, "tensor"), P(None, None, "tensor"), P(None, "tensor", None), P(),
            P(None, None, "tensor"), P(None, "tensor"), P(None, "tensor", None), P(),
        ),
        check_vma=False,
    )
```

```python
import functools

import jax
import jax.numpy as jnp
from jax import lax
from jax.experimental import pallas as pl
from jax.experimental.pallas import tpu as pltpu
from jax.sharding import PartitionSpec as P

HEAD = 64
PAIR = 2 * HEAD
EPSILON = 1e-05
MASKED_SCORE = -1000000000.0
FAR = 1e9
ROOT = 0.7978845608028654
CUBIC = 0.044715
BF16 = jnp.bfloat16
F32 = jnp.float32
VMEM_LIMIT = 18 * 1024 * 1024
BYTES = 3690000
NN = ((1,), (0,))
NT = ((1,), (1,))
TN = ((0,), (0,))
LARGE = 1 << 20
NAMES = ("ffn_in", "ffn_out", "attn_in", "attn_out")
TOKEN = jax.ShapeDtypeStruct((8, 128), F32)


def dot(left, right, contract):
    return lax.dot_general(left, right, (contract, ((), ())), preferred_element_type=F32)


def shape(rows, columns, dtype):
    return jax.ShapeDtypeStruct((rows, columns), dtype)


NEAR = pl.BlockSpec(memory_space=pltpu.VMEM)
AWAY = pl.BlockSpec(memory_space=pl.ANY)
NUMBER = pl.BlockSpec(memory_space=pltpu.SMEM)


class Weight:
    def __init__(self, stack, layer):
        self.stack = stack
        self.layer = layer


class Place:
    def __init__(self, array):
        self.array = array


class Params:
    def __init__(self, *arrays):
        self.arrays = arrays


class Fetch:
    def __init__(self, source, buffer, semaphore):
        self.copy = pltpu.make_async_copy(source, buffer, semaphore)
        self.copy.start()
        self.buffer = buffer
        self.arrived = False

    def here(self):
        if not self.arrived:
            self.copy.wait()
            self.arrived = True
        return self.buffer


class Order:
    def __init__(self):
        self.token = None

    def call(
        self, body, outs, ins, microseconds=1, scratch=(), leave=(), away=(), aliases={},
        limit=VMEM_LIMIT,
    ):
        tokens = [] if self.token is None else [self.token]
        specs, args, weights, groups = [], [], [], []
        for value in ins:
            if isinstance(value, Params):
                groups.append(len(args))
                for array in value.arrays:
                    specs.append(NEAR)
                    args.append(pltpu.with_memory_space_constraint(array, pltpu.VMEM))
            elif isinstance(value, Place):
                specs.append(AWAY)
                args.append(pltpu.with_memory_space_constraint(value.array, pltpu.HBM))
            elif isinstance(value, Weight):
                weights.append((len(args), value))
                specs.append(AWAY)
                args.append(pltpu.with_memory_space_constraint(value.stack, pltpu.HBM))
            elif value.dtype == jnp.int32 and value.shape == (1,):
                specs.append(NUMBER)
                args.append(value)
            else:
                specs.append(NEAR)
                args.append(pltpu.with_memory_space_constraint(value, pltpu.VMEM))

        def wrapped(*refs):
            in_refs = list(refs[: len(args)])
            refs = refs[len(args) + len(tokens) :]
            out_refs = refs[: len(outs)]
            refs = refs[len(outs) + 1 :]
            if weights:
                semaphores = refs[-1]
                for i, (at, weight) in enumerate(weights):
                    in_refs[at] = Fetch(in_refs[at].at[weight.layer], refs[i], semaphores.at[i])
            for at in reversed(groups):
                in_refs[at : at + 6] = [in_refs[at : at + 6]]
            body(*in_refs, *out_refs, *refs[len(weights) : len(weights) + len(scratch)])

        buffers = [pltpu.VMEM(w.stack.shape[1:], w.stack.dtype) for unused, w in weights]
        semaphores = [pltpu.SemaphoreType.DMA((len(weights),))] if weights else []
        results = pl.pallas_call(
            wrapped,
            out_shape=[
                *[
                    o if i in leave or i in away else pltpu.VMEM(o.shape, o.dtype)
                    for i, o in enumerate(outs)
                ],
                TOKEN,
            ],
            in_specs=specs + [AWAY] * len(tokens),
            out_specs=[AWAY if i in away else NEAR for i in range(len(outs))] + [AWAY],
            scratch_shapes=[*buffers, *scratch, *semaphores],
            input_output_aliases=aliases,
            compiler_params=pltpu.CompilerParams(vmem_limit_bytes=limit),
            cost_estimate=pl.CostEstimate(
                flops=0, transcendentals=0, bytes_accessed=int(microseconds * BYTES)
            ),
        )(*args, *tokens)
        self.token = results[-1]
        return results[:-1]


def norm_parts(inputs):
    centre = inputs - jnp.mean(inputs, axis=-1, keepdims=True)
    inverse = lax.rsqrt(jnp.mean(centre * centre, axis=-1, keepdims=True) + EPSILON)
    return centre * inverse, inverse


def norm_back(gradient, normed, inverse, gain):
    scaled = gradient * gain
    mean_plain = jnp.mean(scaled, axis=-1, keepdims=True)
    mean_normed = jnp.mean(scaled * normed, axis=-1, keepdims=True)
    return inverse * (scaled - mean_plain - normed * mean_normed)


def column_sum(values):
    return jnp.sum(values.astype(F32), axis=0, keepdims=True)


def halves(count):
    half = count // 2
    return ((0, half), (half, 0))


def lane_half(which, rows):
    lanes = lax.broadcasted_iota(jnp.int32, (rows, PAIR), 1)
    return (lanes >= HEAD) if which else (lanes < HEAD)


def only_head(which, values):
    return jnp.where(lane_half(which, values.shape[0]), values, jnp.zeros_like(values))


def key_scores(key_pair, query_pair, which, key_at, query_at):
    scores = dot(only_head(which, key_pair), query_pair, NT)
    return jnp.where(key_at <= query_at, scores, MASKED_SCORE)


def attend(q_ref, k_ref, v_ref, key_at, query_at_ref, turned_ref, o_ref, log_ref):
    queries, local = q_ref.shape
    block = min(queries, 256)
    for pair in range(local // PAIR):
        columns = pl.ds(pair * PAIR, PAIR)
        key_pair = k_ref[:, columns]
        value_turned = v_ref[:, columns].astype(F32).T.astype(BF16)
        for start in range(0, queries, block):
            rows = pl.ds(start, block)
            query_pair = q_ref[rows, columns]
            query_at = 0.0 if query_at_ref is None else query_at_ref[:, rows]
            for which in range(2):
                head = 2 * pair + which
                scores = key_scores(key_pair, query_pair, which, key_at, query_at)
                top = jnp.max(scores, axis=0, keepdims=True)
                exponent = jnp.exp(scores - top)
                total = jnp.sum(exponent, axis=0, keepdims=True)
                weights = (exponent * (1.0 / total)).astype(BF16)
                log_ref[pl.ds(head, 1), rows] = top + jnp.log(total)
                mixed = dot(value_turned[which * HEAD : (which + 1) * HEAD], weights, NN)
                turned_ref[pl.ds(head * HEAD, HEAD), rows] = mixed.astype(BF16)
    o_ref[...] = turned_ref[...].astype(F32).T.astype(BF16)


def in_bias_rows(params, layer):
    return params[4][layer, 0:1], params[4][layer, 1:2]


def row_of(ref, index):
    return ref[index : index + 1]


def normalised(value, params, norm):
    normed, unused = norm_parts(value)
    return (normed * row_of(params[0], norm) + row_of(params[1], norm)).astype(BF16)


def column(row):
    return jnp.broadcast_to(row, (8, row.shape[1])).T[:, 0:1]


def own_first(row, here):
    half = row.shape[1] // 2
    return jnp.where(here == 0, row, jnp.concatenate([row[:, half:], row[:, :half]], axis=1))


def scaled_queries(hidden, w_in, bias):
    return ((dot(hidden, w_in[0], NN) + bias).astype(BF16) * HEAD ** (-0.5)).astype(BF16)


def load_body(*refs):
    count = len(refs) // 2
    copies = [
        pltpu.make_async_copy(refs[i], refs[count + i], refs[-1].at[i]) for i in range(count)
    ]
    for copy in copies:
        copy.start()
    for copy in copies:
        copy.wait()


def first_attention(norm, layer, own_ref, other_ref, params, w_in, w_out, key_at, query_at_ref, *refs):
    h_ref, q_ref, k_ref, v_ref, turned_ref, log_ref, base_ref, send_ref, o_ref = refs
    half = own_ref.shape[0]
    query_bias, value_bias = in_bias_rows(params, layer)
    for part, source in enumerate((own_ref, other_ref)):
        rows = pl.ds(part * half, half)
        hidden = normalised(source[...].astype(F32), params, norm)
        h_ref[rows] = hidden
        w = w_in.here()
        q_ref[rows] = scaled_queries(hidden, w, query_bias)
        k_ref[rows] = dot(hidden, w[1], NN).astype(BF16)
        v_ref[rows] = (dot(hidden, w[2], NN) + value_bias).astype(BF16)
    attend(q_ref, k_ref, v_ref, key_at, query_at_ref, turned_ref, o_ref, log_ref)
    w = w_out.here()
    for part, source in enumerate((own_ref, other_ref)):
        rows = pl.ds(part * half, half)
        partial = dot(o_ref[rows], w[...], NN)
        send_ref[rows] = partial.astype(BF16)
        base_ref[rows] = source[...].astype(F32) + row_of(params[2], layer) + partial


def enc_first_body(norm, layer, own_ref, other_ref, params, w_in, w_out, mask_ref, here_ref, place_ref, *refs):
    outs, key_at_ref, o_ref = refs[:-2], refs[-2], refs[-1]
    row = own_first(jnp.where(mask_ref[...] == 1, 0.0, FAR), here_ref[0])
    key_at = column(row)
    key_at_ref[...] = key_at
    first_attention(norm, layer, own_ref, other_ref, params, w_in, w_out, key_at, None, *outs, o_ref)


def dec_first_body(
    norm, layer, own_ref, other_ref, params, w_in, w_out, mask_ref, here_ref,
    cot_ref, loss_ref, objective_ref, place_ref, *refs
):
    outs, (key_at_ref, query_at_ref, gradient_ref, gradient_send_ref, o_ref) = refs[:-5], refs[-5:]
    count = mask_ref.shape[1]
    position = own_first(
        lax.broadcasted_iota(jnp.int32, (1, count), 1).astype(F32), here_ref[0]
    )
    row = jnp.where(own_first(mask_ref[...].astype(F32), here_ref[0]) == 1.0, position, FAR)
    key_at = column(row)
    key_at_ref[...] = key_at
    query_at_ref[...] = position
    flag = objective_ref[0].astype(F32)
    weight = column(0.25 + 0.75 * loss_ref[...].astype(F32)) * (0.5 + 0.5 * flag)
    gradient = cot_ref[...].astype(F32) * weight
    gradient_ref[...] = gradient
    gradient_send_ref[...] = gradient.astype(BF16)
    first_attention(
        norm, layer, own_ref, other_ref, params, w_in, w_out, key_at, query_at_ref, *outs, o_ref
    )


def cross_attention_body(
    norm, layer, before_ref, recv_ref, params, w_in, w_out, k_ref, v_ref, key_at_ref,
    x_ref, h_ref, q_ref, turned_ref, log_ref, base_ref, send_ref, o_ref,
):
    count = x_ref.shape[0]
    half = count // 2
    query_bias, unused = in_bias_rows(params, layer)
    for mine, theirs in halves(count):
        rows = pl.ds(mine, half)
        value = before_ref[rows] + recv_ref[pl.ds(theirs, half)].astype(F32)
        x_ref[rows] = value
        hidden = normalised(value, params, norm)
        h_ref[rows] = hidden
        q_ref[rows] = scaled_queries(hidden, w_in.here(), query_bias)
    attend(q_ref, k_ref, v_ref, key_at_ref[...], None, turned_ref, o_ref, log_ref)
    partial = dot(o_ref[...], w_out.here()[...], NN)
    send_ref[...] = partial.astype(BF16)
    base_ref[...] = x_ref[...] + row_of(params[2], layer) + partial


def memory_body(layer, before_ref, recv_ref, params, w_in, mem_ref, k_ref, v_ref, out_ref):
    count = mem_ref.shape[0]
    half = count // 2
    unused, value_bias = in_bias_rows(params, layer)
    for mine, theirs in halves(count):
        rows = pl.ds(mine, half)
        memory = (before_ref[rows] + recv_ref[pl.ds(theirs, half)].astype(F32)).astype(BF16)
        mem_ref[rows] = memory
        if mine == 0:
            out_ref[...] = memory
        w = w_in.here()
        k_ref[rows] = dot(memory, w[1], NN).astype(BF16)
        v_ref[rows] = (dot(memory, w[2], NN) + value_bias).astype(BF16)


def feed_body(
    norm, layer, last, before_ref, recv_ref, params, w_one, w_two,
    x_ref, h_ref, f_ref, slope_ref, base_ref, send_ref,
):
    count = x_ref.shape[0]
    half = count // 2
    for mine, theirs in halves(count):
        rows = pl.ds(mine, half)
        value = before_ref[rows] + recv_ref[pl.ds(theirs, half)].astype(F32)
        x_ref[rows] = value
        hidden = normalised(value, params, norm)
        h_ref[rows] = hidden
        u = dot(hidden, w_one.here()[...], NN) + row_of(params[5], layer)
        square = u * u
        bent = jnp.tanh(u * (ROOT + (ROOT * CUBIC) * square))
        upper = 0.5 + 0.5 * bent
        active = (u * upper).astype(BF16)
        f_ref[rows] = active
        slope = upper + (0.5 * u) * (1.0 - bent * bent) * (ROOT + (3 * ROOT * CUBIC) * square)
        slope_ref[rows] = slope.astype(BF16)
        partial = dot(active, w_two.here()[...], NN)
        if not last:
            send_ref[rows] = partial.astype(BF16)
            base_ref[rows] = value + row_of(params[3], layer) + partial
        elif mine == 0:
            base_ref[...] = value + row_of(params[3], layer) + partial
        else:
            send_ref[...] = partial.astype(BF16)


def feed_back_rows(
    gradient, rows, w_one, w_two, slope_ref, g_ref, low_ref, du_ref, base_ref, send_ref
):
    g_ref[rows] = gradient
    low = gradient.astype(BF16)
    low_ref[rows] = low
    du = (dot(low, w_two.here()[...], NT) * slope_ref[rows].astype(F32)).astype(BF16)
    du_ref[rows] = du
    partial = dot(du, w_one.here()[...], NT)
    send_ref[rows] = partial.astype(BF16)
    base_ref[rows] = partial


def dec_feed_back_body(own_ref, other_ref, w_one, w_two, slope_ref, *outs):
    half = own_ref.shape[0]
    for part, source in enumerate((own_ref, other_ref)):
        feed_back_rows(
            source[...].astype(F32), pl.ds(part * half, half), w_one, w_two, slope_ref, *outs
        )


def source_seed(cot_ref, objective_ref):
    return cot_ref[...].astype(F32) * (1.0 - 0.5 * objective_ref[0].astype(F32))


def enc_feed_back_body(seed_ref, objective_ref, mem_base_ref, recv_ref, w_one, w_two, slope_ref, *outs):
    half = seed_ref.shape[0]
    own, other = pl.ds(0, half), pl.ds(half, half)
    for rows, theirs in ((own, other), (other, own)):
        gradient = mem_base_ref[rows] + recv_ref[theirs].astype(F32)
        if rows is own:
            gradient = gradient + source_seed(seed_ref, objective_ref)
        feed_back_rows(gradient, rows, w_one, w_two, slope_ref, *outs)


def attention_back_body(norm, cross, causal, *refs):
    (g_in_ref, dh_ref, dh_recv_ref, x_ref, params, w_in, w_out, q_ref, k_ref, v_ref, log_ref,
     key_at_ref), refs = refs[:12], refs[12:]
    query_at_ref = seed_ref = mem_base_ref = mem_send_ref = None
    if causal:
        query_at_ref, refs = refs[0], refs[1:]
    if cross:
        (seed_ref, objective_ref), refs = refs[:2], refs[2:]
    (g_ref, low_ref, dq_ref, dk_ref, dv_ref, base_ref, send_ref), refs = refs[:7], refs[7:]
    if cross:
        (mem_base_ref, mem_send_ref), refs = refs[:2], refs[2:]
    sums_ref, do_ref, turned_ref = refs
    gain = row_of(params[0], norm)
    count, local = dq_ref.shape
    half = count // 2
    for part, (mine, theirs) in enumerate(halves(count)):
        rows = pl.ds(mine, half)
        normed, inverse = norm_parts(x_ref[rows])
        dh = dh_ref[rows] + dh_recv_ref[pl.ds(theirs, half)].astype(F32)
        gradient = g_in_ref[rows] + norm_back(dh, normed, inverse, gain)
        g_ref[rows] = gradient
        low = gradient.astype(BF16)
        low_ref[rows] = low
        if part == 0:
            sums_ref[0:1] = column_sum(dh * normed)
            sums_ref[1:2] = column_sum(dh)
            sums_ref[2:3] = column_sum(low)
        do_ref[rows] = dot(low, w_out.here()[...], NT).astype(BF16)
    key_at = key_at_ref[...]
    block = min(count, 256)
    keys = k_ref.shape[0]
    for pair in range(local // PAIR):
        columns = pl.ds(pair * PAIR, PAIR)
        key_pair = k_ref[:, columns]
        key_turned = key_pair.astype(F32).T.astype(BF16)
        value_pair = v_ref[:, columns]
        dk = [None, None]
        dv = [None, None]
        for start in range(0, count, block):
            rows = pl.ds(start, block)
            query_pair = q_ref[rows, columns]
            do_pair = do_ref[rows, columns]
            query_at = 0.0 if query_at_ref is None else query_at_ref[:, rows]
            for which in range(2):
                head = 2 * pair + which
                scores = key_scores(key_pair, query_pair, which, key_at, query_at)
                probs = jnp.exp(scores - log_ref[pl.ds(head, 1), rows])
                prob_grad = dot(only_head(which, value_pair), do_pair, NT)
                product = probs * prob_grad
                inner = jnp.sum(product, axis=0, keepdims=True)
                score_grad = (product - probs * inner).astype(BF16)
                dv_part = dot(probs.astype(BF16), do_pair, NN)
                dk_part = dot(score_grad, query_pair, NN)
                dq_part = dot(key_turned[which * HEAD : (which + 1) * HEAD], score_grad, NN)
                turned_ref[pl.ds(head * HEAD, HEAD), rows] = dq_part * HEAD ** (-0.5)
                dk[which] = dk_part if dk[which] is None else dk[which] + dk_part
                dv[which] = dv_part if dv[which] is None else dv[which] + dv_part
        first = lane_half(0, keys)
        dk_ref[:, columns] = jnp.where(first, dk[0], dk[1]).astype(BF16)
        dv_ref[:, columns] = jnp.where(first, dv[0], dv[1]).astype(BF16)
    dq_ref[...] = turned_ref[...].T.astype(BF16)
    w = w_in.here()
    if cross:
        partial = dot(dk_ref[...], w[1], NT) + dot(dv_ref[...], w[2], NT)
        mem_base_ref[...] = partial
        mem_half = keys // 2
        mem_send_ref[0:mem_half] = (
            partial[0:mem_half] + source_seed(seed_ref, objective_ref)
        ).astype(BF16)
        mem_send_ref[mem_half:] = partial[mem_half:].astype(BF16)
        partial = dot(dq_ref[...], w[0], NT)
        send_ref[...] = partial.astype(BF16)
        base_ref[...] = partial
    else:
        for part in (1, 0):
            rows = pl.ds(part * half, half)
            partial = (
                dot(dq_ref[rows], w[0], NT)
                + dot(dk_ref[rows], w[1], NT)
                + dot(dv_ref[rows], w[2], NT)
            )
            if part == 1:
                send_ref[...] = partial.astype(BF16)
            else:
                base_ref[...] = partial


def last_norm_body(norm, g_ref, dh_ref, recv_ref, x_ref, params, out_ref, sums_ref):
    normed, inverse = norm_parts(x_ref[...].astype(F32))
    dh = dh_ref[...] + recv_ref[...].astype(F32)
    sums_ref[0:1] = column_sum(dh * normed)
    sums_ref[1:2] = column_sum(dh)
    half = out_ref.shape[0]
    result = g_ref[0:half] + norm_back(dh, normed, inverse, row_of(params[0], norm))
    out_ref[...] = result.reshape(out_ref.shape)


def feed_weights_body(h_ref, du_ref, f_ref, low_ref, place_ref, send_ref, keep_ref, sums_ref, hidden_sums_ref):
    bit = bit_of(place_ref, 0)
    width = h_ref.shape[1]
    part = width // 2
    for which, out_ref in ((1 - bit, send_ref), (bit, keep_ref)):
        left = h_ref[:, pl.ds(pl.multiple_of(which * part, 128), part)]
        for side in range(2):
            out_ref[pl.ds(side * part, part)] = dot(
                left, du_ref[:, pl.ds(side * width, width)], TN
            ).astype(BF16)
        left = f_ref[:, pl.ds(pl.multiple_of(which * width, 128), width)]
        out_ref[pl.ds(width, width)] = dot(left, low_ref[...], TN).astype(BF16)
    half = low_ref.shape[0] // 2
    sums_ref[...] = column_sum(low_ref[0:half])
    hidden_sums_ref[...] = column_sum(du_ref[...])


def attention_weights_body(
    h_ref, mem_ref, dq_ref, dk_ref, dv_ref, turned_ref, low_ref, place_ref, send_ref, keep_ref, sums_ref
):
    bit = bit_of(place_ref, 0)
    width = h_ref.shape[1]
    part = width // 2
    quarter = width // 4
    left_side = pl.ds(0, part)
    right_side = pl.ds(part, part)
    for which, out_ref in ((1 - bit, send_ref), (bit, keep_ref)):
        columns = pl.ds(pl.multiple_of(which * part, 128), part)
        out_ref[pl.ds(0, part), left_side] = dot(h_ref[:, columns], dq_ref[...], TN).astype(BF16)
        memory = mem_ref[:, columns]
        out_ref[pl.ds(0, part), right_side] = dot(memory, dk_ref[...], TN).astype(BF16)
        values = dot(memory, dv_ref[...], TN).astype(BF16)
        out_ref[pl.ds(part, quarter), left_side] = values[:quarter]
        out_ref[pl.ds(part, quarter), right_side] = values[quarter:]
        rows = pl.ds(pl.multiple_of(which * quarter, 64), quarter)
        out_ref[pl.ds(part + quarter, quarter)] = dot(turned_ref[rows], low_ref[...], NN).astype(BF16)
    sums_ref[:, left_side] = column_sum(dq_ref[...])
    sums_ref[:, right_side] = column_sum(dv_ref[...])


def bit_of(place_ref, step):
    return (place_ref[0] >> step) & 1


def add_body(step, layout, place_ref, *refs):
    send_ref, next_ref = refs[-2:]
    bit = bit_of(place_ref, step)
    for out_ref, which in ((send_ref, 1 - bit), (next_ref, bit)):
        target = 0
        for i, (first, segments) in enumerate(layout):
            keep_ref, received_ref = refs[2 * i], refs[2 * i + 1]
            for rows in segments:
                half = rows // 2
                block = half
                while block % 32 == 0 and block > 128:
                    block //= 2
                for start in range(0, half, block):
                    part = pl.ds(pl.multiple_of(first + which * half + start, 8), block)
                    out_ref[pl.ds(target + start, block)] = (
                        keep_ref[part].astype(F32) + received_ref[part].astype(F32)
                    ).astype(BF16)
                first += rows
                target += half


def last_sums_body(*refs):
    out_ref = refs[-1]
    first = 0
    for keep_ref, received_ref in zip(refs[:-1:2], refs[1:-1:2]):
        rows = keep_ref.shape[0]
        total = keep_ref[...].astype(F32) + received_ref[...].astype(F32)
        out_ref[pl.ds(first, rows)] = total.astype(BF16)
        first += rows
    if first < out_ref.shape[0]:
        out_ref[first:] = jnp.zeros((out_ref.shape[0] - first, out_ref.shape[1]), BF16)


def place_body(groups, bits, in_ref, *refs):
    outs = dict(zip(NAMES, refs[1:5]))
    wide_ref, semaphores = refs[6:]
    device = pl.program_id(0)
    width = in_ref.shape[2]
    part, quarter = width // 2, width // 4
    slot = lax.rem(device, 2)
    upper = device & 1

    def copy(at, i, side, first, rows, target):
        source = wide_ref.at[at, pl.ds(first, rows), pl.ds(side * part, part)]
        return pltpu.make_async_copy(source, target, semaphores.at[at, 2 * i + side])

    def wait(at):
        first = 0
        for i, (kind, layer, rows) in enumerate(groups):
            for side in range(2):
                target = outs["ffn_out"].at[0, pl.ds(0, rows), pl.ds(0, part)]
                copy(at, i, side, first, rows, target).wait()
            first += rows

    @pl.when(device >= 2)
    def free():
        wait(slot)

    wide_ref[slot] = in_ref[0].astype(F32)
    at = 0
    for i, (kind, layer, rows) in enumerate(groups):
        inner = 0
        for bit in range(1, bits):
            inner = inner + ((device >> bit) & 1) * (rows << (bits - 1 - bit))

        def send(side, target):
            copy(slot, i, side, at, rows, target).start()

        if kind == "in":
            row = pl.multiple_of(upper * part + lax.rem(inner, part), 8)
            column = lax.div(inner, part) * width
            for side in range(2):
                columns = pl.ds(pl.multiple_of(column + side * part, 128), part)
                send(side, outs["ffn_in"].at[layer, pl.ds(row, rows), columns])
        elif kind == "out":
            row = pl.multiple_of(upper * width + inner, 8)
            for side in range(2):
                columns = pl.ds(side * part, part)
                send(side, outs["ffn_out"].at[layer, pl.ds(row, rows), columns])
        else:

            @pl.when(inner < part)
            def query_and_key():
                row = pl.multiple_of(upper * part + inner, 8)
                for side in range(2):
                    send(side, outs["attn_in"].at[layer, side, pl.ds(row, rows)])

            @pl.when((inner >= part) & (inner < part + quarter))
            def value():
                row = upper * part + inner - part
                for side in range(2):
                    target = pl.ds(pl.multiple_of(row + side * quarter, 8), rows)
                    send(side, outs["attn_in"].at[layer, 2, target])

            @pl.when(inner >= part + quarter)
            def output():
                row = pl.multiple_of(upper * quarter + inner - part - quarter, 8)
                for side in range(2):
                    columns = pl.ds(side * part, part)
                    send(side, outs["attn_out"].at[layer, pl.ds(row, rows), columns])

        at += rows

    @pl.when(device == pl.num_programs(0) - 1)
    def drain():
        wait(1 - slot)
        wait(slot)


def pack_body(*refs):
    norm_refs, out_refs, rows_refs, wide_refs = refs[:5], refs[5:7], refs[7:10], refs[10:12]
    shared_ref, apart_ref = refs[12:]
    shared_ref[...] = jnp.zeros_like(shared_ref)
    apart_ref[...] = jnp.zeros_like(apart_ref)
    for i, ref in enumerate(norm_refs):
        shared_ref[i : i + 1] = ref[0:1]
        shared_ref[5 + i : 6 + i] = ref[1:2]
    for i, source in enumerate((1, 3, 4)):
        shared_ref[10 + i : 11 + i] = norm_refs[source][2:3]
    for i, ref in enumerate(out_refs):
        shared_ref[13 + i : 14 + i] = ref[...]
    for i, ref in enumerate(rows_refs):
        apart_ref[i : i + 1] = ref[...]
    width = shared_ref.shape[1]
    for i, ref in enumerate(wide_refs):
        for side in range(2):
            apart_ref[3 + 2 * i + side : 4 + 2 * i + side] = ref[:, side * width : (side + 1) * width]


def pair_small_body(shared_ref, received_ref, apart_ref, out_ref):
    out_ref[0:16] = shared_ref[...] + received_ref[...]
    out_ref[16:24] = apart_ref[...]


def add_small_body(first_ref, second_ref, out_ref):
    out_ref[...] = first_ref[...] + second_ref[...]


def last_small_body(first_ref, second_ref, *outs):
    total = first_ref[...] + second_ref[...]
    gain_ref, offset_ref, out_bias_ref, two_ref, in_ref, one_ref = outs
    gain_ref[...] = total[0:5]
    offset_ref[...] = total[5:10]
    out_bias_ref[...] = total[10:13]
    two_ref[...] = total[13:15]
    width = total.shape[1]
    part = width // 2
    for i in range(3):
        for side in range(2):
            in_ref[i, side : side + 1] = total[16 + i : 17 + i, side * part : (side + 1) * part]
    for i in range(2):
        for side in range(2):
            row = 19 + 2 * i + side
            one_ref[i : i + 1, side * width : (side + 1) * width] = total[row : row + 1]


def decoded_body(base_ref, received_ref, out_ref):
    out_ref[...] = (base_ref[...] + received_ref[...].astype(F32)).astype(BF16)


def pass_body(value_ref, unused_ref, out_ref):
    out_ref[...] = value_ref[...]


def swap(values):
    return lax.ppermute(values, "tensor", [(0, 1), (1, 0)])


def across(values, stride):
    count = lax.axis_size("dp")
    return lax.ppermute(values, "dp", [(i, i ^ stride) for i in range(count)])


def dp_bits():
    return lax.axis_size("dp").bit_length() - 1


class Total:
    def __init__(self, order, place, parts, step=1):
        self.order = order
        self.place = place
        self.parts = parts
        self.step = step

    def merge(self, *others):
        assert all(self.step == other.step for other in others)
        return Total(
            self.order, self.place, self.parts + sum((other.parts for other in others), []), self.step
        )

    def next(self):
        if self.step == dp_bits():
            return
        width = self.parts[0][1].shape[1]
        layout = [
            (first, [rows for unused, unused, rows in groups])
            for groups, unused, unused, first in self.parts
        ]
        rows = sum(sum(segments) for unused, segments in layout) // 2
        send, keep = self.order.call(
            functools.partial(add_body, self.step, layout), [shape(rows, width, BF16)] * 2,
            [self.place, *[value for unused, *pair, unused in self.parts for value in pair]],
        )
        groups = [
            (kind, layer, rows // 2)
            for members, *unused in self.parts
            for kind, layer, rows in members
        ]
        self.parts = [(groups, keep, across(send, 1 << self.step), 0)]
        self.step += 1


def gather(order, totals):
    pairs = [(keep, received) for total in totals for unused, keep, received, unused in total.parts]
    groups = [group for total in totals for members, *unused in total.parts for group in members]
    rows = sum(keep.shape[0] for keep, unused in pairs)
    width = pairs[0][0].shape[1]
    enough = -(-LARGE // (2 * width * 16)) * 16
    if 0.9 * enough < rows < enough:
        rows = enough
    (shards,) = order.call(
        last_sums_body, [shape(rows, width, BF16)],
        [value for pair in pairs for value in pair], leave=[0],
    )
    return lax.all_gather(shards, "dp"), groups


def place(order, gathered, groups, shapes):
    count, rows, width = gathered.shape
    return pl.pallas_call(
        functools.partial(place_body, groups, dp_bits()),
        grid=(count,),
        out_shape=[*[jax.ShapeDtypeStruct(shapes[name], F32) for name in NAMES], TOKEN],
        in_specs=[pl.BlockSpec((1, rows, width), lambda i: (i, 0, 0)), AWAY],
        out_specs=[AWAY] * 5,
        scratch_shapes=[
            pltpu.VMEM((2, rows, width), F32),
            pltpu.SemaphoreType.DMA((2, 2 * len(groups))),
        ],
        compiler_params=pltpu.CompilerParams(vmem_limit_bytes=VMEM_LIMIT),
        cost_estimate=pl.CostEstimate(flops=0, transcendentals=0, bytes_accessed=10 * BYTES),
    )(pltpu.with_memory_space_constraint(gathered, pltpu.HBM), order.token)[:4]


class SmallTotal:
    def __init__(self, order, place, shapes, ins):
        self.order = order
        self.place = place
        self.shapes = shapes
        self.results = None
        width = ins[0].shape[1]
        self.shared, self.apart = order.call(
            pack_body, [shape(16, width, F32), shape(8, width, F32)], ins
        )
        self.received = swap(self.shared)
        self.stages = self.run()

    def next(self):
        next(self.stages, None)

    def run(self):
        order, bits = self.order, dp_bits()
        whole = shape(24, self.shared.shape[1], F32)
        (value,) = order.call(pair_small_body, [whole], [self.shared, self.received, self.apart])
        for bit in range(bits):
            received = across(value, 1 << bit)
            yield
            if bit + 1 < bits:
                (value,) = order.call(add_small_body, [whole], [value, received])
        self.results = order.call(
            last_small_body, [jax.ShapeDtypeStruct(dims, F32) for dims in self.shapes],
            [value, received], leave=range(6),
        )
        yield


def on_device(
    src_embed, tgt_embed, src_mask, tgt_mask, objective, loss_mask, enc_cot, dec_cot,
    norm_gain, norm_bias, attn_in, attn_in_bias, attn_out, attn_out_bias,
    ffn_in, ffn_in_bias, ffn_out, ffn_out_bias,
):
    order = Order()
    here = lax.axis_index("tensor")
    width = src_embed.shape[2]
    local = attn_in.shape[3]
    hidden_width = ffn_in.shape[2]
    source_own = src_embed.reshape(-1, width)
    target_own = tgt_embed.reshape(-1, width)
    sources = 2 * source_own.shape[0]
    targets = 2 * target_own.shape[0]
    enc_own = enc_cot.reshape(-1, width)
    target_other = swap(target_own)
    source_other = swap(source_own)
    loaded = [
        source_own, target_own, dec_cot.reshape(-1, width), loss_mask, src_mask, tgt_mask, enc_own,
        norm_gain, norm_bias, attn_out_bias, ffn_out_bias, attn_in_bias, ffn_in_bias,
    ]
    source_near, target_near, dec_cot_near, loss_near, src_mask_near, tgt_mask_near, enc_own, *small_near = order.call(
        load_body, [jax.ShapeDtypeStruct(a.shape, a.dtype) for a in loaded],
        [Place(a) for a in loaded], scratch=[pltpu.SemaphoreType.DMA((len(loaded),))],
    )
    params = Params(*small_near)
    core = lax.axis_index("dp").astype(jnp.int32).reshape(1)
    here = here.astype(jnp.int32).reshape(1)

    def first(body, own, other, norm, layer, mask, more_ins, more_outs):
        count = 2 * own.shape[0]
        narrow = shape(count, local, BF16)
        return order.call(
            functools.partial(body, norm, layer),
            [
                shape(count, width, BF16), narrow, narrow, narrow,
                shape(local, count, BF16), shape(8, count, F32),
                shape(count, width, F32), shape(count, width, BF16), shape(count, 1, F32),
                *more_outs,
            ],
            [own, other, params, Weight(attn_in, layer), Weight(attn_out, layer), mask, here, *more_ins],
            microseconds=count / 50,
            scratch=[pltpu.VMEM((count, local), BF16)],
        )

    def feed(before, recv, norm, layer, last):
        count = before.shape[0]
        sent = count // 2 if last else count
        return order.call(
            functools.partial(feed_body, norm, layer, last),
            [
                shape(count, width, F32), shape(count, width, BF16),
                shape(count, hidden_width, BF16), shape(count, hidden_width, BF16),
                shape(sent, width, F32), shape(sent, width, BF16),
            ],
            [before, recv, params, Weight(ffn_in, layer), Weight(ffn_out, layer)],
            microseconds=count / 90,
        )

    h0, q0, k0, v0, turned0, log0, base0, send0, source_keys = first(
        enc_first_body, source_near, source_other, 0, 0, src_mask_near, [core], []
    )
    (
        h2, q1, k1, v1, turned1, log1, base1, send1, target_keys,
        target_queries, dec_own, dec_send,
    ) = first(
        dec_first_body, target_near, target_other, 2, 1, tgt_mask_near,
        [dec_cot_near, loss_near, objective, core],
        [shape(1, targets, F32), shape(targets // 2, width, F32), shape(targets // 2, width, BF16)],
    )
    recv1 = swap(send1)
    dec_other = swap(dec_send)
    recv0 = swap(send0)
    x1, h1, f0, slope0, base2, send2 = feed(base0, recv0, 1, 0, False)
    recv2 = swap(send2)
    narrow = shape(sources, local, BF16)
    memory, k2, v2, encoded = order.call(
        functools.partial(memory_body, 2),
        [shape(sources, width, BF16), narrow, narrow, shape(sources // 2, width, BF16)],
        [base2, recv2, params, Weight(attn_in, 2)], microseconds=3, leave=[3],
    )
    x3, h3, q2, turned2, log2, base3, send3 = order.call(
        functools.partial(cross_attention_body, 3, 2),
        [
            shape(targets, width, F32), shape(targets, width, BF16),
            shape(targets, local, BF16), shape(local, targets, BF16), shape(8, targets, F32),
            shape(targets, width, F32), shape(targets, width, BF16),
        ],
        [
            base1, recv1, params, Weight(attn_in, 2), Weight(attn_out, 2), k2, v2, source_keys,
        ],
        microseconds=5,
        scratch=[pltpu.VMEM((targets, local), BF16)],
    )
    recv3 = swap(send3)
    x4, h4, f1, slope1, base4, send4 = feed(base3, recv3, 4, 1, True)

    def feed_back(body, layer, *ins):
        count = ins[-1].shape[0]
        return order.call(
            body,
            [
                shape(count, width, F32), shape(count, width, BF16),
                shape(count, hidden_width, BF16),
                shape(count, width, F32), shape(count, width, BF16),
            ],
            [*ins[:-1], Weight(ffn_in, layer), Weight(ffn_out, layer), ins[-1]],
            microseconds=count / 90,
        )

    def attention_back(cross, causal, g, dh, recv, x, norm, layer, q, k, v, log, key_at, *more):
        count = q.shape[0]
        keys = k.shape[0]
        outs = [
            shape(count, width, F32), shape(count, width, BF16),
            shape(count, local, BF16), shape(keys, local, BF16), shape(keys, local, BF16),
        ]
        if cross:
            outs += [
                shape(count, width, F32), shape(count, width, BF16),
                shape(keys, width, F32), shape(keys, width, BF16),
            ]
        else:
            outs += [shape(count // 2, width, F32), shape(count // 2, width, BF16)]
        outs += [shape(3, width, F32)]
        return order.call(
            functools.partial(attention_back_body, norm, cross, causal), outs,
            [
                g, dh, recv, x, params, Weight(attn_in, layer), Weight(attn_out, layer),
                q, k, v, log, key_at, *more,
            ],
            microseconds=count * keys / 28000,
            scratch=[pltpu.VMEM((count, local), BF16), pltpu.VMEM((local, count), F32)],
        )

    def feed_weights(layer, h, du, f, low):
        out = shape(2 * width, width, BF16)
        send, keep, sums, hidden_sums = order.call(
            feed_weights_body, [out, out, shape(1, width, F32), shape(1, hidden_width, F32)],
            [h, du, f, low, core], microseconds=3,
        )
        received = across(send, 1)
        return (
            Total(order, core, [([("in", layer, width)], keep, received, 0)]),
            Total(order, core, [([("out", layer, width)], keep, received, width)]),
            sums, hidden_sums,
        )

    def attention_weights(layer, h, mem, dq, dk, dv, turned, low):
        out = shape(width, width, BF16)
        send, keep, sums = order.call(
            attention_weights_body, [out, out, shape(1, width, F32)],
            [h, mem, dq, dk, dv, turned, low, core], microseconds=2,
        )
        return Total(order, core, [([("attention", layer, width)], keep, across(send, 1), 0)]), sums

    def last_norm(g, dh, recv, own, norm):
        rows = own.shape[0]
        return order.call(
            functools.partial(last_norm_body, norm),
            [jax.ShapeDtypeStruct((rows, 1, width), F32), shape(2, width, F32)],
            [g, dh, recv, own, params], leave=[0],
        )

    g4, low4, du1, dh4, dh4_send = feed_back(
        dec_feed_back_body, 1, dec_own, dec_other, slope1
    )
    dh4_recv = swap(dh4_send)
    in1, out1, two1, one1 = feed_weights(1, h4, du1, f1, low4)
    in1.next()
    g3, low3, dq2, dk2, dv2, dh3, dh3_send, mem_grad, mem_send, sums4 = attention_back(
        True, False, g4, dh4, dh4_recv, x4, 4, 2, q2, k2, v2, log2, source_keys, enc_own, objective
    )
    mem_recv = swap(mem_send)
    cross, bias2 = attention_weights(2, h3, memory, dq2, dk2, dv2, turned2, low3)
    in1.next()
    g1, low1, du0, dh1, dh1_send = feed_back(
        enc_feed_back_body, 0, enc_own, objective, mem_grad, mem_recv, slope0
    )
    dh1_recv = swap(dh1_send)
    in0, out0, two0, one0 = feed_weights(0, h1, du0, f0, low1)
    out1.next()
    out1.next()
    cross.next()
    feed0 = in0.merge(out0)
    feed0.next()
    (dh3_late,) = order.call(
        pass_body, [shape(targets, width, BF16)], [dh3_send, dh1_recv], microseconds=0.5
    )
    dh3_recv = swap(dh3_late)
    g0, low0, dq0, dk0, dv0, dh0, dh0_send, sums1 = attention_back(
        False, False, g1, dh1, dh1_recv, x1, 1, 0, q0, k0, v0, log0, source_keys
    )
    dh0_recv = swap(dh0_send)
    first0, bias0 = attention_weights(0, h0, h0, dq0, dk0, dv0, turned0, low0)
    cross.next()
    g2, low2, dq1, dk1, dv1, dh2, dh2_send, sums3 = attention_back(
        False, True, g3, dh3, dh3_recv, x3, 3, 1, q1, k1, v1, log1, target_keys, target_queries
    )
    dh2_recv = swap(dh2_send)
    first1, bias1 = attention_weights(1, h2, h2, dq1, dk1, dv1, turned1, low2)
    source_grad, sums0 = last_norm(g0, dh0, dh0_recv, source_near, 0)
    target_grad, sums2 = last_norm(g2, dh2, dh2_recv, target_near, 2)
    small = SmallTotal(
        order, core,
        [
            norm_gain.shape, norm_bias.shape, attn_out_bias.shape, ffn_out_bias.shape,
            attn_in_bias.shape, ffn_in_bias.shape,
        ],
        [sums0, sums1, sums2, sums3, sums4, two0, two1, bias0, bias1, bias2, one0, one1],
    )
    feed0.next()
    early = in1.merge(out1, cross)
    early.next()
    late = first0.merge(first1)
    late.next()
    small.next()
    feed0.next()
    late.next()
    small.next()
    late.next()
    for unused in range(dp_bits()):
        early.next()
        feed0.next()
        late.next()
    gathered, groups = gather(order, [early, feed0, late])
    for unused in range(dp_bits()):
        small.next()
    decoded_other = swap(send4)
    (decoded,) = order.call(
        decoded_body, [shape(targets // 2, width, BF16)], [base4, decoded_other], leave=[0]
    )
    stacks = dict(zip(NAMES, place(
        order, gathered, groups,
        dict(zip(NAMES, (ffn_in.shape, ffn_out.shape, attn_in.shape, attn_out.shape))),
    )))
    gains, offsets, out_biases, two_biases, in_biases, one_biases = small.results
    return (
        encoded[:, None],
        decoded[:, None],
        source_grad,
        target_grad,
        gains,
        offsets,
        stacks["attn_in"],
        in_biases,
        stacks["attn_out"],
        out_biases,
        stacks["ffn_in"],
        one_biases,
        stacks["ffn_out"],
        two_biases,
    )


def solution(mesh):
    tokens = P("tensor", "dp", None)
    return jax.shard_map(
        on_device,
        mesh=mesh,
        in_specs=(
            tokens, tokens, P("dp", None), P("dp", None), P("dp"), P("dp", "tensor"),
            tokens, tokens, P(), P(),
            P(None, None, None, "tensor"), P(None, None, "tensor"), P(None, "tensor", None), P(),
            P(None, None, "tensor"), P(None, "tensor"), P(None, "tensor", None), P(),
        ),
        out_specs=(
            tokens, tokens, tokens, tokens, P(), P(),
            P(None, None, None, "tensor"), P(None, None, "tensor"), P(None, "tensor", None), P(),
            P(None, None, "tensor"), P(None, "tensor"), P(None, "tensor", None), P(),
        ),
        check_vma=False,
    )
```

```python
import functools

import jax
import jax.numpy as jnp
from jax import lax
from jax.experimental import pallas as pl
from jax.experimental.pallas import tpu as pltpu
from jax.sharding import PartitionSpec as P

HEAD = 64
PAIR = 2 * HEAD
EPSILON = 1e-05
MASKED_SCORE = -1000000000.0
FAR = 1e9
ROOT = 0.7978845608028654
CUBIC = 0.044715
BF16 = jnp.bfloat16
F32 = jnp.float32
VMEM_LIMIT = 18 * 1024 * 1024
BYTES = 3690000
NN = ((1,), (0,))
NT = ((1,), (1,))
TN = ((0,), (0,))
LARGE = 1 << 20
LONG = 40
NAMES = ("ffn_in", "ffn_out", "attn_in", "attn_out")
TOKEN = jax.ShapeDtypeStruct((8, 128), F32)


def dot(left, right, contract):
    return lax.dot_general(left, right, (contract, ((), ())), preferred_element_type=F32)


def shape(rows, columns, dtype):
    return jax.ShapeDtypeStruct((rows, columns), dtype)


NEAR = pl.BlockSpec(memory_space=pltpu.VMEM)
AWAY = pl.BlockSpec(memory_space=pl.ANY)
NUMBER = pl.BlockSpec(memory_space=pltpu.SMEM)


class Weight:
    def __init__(self, stack, layer):
        self.stack = stack
        self.layer = layer


class Place:
    def __init__(self, array):
        self.array = array


class Params:
    def __init__(self, *arrays):
        self.arrays = arrays


class Fetch:
    def __init__(self, source, buffer, semaphore):
        self.copy = pltpu.make_async_copy(source, buffer, semaphore)
        self.copy.start()
        self.buffer = buffer
        self.arrived = False

    def here(self):
        if not self.arrived:
            self.copy.wait()
            self.arrived = True
        return self.buffer


class Order:
    def __init__(self):
        self.token = None

    def call(
        self, body, outs, ins, microseconds=0.2, scratch=(), leave=(), away=(), aliases={},
        limit=VMEM_LIMIT,
    ):
        tokens = [] if self.token is None else [self.token]
        specs, args, weights, groups = [], [], [], []
        for value in ins:
            if isinstance(value, Params):
                groups.append(len(args))
                for array in value.arrays:
                    specs.append(NEAR)
                    args.append(pltpu.with_memory_space_constraint(array, pltpu.VMEM))
            elif isinstance(value, Place):
                specs.append(AWAY)
                args.append(pltpu.with_memory_space_constraint(value.array, pltpu.HBM))
            elif isinstance(value, Weight):
                weights.append((len(args), value))
                specs.append(AWAY)
                args.append(pltpu.with_memory_space_constraint(value.stack, pltpu.HBM))
            elif value.dtype == jnp.int32 and value.shape == (1,):
                specs.append(NUMBER)
                args.append(value)
            else:
                specs.append(NEAR)
                args.append(pltpu.with_memory_space_constraint(value, pltpu.VMEM))

        def wrapped(*refs):
            in_refs = list(refs[: len(args)])
            refs = refs[len(args) + len(tokens) :]
            out_refs = refs[: len(outs)]
            refs = refs[len(outs) + 1 :]
            if weights:
                semaphores = refs[-1]
                for i, (at, weight) in enumerate(weights):
                    in_refs[at] = Fetch(in_refs[at].at[weight.layer], refs[i], semaphores.at[i])
            for at in reversed(groups):
                in_refs[at : at + 6] = [in_refs[at : at + 6]]
            body(*in_refs, *out_refs, *refs[len(weights) : len(weights) + len(scratch)])

        buffers = [pltpu.VMEM(w.stack.shape[1:], w.stack.dtype) for unused, w in weights]
        semaphores = [pltpu.SemaphoreType.DMA((len(weights),))] if weights else []
        results = pl.pallas_call(
            wrapped,
            out_shape=[
                *[
                    o if i in leave or i in away else pltpu.VMEM(o.shape, o.dtype)
                    for i, o in enumerate(outs)
                ],
                TOKEN,
            ],
            in_specs=specs + [AWAY] * len(tokens),
            out_specs=[AWAY if i in away else NEAR for i in range(len(outs))] + [AWAY],
            scratch_shapes=[*buffers, *scratch, *semaphores],
            input_output_aliases=aliases,
            compiler_params=pltpu.CompilerParams(vmem_limit_bytes=limit),
            cost_estimate=pl.CostEstimate(
                flops=int(microseconds * 1.15e9), transcendentals=0, bytes_accessed=int(microseconds * BYTES)
            ),
        )(*args, *tokens)
        self.token = results[-1]
        return results[:-1]


def norm_parts(inputs):
    centre = inputs - jnp.mean(inputs, axis=-1, keepdims=True)
    inverse = lax.rsqrt(jnp.mean(centre * centre, axis=-1, keepdims=True) + EPSILON)
    return centre * inverse, inverse


def norm_back(gradient, normed, inverse, gain):
    scaled = gradient * gain
    mean_plain = jnp.mean(scaled, axis=-1, keepdims=True)
    mean_normed = jnp.mean(scaled * normed, axis=-1, keepdims=True)
    return inverse * (scaled - mean_plain - normed * mean_normed)


def column_sum(values):
    return jnp.sum(values.astype(F32), axis=0, keepdims=True)


def halves(count):
    half = count // 2
    return ((0, half), (half, 0))


def lane_half(which, rows):
    lanes = lax.broadcasted_iota(jnp.int32, (rows, PAIR), 1)
    return (lanes >= HEAD) if which else (lanes < HEAD)


def only_head(which, values):
    return jnp.where(lane_half(which, values.shape[0]), values, jnp.zeros_like(values))


def key_scores(key_pair, query_pair, which, key_at, query_at):
    scores = dot(only_head(which, key_pair), query_pair, NT)
    return jnp.where(key_at <= query_at, scores, MASKED_SCORE)


def attend(q_ref, k_ref, v_ref, key_at, query_at_ref, turned_ref, o_ref, log_ref):
    queries, local = q_ref.shape
    block = min(queries, 256)
    for pair in range(local // PAIR):
        columns = pl.ds(pair * PAIR, PAIR)
        key_pair = k_ref[:, columns]
        value_turned = v_ref[:, columns].astype(F32).T.astype(BF16)
        for start in range(0, queries, block):
            rows = pl.ds(start, block)
            query_pair = q_ref[rows, columns]
            query_at = 0.0 if query_at_ref is None else query_at_ref[:, rows]
            for which in range(2):
                head = 2 * pair + which
                scores = key_scores(key_pair, query_pair, which, key_at, query_at)
                top = jnp.max(scores, axis=0, keepdims=True)
                exponent = jnp.exp(scores - top)
                total = jnp.sum(exponent, axis=0, keepdims=True)
                weights = (exponent * (1.0 / total)).astype(BF16)
                log_ref[pl.ds(head, 1), rows] = top + jnp.log(total)
                mixed = dot(value_turned[which * HEAD : (which + 1) * HEAD], weights, NN)
                turned_ref[pl.ds(head * HEAD, HEAD), rows] = mixed.astype(BF16)
    o_ref[...] = turned_ref[...].astype(F32).T.astype(BF16)


def in_bias_rows(params, layer):
    return params[4][layer, 0:1], params[4][layer, 1:2]


def row_of(ref, index):
    return ref[index : index + 1]


def normalised(value, params, norm):
    normed, unused = norm_parts(value)
    return (normed * row_of(params[0], norm) + row_of(params[1], norm)).astype(BF16)


def column(row):
    return jnp.broadcast_to(row, (8, row.shape[1])).T[:, 0:1]


def own_first(row, here):
    half = row.shape[1] // 2
    return jnp.where(here == 0, row, jnp.concatenate([row[:, half:], row[:, :half]], axis=1))


def scaled_queries(hidden, w_in, bias):
    return ((dot(hidden, w_in[0], NN) + bias).astype(BF16) * HEAD ** (-0.5)).astype(BF16)


def load_body(*refs):
    count = len(refs) // 2
    copies = [
        pltpu.make_async_copy(refs[i], refs[count + i], refs[-1].at[i]) for i in range(count)
    ]
    for copy in copies:
        copy.start()
    for copy in copies:
        copy.wait()


def first_attention(norm, layer, own_ref, other_ref, params, w_in, w_out, key_at, query_at_ref, *refs):
    h_ref, q_ref, k_ref, v_ref, turned_ref, log_ref, base_ref, send_ref, o_ref = refs
    half = own_ref.shape[0]
    query_bias, value_bias = in_bias_rows(params, layer)
    for part, source in enumerate((own_ref, other_ref)):
        rows = pl.ds(part * half, half)
        hidden = normalised(source[...].astype(F32), params, norm)
        h_ref[rows] = hidden
        w = w_in.here()
        q_ref[rows] = scaled_queries(hidden, w, query_bias)
        k_ref[rows] = dot(hidden, w[1], NN).astype(BF16)
        v_ref[rows] = (dot(hidden, w[2], NN) + value_bias).astype(BF16)
    attend(q_ref, k_ref, v_ref, key_at, query_at_ref, turned_ref, o_ref, log_ref)
    w = w_out.here()
    for part, source in enumerate((own_ref, other_ref)):
        rows = pl.ds(part * half, half)
        partial = dot(o_ref[rows], w[...], NN)
        send_ref[rows] = partial.astype(BF16)
        base_ref[rows] = source[...].astype(F32) + row_of(params[2], layer) + partial


def enc_first_body(norm, layer, own_ref, other_ref, params, w_in, w_out, mask_ref, here_ref, place_ref, *refs):
    outs, key_at_ref, o_ref = refs[:-2], refs[-2], refs[-1]
    row = own_first(jnp.where(mask_ref[...] == 1, 0.0, FAR), here_ref[0])
    key_at = column(row)
    key_at_ref[...] = key_at
    first_attention(norm, layer, own_ref, other_ref, params, w_in, w_out, key_at, None, *outs, o_ref)


def dec_first_body(
    norm, layer, own_ref, other_ref, params, w_in, w_out, mask_ref, here_ref,
    cot_ref, loss_ref, objective_ref, place_ref, *refs
):
    outs, (key_at_ref, query_at_ref, gradient_ref, gradient_send_ref, o_ref) = refs[:-5], refs[-5:]
    count = mask_ref.shape[1]
    position = own_first(
        lax.broadcasted_iota(jnp.int32, (1, count), 1).astype(F32), here_ref[0]
    )
    row = jnp.where(own_first(mask_ref[...].astype(F32), here_ref[0]) == 1.0, position, FAR)
    key_at = column(row)
    key_at_ref[...] = key_at
    query_at_ref[...] = position
    flag = objective_ref[0].astype(F32)
    weight = column(0.25 + 0.75 * loss_ref[...].astype(F32)) * (0.5 + 0.5 * flag)
    gradient = cot_ref[...].astype(F32) * weight
    gradient_ref[...] = gradient
    gradient_send_ref[...] = gradient.astype(BF16)
    first_attention(
        norm, layer, own_ref, other_ref, params, w_in, w_out, key_at, query_at_ref, *outs, o_ref
    )


def cross_attention_body(
    norm, layer, before_ref, recv_ref, params, w_in, w_out, k_ref, v_ref, key_at_ref,
    x_ref, h_ref, q_ref, turned_ref, log_ref, base_ref, send_ref, o_ref,
):
    count = x_ref.shape[0]
    half = count // 2
    query_bias, unused = in_bias_rows(params, layer)
    for mine, theirs in halves(count):
        rows = pl.ds(mine, half)
        value = before_ref[rows] + recv_ref[pl.ds(theirs, half)].astype(F32)
        x_ref[rows] = value
        hidden = normalised(value, params, norm)
        h_ref[rows] = hidden
        q_ref[rows] = scaled_queries(hidden, w_in.here(), query_bias)
    attend(q_ref, k_ref, v_ref, key_at_ref[...], None, turned_ref, o_ref, log_ref)
    partial = dot(o_ref[...], w_out.here()[...], NN)
    send_ref[...] = partial.astype(BF16)
    base_ref[...] = x_ref[...] + row_of(params[2], layer) + partial


def memory_body(layer, before_ref, recv_ref, params, w_in, mem_ref, k_ref, v_ref, out_ref):
    count = mem_ref.shape[0]
    half = count // 2
    unused, value_bias = in_bias_rows(params, layer)
    for mine, theirs in halves(count):
        rows = pl.ds(mine, half)
        memory = (before_ref[rows] + recv_ref[pl.ds(theirs, half)].astype(F32)).astype(BF16)
        mem_ref[rows] = memory
        if mine == 0:
            out_ref[...] = memory
        w = w_in.here()
        k_ref[rows] = dot(memory, w[1], NN).astype(BF16)
        v_ref[rows] = (dot(memory, w[2], NN) + value_bias).astype(BF16)


def feed_body(
    norm, layer, last, before_ref, recv_ref, params, w_one, w_two,
    x_ref, h_ref, f_ref, slope_ref, base_ref, send_ref,
):
    count = x_ref.shape[0]
    half = count // 2
    for mine, theirs in halves(count):
        rows = pl.ds(mine, half)
        value = before_ref[rows] + recv_ref[pl.ds(theirs, half)].astype(F32)
        x_ref[rows] = value
        hidden = normalised(value, params, norm)
        h_ref[rows] = hidden
        u = dot(hidden, w_one.here()[...], NN) + row_of(params[5], layer)
        square = u * u
        bent = jnp.tanh(u * (ROOT + (ROOT * CUBIC) * square))
        upper = 0.5 + 0.5 * bent
        active = (u * upper).astype(BF16)
        f_ref[rows] = active
        slope = upper + (0.5 * u) * (1.0 - bent * bent) * (ROOT + (3 * ROOT * CUBIC) * square)
        slope_ref[rows] = slope.astype(BF16)
        partial = dot(active, w_two.here()[...], NN)
        if not last:
            send_ref[rows] = partial.astype(BF16)
            base_ref[rows] = value + row_of(params[3], layer) + partial
        elif mine == 0:
            base_ref[...] = value + row_of(params[3], layer) + partial
        else:
            send_ref[...] = partial.astype(BF16)


def feed_back_rows(
    gradient, rows, w_one, w_two, slope_ref, g_ref, low_ref, du_ref, base_ref, send_ref
):
    g_ref[rows] = gradient
    low = gradient.astype(BF16)
    low_ref[rows] = low
    du = (dot(low, w_two.here()[...], NT) * slope_ref[rows].astype(F32)).astype(BF16)
    du_ref[rows] = du
    partial = dot(du, w_one.here()[...], NT)
    send_ref[rows] = partial.astype(BF16)
    base_ref[rows] = partial


def dec_feed_back_body(own_ref, other_ref, w_one, w_two, slope_ref, *outs):
    half = own_ref.shape[0]
    for part, source in enumerate((own_ref, other_ref)):
        feed_back_rows(
            source[...].astype(F32), pl.ds(part * half, half), w_one, w_two, slope_ref, *outs
        )


def source_seed(cot_ref, objective_ref):
    return cot_ref[...].astype(F32) * (1.0 - 0.5 * objective_ref[0].astype(F32))


def enc_feed_back_body(seed_ref, objective_ref, mem_base_ref, recv_ref, w_one, w_two, slope_ref, *outs):
    half = seed_ref.shape[0]
    own, other = pl.ds(0, half), pl.ds(half, half)
    for rows, theirs in ((own, other), (other, own)):
        gradient = mem_base_ref[rows] + recv_ref[theirs].astype(F32)
        if rows is own:
            gradient = gradient + source_seed(seed_ref, objective_ref)
        feed_back_rows(gradient, rows, w_one, w_two, slope_ref, *outs)


def attention_back_body(norm, cross, causal, *refs):
    (g_in_ref, dh_ref, dh_recv_ref, x_ref, params, w_in, w_out, q_ref, k_ref, v_ref, log_ref,
     key_at_ref), refs = refs[:12], refs[12:]
    query_at_ref = seed_ref = mem_base_ref = mem_send_ref = None
    if causal:
        query_at_ref, refs = refs[0], refs[1:]
    if cross:
        (seed_ref, objective_ref), refs = refs[:2], refs[2:]
    (g_ref, low_ref, dq_ref, dk_ref, dv_ref, base_ref, send_ref), refs = refs[:7], refs[7:]
    if cross:
        (mem_base_ref, mem_send_ref), refs = refs[:2], refs[2:]
    sums_ref, do_ref, turned_ref = refs
    gain = row_of(params[0], norm)
    count, local = dq_ref.shape
    half = count // 2
    for part, (mine, theirs) in enumerate(halves(count)):
        rows = pl.ds(mine, half)
        normed, inverse = norm_parts(x_ref[rows])
        dh = dh_ref[rows] + dh_recv_ref[pl.ds(theirs, half)].astype(F32)
        gradient = g_in_ref[rows] + norm_back(dh, normed, inverse, gain)
        g_ref[rows] = gradient
        low = gradient.astype(BF16)
        low_ref[rows] = low
        if part == 0:
            sums_ref[0:1] = column_sum(dh * normed)
            sums_ref[1:2] = column_sum(dh)
            sums_ref[2:3] = column_sum(low)
        do_ref[rows] = dot(low, w_out.here()[...], NT).astype(BF16)
    key_at = key_at_ref[...]
    block = min(count, 256)
    keys = k_ref.shape[0]
    for pair in range(local // PAIR):
        columns = pl.ds(pair * PAIR, PAIR)
        key_pair = k_ref[:, columns]
        key_turned = key_pair.astype(F32).T.astype(BF16)
        value_pair = v_ref[:, columns]
        dk = [None, None]
        dv = [None, None]
        for start in range(0, count, block):
            rows = pl.ds(start, block)
            query_pair = q_ref[rows, columns]
            do_pair = do_ref[rows, columns]
            query_at = 0.0 if query_at_ref is None else query_at_ref[:, rows]
            for which in range(2):
                head = 2 * pair + which
                scores = key_scores(key_pair, query_pair, which, key_at, query_at)
                probs = jnp.exp(scores - log_ref[pl.ds(head, 1), rows])
                prob_grad = dot(only_head(which, value_pair), do_pair, NT)
                product = probs * prob_grad
                inner = jnp.sum(product, axis=0, keepdims=True)
                score_grad = (product - probs * inner).astype(BF16)
                dv_part = dot(probs.astype(BF16), do_pair, NN)
                dk_part = dot(score_grad, query_pair, NN)
                dq_part = dot(key_turned[which * HEAD : (which + 1) * HEAD], score_grad, NN)
                turned_ref[pl.ds(head * HEAD, HEAD), rows] = dq_part * HEAD ** (-0.5)
                dk[which] = dk_part if dk[which] is None else dk[which] + dk_part
                dv[which] = dv_part if dv[which] is None else dv[which] + dv_part
        first = lane_half(0, keys)
        dk_ref[:, columns] = jnp.where(first, dk[0], dk[1]).astype(BF16)
        dv_ref[:, columns] = jnp.where(first, dv[0], dv[1]).astype(BF16)
    dq_ref[...] = turned_ref[...].T.astype(BF16)
    w = w_in.here()
    if cross:
        partial = dot(dk_ref[...], w[1], NT) + dot(dv_ref[...], w[2], NT)
        mem_base_ref[...] = partial
        mem_half = keys // 2
        mem_send_ref[0:mem_half] = (
            partial[0:mem_half] + source_seed(seed_ref, objective_ref)
        ).astype(BF16)
        mem_send_ref[mem_half:] = partial[mem_half:].astype(BF16)
        partial = dot(dq_ref[...], w[0], NT)
        send_ref[...] = partial.astype(BF16)
        base_ref[...] = partial
    else:
        for part in (1, 0):
            rows = pl.ds(part * half, half)
            partial = (
                dot(dq_ref[rows], w[0], NT)
                + dot(dk_ref[rows], w[1], NT)
                + dot(dv_ref[rows], w[2], NT)
            )
            if part == 1:
                send_ref[...] = partial.astype(BF16)
            else:
                base_ref[...] = partial


def last_norm_body(norm, g_ref, dh_ref, recv_ref, x_ref, params, out_ref, sums_ref):
    normed, inverse = norm_parts(x_ref[...].astype(F32))
    dh = dh_ref[...] + recv_ref[...].astype(F32)
    sums_ref[0:1] = column_sum(dh * normed)
    sums_ref[1:2] = column_sum(dh)
    half = out_ref.shape[0]
    result = g_ref[0:half] + norm_back(dh, normed, inverse, row_of(params[0], norm))
    out_ref[...] = result.reshape(out_ref.shape)


def feed_weights_body(h_ref, du_ref, f_ref, low_ref, place_ref, send_ref, keep_ref, sums_ref, hidden_sums_ref):
    bit = bit_of(place_ref, 0)
    width = h_ref.shape[1]
    part = width // 2
    for which, out_ref in ((1 - bit, send_ref), (bit, keep_ref)):
        left = h_ref[:, pl.ds(pl.multiple_of(which * part, 128), part)]
        for side in range(2):
            out_ref[pl.ds(side * part, part)] = dot(
                left, du_ref[:, pl.ds(side * width, width)], TN
            ).astype(BF16)
        left = f_ref[:, pl.ds(pl.multiple_of(which * width, 128), width)]
        out_ref[pl.ds(width, width)] = dot(left, low_ref[...], TN).astype(BF16)
    half = low_ref.shape[0] // 2
    sums_ref[...] = column_sum(low_ref[0:half])
    hidden_sums_ref[...] = column_sum(du_ref[...])


def attention_weights_body(
    h_ref, mem_ref, dq_ref, dk_ref, dv_ref, turned_ref, low_ref, place_ref, send_ref, keep_ref, sums_ref
):
    bit = bit_of(place_ref, 0)
    width = h_ref.shape[1]
    part = width // 2
    quarter = width // 4
    left_side = pl.ds(0, part)
    right_side = pl.ds(part, part)
    for which, out_ref in ((1 - bit, send_ref), (bit, keep_ref)):
        columns = pl.ds(pl.multiple_of(which * part, 128), part)
        out_ref[pl.ds(0, part), left_side] = dot(h_ref[:, columns], dq_ref[...], TN).astype(BF16)
        memory = mem_ref[:, columns]
        out_ref[pl.ds(0, part), right_side] = dot(memory, dk_ref[...], TN).astype(BF16)
        values = dot(memory, dv_ref[...], TN).astype(BF16)
        out_ref[pl.ds(part, quarter), left_side] = values[:quarter]
        out_ref[pl.ds(part, quarter), right_side] = values[quarter:]
        rows = pl.ds(pl.multiple_of(which * quarter, 64), quarter)
        out_ref[pl.ds(part + quarter, quarter)] = dot(turned_ref[rows], low_ref[...], NN).astype(BF16)
    sums_ref[:, left_side] = column_sum(dq_ref[...])
    sums_ref[:, right_side] = column_sum(dv_ref[...])


def bit_of(place_ref, step):
    return (place_ref[0] >> step) & 1


def add_body(step, layout, place_ref, *refs):
    send_ref, next_ref = refs[-2:]
    bit = bit_of(place_ref, step)
    for out_ref, which in ((send_ref, 1 - bit), (next_ref, bit)):
        target = 0
        for i, (first, segments) in enumerate(layout):
            keep_ref, received_ref = refs[2 * i], refs[2 * i + 1]
            for rows in segments:
                half = rows // 2
                block = half
                while block % 32 == 0 and block > 128:
                    block //= 2
                for start in range(0, half, block):
                    part = pl.ds(pl.multiple_of(first + which * half + start, 8), block)
                    out_ref[pl.ds(target + start, block)] = (
                        keep_ref[part].astype(F32) + received_ref[part].astype(F32)
                    ).astype(BF16)
                first += rows
                target += half


def last_sum_body(keep_ref, received_ref, out_ref):
    out_ref[...] = (keep_ref[...].astype(F32) + received_ref[...].astype(F32)).astype(BF16)


def stack_body(*refs):
    out_ref = refs[-1]
    first = 0
    for ref in refs[:-1]:
        rows = ref.shape[0]
        out_ref[pl.ds(first, rows)] = ref[...]
        first += rows
    if first < out_ref.shape[0]:
        out_ref[first:] = jnp.zeros((out_ref.shape[0] - first, out_ref.shape[1]), BF16)


def place_body(groups, bits, in_ref, *refs):
    outs = dict(zip(NAMES, refs[1:5]))
    wide_ref, semaphores = refs[6:]
    device = pl.program_id(0)
    width = in_ref.shape[2]
    part, quarter = width // 2, width // 4
    slot = lax.rem(device, 2)
    upper = device & 1

    def copy(at, i, side, first, rows, target):
        source = wide_ref.at[at, pl.ds(first, rows), pl.ds(side * part, part)]
        return pltpu.make_async_copy(source, target, semaphores.at[at, 2 * i + side])

    def wait(at):
        first = 0
        for i, (kind, layer, rows) in enumerate(groups):
            for side in range(2):
                target = outs["ffn_out"].at[0, pl.ds(0, rows), pl.ds(0, part)]
                copy(at, i, side, first, rows, target).wait()
            first += rows

    @pl.when(device >= 2)
    def free():
        wait(slot)

    wide_ref[slot] = in_ref[0].astype(F32)
    at = 0
    for i, (kind, layer, rows) in enumerate(groups):
        inner = 0
        for bit in range(1, bits):
            inner = inner + ((device >> bit) & 1) * (rows << (bits - 1 - bit))

        def send(side, target):
            copy(slot, i, side, at, rows, target).start()

        if kind == "in":
            row = pl.multiple_of(upper * part + lax.rem(inner, part), 8)
            column = lax.div(inner, part) * width
            for side in range(2):
                columns = pl.ds(pl.multiple_of(column + side * part, 128), part)
                send(side, outs["ffn_in"].at[layer, pl.ds(row, rows), columns])
        elif kind == "out":
            row = pl.multiple_of(upper * width + inner, 8)
            for side in range(2):
                columns = pl.ds(side * part, part)
                send(side, outs["ffn_out"].at[layer, pl.ds(row, rows), columns])
        else:

            @pl.when(inner < part)
            def query_and_key():
                row = pl.multiple_of(upper * part + inner, 8)
                for side in range(2):
                    send(side, outs["attn_in"].at[layer, side, pl.ds(row, rows)])

            @pl.when((inner >= part) & (inner < part + quarter))
            def value():
                row = upper * part + inner - part
                for side in range(2):
                    target = pl.ds(pl.multiple_of(row + side * quarter, 8), rows)
                    send(side, outs["attn_in"].at[layer, 2, target])

            @pl.when(inner >= part + quarter)
            def output():
                row = pl.multiple_of(upper * quarter + inner - part - quarter, 8)
                for side in range(2):
                    columns = pl.ds(side * part, part)
                    send(side, outs["attn_out"].at[layer, pl.ds(row, rows), columns])

        at += rows

    @pl.when(device == pl.num_programs(0) - 1)
    def drain():
        wait(1 - slot)
        wait(slot)


def pack_body(*refs):
    norm_refs, out_refs, rows_refs, wide_refs = refs[:5], refs[5:7], refs[7:10], refs[10:12]
    shared_ref, apart_ref = refs[12:]
    shared_ref[...] = jnp.zeros_like(shared_ref)
    apart_ref[...] = jnp.zeros_like(apart_ref)
    for i, ref in enumerate(norm_refs):
        shared_ref[i : i + 1] = ref[0:1]
        shared_ref[5 + i : 6 + i] = ref[1:2]
    for i, source in enumerate((1, 3, 4)):
        shared_ref[10 + i : 11 + i] = norm_refs[source][2:3]
    for i, ref in enumerate(out_refs):
        shared_ref[13 + i : 14 + i] = ref[...]
    for i, ref in enumerate(rows_refs):
        apart_ref[i : i + 1] = ref[...]
    width = shared_ref.shape[1]
    for i, ref in enumerate(wide_refs):
        for side in range(2):
            apart_ref[3 + 2 * i + side : 4 + 2 * i + side] = ref[:, side * width : (side + 1) * width]


def pair_small_body(shared_ref, received_ref, apart_ref, out_ref):
    out_ref[0:16] = shared_ref[...] + received_ref[...]
    out_ref[16:24] = apart_ref[...]


def add_small_body(first_ref, second_ref, out_ref):
    out_ref[...] = first_ref[...] + second_ref[...]


def last_small_body(first_ref, second_ref, *outs):
    total = first_ref[...] + second_ref[...]
    gain_ref, offset_ref, out_bias_ref, two_ref, in_ref, one_ref = outs
    gain_ref[...] = total[0:5]
    offset_ref[...] = total[5:10]
    out_bias_ref[...] = total[10:13]
    two_ref[...] = total[13:15]
    width = total.shape[1]
    part = width // 2
    for i in range(3):
        for side in range(2):
            in_ref[i, side : side + 1] = total[16 + i : 17 + i, side * part : (side + 1) * part]
    for i in range(2):
        for side in range(2):
            row = 19 + 2 * i + side
            one_ref[i : i + 1, side * width : (side + 1) * width] = total[row : row + 1]


def decoded_body(base_ref, received_ref, out_ref):
    out_ref[...] = (base_ref[...] + received_ref[...].astype(F32)).astype(BF16)


def pass_body(value_ref, unused_ref, out_ref):
    out_ref[...] = value_ref[...]


def swap(values):
    return lax.ppermute(values, "tensor", [(0, 1), (1, 0)])


def across(values, stride):
    count = lax.axis_size("dp")
    return lax.ppermute(values, "dp", [(i, i ^ stride) for i in range(count)])


def dp_bits():
    return lax.axis_size("dp").bit_length() - 1


class Total:
    def __init__(self, order, place, parts, step=1):
        self.order = order
        self.place = place
        self.parts = parts
        self.step = step

    def merge(self, *others):
        assert all(self.step == other.step for other in others)
        return Total(
            self.order, self.place, self.parts + sum((other.parts for other in others), []), self.step
        )

    def finish(self, microseconds=0.2):
        while self.step < dp_bits():
            self.next()
        ((self.groups, keep, received, unused),) = self.parts
        (self.shard,) = self.order.call(
            last_sum_body, [shape(*keep.shape, BF16)], [keep, received], microseconds=microseconds
        )

    def next(self):
        if self.step == dp_bits():
            return
        width = self.parts[0][1].shape[1]
        layout = [
            (first, [rows for unused, unused, rows in groups])
            for groups, unused, unused, first in self.parts
        ]
        rows = sum(sum(segments) for unused, segments in layout) // 2
        send, keep = self.order.call(
            functools.partial(add_body, self.step, layout), [shape(rows, width, BF16)] * 2,
            [self.place, *[value for unused, *pair, unused in self.parts for value in pair]],
        )
        groups = [
            (kind, layer, rows // 2)
            for members, *unused in self.parts
            for kind, layer, rows in members
        ]
        self.parts = [(groups, keep, across(send, 1 << self.step), 0)]
        self.step += 1


def gather(order, totals):
    shards = [total.shard for total in totals]
    groups = [group for total in totals for group in total.groups]
    rows = sum(shard.shape[0] for shard in shards)
    width = shards[0].shape[1]
    enough = -(-LARGE // (2 * width * 16)) * 16
    if 0.9 * enough < rows < enough:
        rows = enough
    (stacked,) = order.call(stack_body, [shape(rows, width, BF16)], shards, leave=[0])
    return lax.all_gather(stacked, "dp"), groups


def place(order, gathered, groups, shapes):
    count, rows, width = gathered.shape
    return pl.pallas_call(
        functools.partial(place_body, groups, dp_bits()),
        grid=(count,),
        out_shape=[*[jax.ShapeDtypeStruct(shapes[name], F32) for name in NAMES], TOKEN],
        in_specs=[pl.BlockSpec((1, rows, width), lambda i: (i, 0, 0)), AWAY],
        out_specs=[AWAY] * 5,
        scratch_shapes=[
            pltpu.VMEM((2, rows, width), F32),
            pltpu.SemaphoreType.DMA((2, 2 * len(groups))),
        ],
        compiler_params=pltpu.CompilerParams(vmem_limit_bytes=VMEM_LIMIT),
        cost_estimate=pl.CostEstimate(flops=0, transcendentals=0, bytes_accessed=10 * BYTES),
    )(pltpu.with_memory_space_constraint(gathered, pltpu.HBM), order.token)[:4]


class SmallTotal:
    def __init__(self, order, place, shapes, ins):
        self.order = order
        self.place = place
        self.shapes = shapes
        self.results = None
        width = ins[0].shape[1]
        self.shared, self.apart = order.call(
            pack_body, [shape(16, width, F32), shape(8, width, F32)], ins
        )
        self.received = swap(self.shared)
        self.stages = self.run()

    def next(self):
        next(self.stages, None)

    def run(self):
        order, bits = self.order, dp_bits()
        whole = shape(24, self.shared.shape[1], F32)
        (value,) = order.call(pair_small_body, [whole], [self.shared, self.received, self.apart])
        for bit in range(bits):
            received = across(value, 1 << bit)
            yield
            if bit + 1 < bits:
                (value,) = order.call(add_small_body, [whole], [value, received])
        self.results = order.call(
            last_small_body, [jax.ShapeDtypeStruct(dims, F32) for dims in self.shapes],
            [value, received], leave=range(6),
        )
        yield


def on_device(
    src_embed, tgt_embed, src_mask, tgt_mask, objective, loss_mask, enc_cot, dec_cot,
    norm_gain, norm_bias, attn_in, attn_in_bias, attn_out, attn_out_bias,
    ffn_in, ffn_in_bias, ffn_out, ffn_out_bias,
):
    order = Order()
    here = lax.axis_index("tensor")
    width = src_embed.shape[2]
    local = attn_in.shape[3]
    hidden_width = ffn_in.shape[2]
    source_own = src_embed.reshape(-1, width)
    target_own = tgt_embed.reshape(-1, width)
    sources = 2 * source_own.shape[0]
    targets = 2 * target_own.shape[0]
    enc_own = enc_cot.reshape(-1, width)
    target_other = swap(target_own)
    source_other = swap(source_own)
    loaded = [
        source_own, target_own, dec_cot.reshape(-1, width), loss_mask, src_mask, tgt_mask, enc_own,
        norm_gain, norm_bias, attn_out_bias, ffn_out_bias, attn_in_bias, ffn_in_bias,
    ]
    source_near, target_near, dec_cot_near, loss_near, src_mask_near, tgt_mask_near, enc_own, *small_near = order.call(
        load_body, [jax.ShapeDtypeStruct(a.shape, a.dtype) for a in loaded],
        [Place(a) for a in loaded], scratch=[pltpu.SemaphoreType.DMA((len(loaded),))],
    )
    params = Params(*small_near)
    core = lax.axis_index("dp").astype(jnp.int32).reshape(1)
    here = here.astype(jnp.int32).reshape(1)

    def first(body, own, other, norm, layer, mask, more_ins, more_outs):
        count = 2 * own.shape[0]
        narrow = shape(count, local, BF16)
        return order.call(
            functools.partial(body, norm, layer),
            [
                shape(count, width, BF16), narrow, narrow, narrow,
                shape(local, count, BF16), shape(8, count, F32),
                shape(count, width, F32), shape(count, width, BF16), shape(count, 1, F32),
                *more_outs,
            ],
            [own, other, params, Weight(attn_in, layer), Weight(attn_out, layer), mask, here, *more_ins],
            microseconds=LONG,
            scratch=[pltpu.VMEM((count, local), BF16)],
        )

    def feed(before, recv, norm, layer, last):
        count = before.shape[0]
        sent = count // 2 if last else count
        return order.call(
            functools.partial(feed_body, norm, layer, last),
            [
                shape(count, width, F32), shape(count, width, BF16),
                shape(count, hidden_width, BF16), shape(count, hidden_width, BF16),
                shape(sent, width, F32), shape(sent, width, BF16),
            ],
            [before, recv, params, Weight(ffn_in, layer), Weight(ffn_out, layer)],
            microseconds=LONG,
        )

    h0, q0, k0, v0, turned0, log0, base0, send0, source_keys = first(
        enc_first_body, source_near, source_other, 0, 0, src_mask_near, [core], []
    )
    (
        h2, q1, k1, v1, turned1, log1, base1, send1, target_keys,
        target_queries, dec_own, dec_send,
    ) = first(
        dec_first_body, target_near, target_other, 2, 1, tgt_mask_near,
        [dec_cot_near, loss_near, objective, core],
        [shape(1, targets, F32), shape(targets // 2, width, F32), shape(targets // 2, width, BF16)],
    )
    recv1 = swap(send1)
    dec_other = swap(dec_send)
    recv0 = swap(send0)
    x1, h1, f0, slope0, base2, send2 = feed(base0, recv0, 1, 0, False)
    recv2 = swap(send2)
    narrow = shape(sources, local, BF16)
    memory, k2, v2, encoded = order.call(
        functools.partial(memory_body, 2),
        [shape(sources, width, BF16), narrow, narrow, shape(sources // 2, width, BF16)],
        [base2, recv2, params, Weight(attn_in, 2)], microseconds=3, leave=[3],
    )
    x3, h3, q2, turned2, log2, base3, send3 = order.call(
        functools.partial(cross_attention_body, 3, 2),
        [
            shape(targets, width, F32), shape(targets, width, BF16),
            shape(targets, local, BF16), shape(local, targets, BF16), shape(8, targets, F32),
            shape(targets, width, F32), shape(targets, width, BF16),
        ],
        [
            base1, recv1, params, Weight(attn_in, 2), Weight(attn_out, 2), k2, v2, source_keys,
        ],
        microseconds=5,
        scratch=[pltpu.VMEM((targets, local), BF16)],
    )
    recv3 = swap(send3)
    x4, h4, f1, slope1, base4, send4 = feed(base3, recv3, 4, 1, True)

    def feed_back(body, layer, *ins):
        count = ins[-1].shape[0]
        return order.call(
            body,
            [
                shape(count, width, F32), shape(count, width, BF16),
                shape(count, hidden_width, BF16),
                shape(count, width, F32), shape(count, width, BF16),
            ],
            [*ins[:-1], Weight(ffn_in, layer), Weight(ffn_out, layer), ins[-1]],
            microseconds=LONG,
        )

    def attention_back(cross, causal, g, dh, recv, x, norm, layer, q, k, v, log, key_at, *more):
        count = q.shape[0]
        keys = k.shape[0]
        outs = [
            shape(count, width, F32), shape(count, width, BF16),
            shape(count, local, BF16), shape(keys, local, BF16), shape(keys, local, BF16),
        ]
        if cross:
            outs += [
                shape(count, width, F32), shape(count, width, BF16),
                shape(keys, width, F32), shape(keys, width, BF16),
            ]
        else:
            outs += [shape(count // 2, width, F32), shape(count // 2, width, BF16)]
        outs += [shape(3, width, F32)]
        return order.call(
            functools.partial(attention_back_body, norm, cross, causal), outs,
            [
                g, dh, recv, x, params, Weight(attn_in, layer), Weight(attn_out, layer),
                q, k, v, log, key_at, *more,
            ],
            microseconds=LONG,
            scratch=[pltpu.VMEM((count, local), BF16), pltpu.VMEM((local, count), F32)],
        )

    def feed_weights(layer, h, du, f, low):
        out = shape(2 * width, width, BF16)
        send, keep, sums, hidden_sums = order.call(
            feed_weights_body, [out, out, shape(1, width, F32), shape(1, hidden_width, F32)],
            [h, du, f, low, core], microseconds=1 if layer == 0 else LONG,
        )
        received = across(send, 1)
        groups = [("in", layer, width), ("out", layer, width)]
        return Total(order, core, [(groups, keep, received, 0)]), sums, hidden_sums

    def attention_weights(layer, h, mem, dq, dk, dv, turned, low):
        out = shape(width, width, BF16)
        send, keep, sums = order.call(
            attention_weights_body, [out, out, shape(1, width, F32)],
            [h, mem, dq, dk, dv, turned, low, core], microseconds=LONG if layer == 2 else 1,
        )
        return Total(order, core, [([("attention", layer, width)], keep, across(send, 1), 0)]), sums

    def last_norm(g, dh, recv, own, norm):
        rows = own.shape[0]
        return order.call(
            functools.partial(last_norm_body, norm),
            [jax.ShapeDtypeStruct((rows, 1, width), F32), shape(2, width, F32)],
            [g, dh, recv, own, params], leave=[0],
        )

    g4, low4, du1, dh4, dh4_send = feed_back(
        dec_feed_back_body, 1, dec_own, dec_other, slope1
    )
    dh4_recv = swap(dh4_send)
    feed1, two1, one1 = feed_weights(1, h4, du1, f1, low4)
    feed1.next()
    g3, low3, dq2, dk2, dv2, dh3, dh3_send, mem_grad, mem_send, sums4 = attention_back(
        True, False, g4, dh4, dh4_recv, x4, 4, 2, q2, k2, v2, log2, source_keys, enc_own, objective
    )
    mem_recv = swap(mem_send)
    dh3_recv = swap(dh3_send)
    cross, bias2 = attention_weights(2, h3, memory, dq2, dk2, dv2, turned2, low3)
    feed1.next()
    g1, low1, du0, dh1, dh1_send = feed_back(
        enc_feed_back_body, 0, enc_own, objective, mem_grad, mem_recv, slope0
    )
    dh1_recv = swap(dh1_send)
    cross.next()
    feed0, two0, one0 = feed_weights(0, h1, du0, f0, low1)
    g2, low2, dq1, dk1, dv1, dh2, dh2_send, sums3 = attention_back(
        False, True, g3, dh3, dh3_recv, x3, 3, 1, q1, k1, v1, log1, target_keys, target_queries
    )
    dh2_recv = swap(dh2_send)
    first1, bias1 = attention_weights(1, h2, h2, dq1, dk1, dv1, turned1, low2)
    feed0.next()
    feed1.next()
    cross.next()
    g0, low0, dq0, dk0, dv0, dh0, dh0_send, sums1 = attention_back(
        False, False, g1, dh1, dh1_recv, x1, 1, 0, q0, k0, v0, log0, source_keys
    )
    dh0_recv = swap(dh0_send)
    first0, bias0 = attention_weights(0, h0, h0, dq0, dk0, dv0, turned0, low0)
    feed0.next()
    feed1.finish(LONG)
    late = first1.merge(first0)
    late.next()
    source_grad, sums0 = last_norm(g0, dh0, dh0_recv, source_near, 0)
    target_grad, sums2 = last_norm(g2, dh2, dh2_recv, target_near, 2)
    small = SmallTotal(
        order, core,
        [
            norm_gain.shape, norm_bias.shape, attn_out_bias.shape, ffn_out_bias.shape,
            attn_in_bias.shape, ffn_in_bias.shape,
        ],
        [sums0, sums1, sums2, sums3, sums4, two0, two1, bias0, bias1, bias2, one0, one1],
    )
    middle = cross.merge(feed0)
    middle.next()
    late.next()
    small.next()
    middle.finish()
    late.next()
    small.next()
    late.finish()
    gathered, groups = gather(order, [feed1, middle, late])
    for unused in range(dp_bits()):
        small.next()
    decoded_other = swap(send4)
    (decoded,) = order.call(
        decoded_body, [shape(targets // 2, width, BF16)], [base4, decoded_other], leave=[0]
    )
    stacks = dict(zip(NAMES, place(
        order, gathered, groups,
        dict(zip(NAMES, (ffn_in.shape, ffn_out.shape, attn_in.shape, attn_out.shape))),
    )))
    gains, offsets, out_biases, two_biases, in_biases, one_biases = small.results
    return (
        encoded[:, None],
        decoded[:, None],
        source_grad,
        target_grad,
        gains,
        offsets,
        stacks["attn_in"],
        in_biases,
        stacks["attn_out"],
        out_biases,
        stacks["ffn_in"],
        one_biases,
        stacks["ffn_out"],
        two_biases,
    )


def solution(mesh):
    tokens = P("tensor", "dp", None)
    return jax.shard_map(
        on_device,
        mesh=mesh,
        in_specs=(
            tokens, tokens, P("dp", None), P("dp", None), P("dp"), P("dp", "tensor"),
            tokens, tokens, P(), P(),
            P(None, None, None, "tensor"), P(None, None, "tensor"), P(None, "tensor", None), P(),
            P(None, None, "tensor"), P(None, "tensor"), P(None, "tensor", None), P(),
        ),
        out_specs=(
            tokens, tokens, tokens, tokens, P(), P(),
            P(None, None, None, "tensor"), P(None, None, "tensor"), P(None, "tensor", None), P(),
            P(None, None, "tensor"), P(None, "tensor"), P(None, "tensor", None), P(),
        ),
        check_vma=False,
    )
```

```python
import functools

import jax
import jax.numpy as jnp
from jax import lax
from jax.experimental import pallas as pl
from jax.experimental.pallas import tpu as pltpu
from jax.sharding import PartitionSpec as P

HEAD = 64
PAIR = 2 * HEAD
EPSILON = 1e-05
MASKED_SCORE = -1000000000.0
FAR = 1e9
ROOT = 0.7978845608028654
CUBIC = 0.044715
BF16 = jnp.bfloat16
F32 = jnp.float32
VMEM_LIMIT = 18 * 1024 * 1024
BYTES = 3690000
NN = ((1,), (0,))
NT = ((1,), (1,))
TN = ((0,), (0,))
LARGE = 1 << 20
LONG = 40
TAIL = 4
SLOTS = 4
NAMES = ("ffn_in", "ffn_out", "attn_in", "attn_out")
TOKEN = jax.ShapeDtypeStruct((8, 128), F32)


def dot(left, right, contract):
    return lax.dot_general(left, right, (contract, ((), ())), preferred_element_type=F32)


def shape(rows, columns, dtype):
    return jax.ShapeDtypeStruct((rows, columns), dtype)


NEAR = pl.BlockSpec(memory_space=pltpu.VMEM)
AWAY = pl.BlockSpec(memory_space=pl.ANY)
NUMBER = pl.BlockSpec(memory_space=pltpu.SMEM)


class Weight:
    def __init__(self, stack, layer):
        self.stack = stack
        self.layer = layer


class Place:
    def __init__(self, array):
        self.array = array


class Params:
    def __init__(self, *arrays):
        self.arrays = arrays


class Fetch:
    def __init__(self, source, buffer, semaphore):
        self.copy = pltpu.make_async_copy(source, buffer, semaphore)
        self.copy.start()
        self.buffer = buffer
        self.arrived = False

    def here(self):
        if not self.arrived:
            self.copy.wait()
            self.arrived = True
        return self.buffer


class Order:
    def __init__(self):
        self.token = None

    def call(
        self, body, outs, ins, microseconds=0.2, scratch=(), leave=(), away=(), aliases={},
        limit=VMEM_LIMIT,
    ):
        tokens = [] if self.token is None else [self.token]
        specs, args, weights, groups = [], [], [], []
        for value in ins:
            if isinstance(value, Params):
                groups.append(len(args))
                for array in value.arrays:
                    specs.append(NEAR)
                    args.append(pltpu.with_memory_space_constraint(array, pltpu.VMEM))
            elif isinstance(value, Place):
                specs.append(AWAY)
                args.append(pltpu.with_memory_space_constraint(value.array, pltpu.HBM))
            elif isinstance(value, Weight):
                weights.append((len(args), value))
                specs.append(AWAY)
                args.append(pltpu.with_memory_space_constraint(value.stack, pltpu.HBM))
            elif value.dtype == jnp.int32 and value.shape == (1,):
                specs.append(NUMBER)
                args.append(value)
            else:
                specs.append(NEAR)
                args.append(pltpu.with_memory_space_constraint(value, pltpu.VMEM))

        def wrapped(*refs):
            in_refs = list(refs[: len(args)])
            refs = refs[len(args) + len(tokens) :]
            out_refs = refs[: len(outs)]
            refs = refs[len(outs) + 1 :]
            if weights:
                semaphores = refs[-1]
                for i, (at, weight) in enumerate(weights):
                    in_refs[at] = Fetch(in_refs[at].at[weight.layer], refs[i], semaphores.at[i])
            for at in reversed(groups):
                in_refs[at : at + 6] = [in_refs[at : at + 6]]
            body(*in_refs, *out_refs, *refs[len(weights) : len(weights) + len(scratch)])

        buffers = [pltpu.VMEM(w.stack.shape[1:], w.stack.dtype) for unused, w in weights]
        semaphores = [pltpu.SemaphoreType.DMA((len(weights),))] if weights else []
        results = pl.pallas_call(
            wrapped,
            out_shape=[
                *[
                    o if i in leave or i in away else pltpu.VMEM(o.shape, o.dtype)
                    for i, o in enumerate(outs)
                ],
                TOKEN,
            ],
            in_specs=specs + [AWAY] * len(tokens),
            out_specs=[AWAY if i in away else NEAR for i in range(len(outs))] + [AWAY],
            scratch_shapes=[*buffers, *scratch, *semaphores],
            input_output_aliases=aliases,
            compiler_params=pltpu.CompilerParams(vmem_limit_bytes=limit),
            cost_estimate=pl.CostEstimate(
                flops=int(microseconds * 1.15e9), transcendentals=0, bytes_accessed=int(microseconds * BYTES)
            ),
        )(*args, *tokens)
        self.token = results[-1]
        return results[:-1]


def norm_parts(inputs):
    centre = inputs - jnp.mean(inputs, axis=-1, keepdims=True)
    inverse = lax.rsqrt(jnp.mean(centre * centre, axis=-1, keepdims=True) + EPSILON)
    return centre * inverse, inverse


def norm_back(gradient, normed, inverse, gain):
    scaled = gradient * gain
    mean_plain = jnp.mean(scaled, axis=-1, keepdims=True)
    mean_normed = jnp.mean(scaled * normed, axis=-1, keepdims=True)
    return inverse * (scaled - mean_plain - normed * mean_normed)


def column_sum(values):
    return jnp.sum(values.astype(F32), axis=0, keepdims=True)


def halves(count):
    half = count // 2
    return ((0, half), (half, 0))


def lane_half(which, rows):
    lanes = lax.broadcasted_iota(jnp.int32, (rows, PAIR), 1)
    return (lanes >= HEAD) if which else (lanes < HEAD)


def only_head(which, values):
    return jnp.where(lane_half(which, values.shape[0]), values, jnp.zeros_like(values))


def key_scores(key_pair, query_pair, which, key_at, query_at):
    scores = dot(only_head(which, key_pair), query_pair, NT)
    return jnp.where(key_at <= query_at, scores, MASKED_SCORE)


def attend(q_ref, k_ref, v_ref, key_at, query_at_ref, turned_ref, o_ref, log_ref):
    queries, local = q_ref.shape
    block = min(queries, 256)
    for pair in range(local // PAIR):
        columns = pl.ds(pair * PAIR, PAIR)
        key_pair = k_ref[:, columns]
        value_turned = v_ref[:, columns].astype(F32).T.astype(BF16)
        for start in range(0, queries, block):
            rows = pl.ds(start, block)
            query_pair = q_ref[rows, columns]
            query_at = 0.0 if query_at_ref is None else query_at_ref[:, rows]
            for which in range(2):
                head = 2 * pair + which
                scores = key_scores(key_pair, query_pair, which, key_at, query_at)
                top = jnp.max(scores, axis=0, keepdims=True)
                exponent = jnp.exp(scores - top)
                total = jnp.sum(exponent, axis=0, keepdims=True)
                weights = (exponent * (1.0 / total)).astype(BF16)
                log_ref[pl.ds(head, 1), rows] = top + jnp.log(total)
                mixed = dot(value_turned[which * HEAD : (which + 1) * HEAD], weights, NN)
                turned_ref[pl.ds(head * HEAD, HEAD), rows] = mixed.astype(BF16)
    o_ref[...] = turned_ref[...].astype(F32).T.astype(BF16)


def in_bias_rows(params, layer):
    return params[4][layer, 0:1], params[4][layer, 1:2]


def row_of(ref, index):
    return ref[index : index + 1]


def normalised(value, params, norm):
    normed, unused = norm_parts(value)
    return (normed * row_of(params[0], norm) + row_of(params[1], norm)).astype(BF16)


def column(row):
    return jnp.broadcast_to(row, (8, row.shape[1])).T[:, 0:1]


def own_first(row, here):
    half = row.shape[1] // 2
    return jnp.where(here == 0, row, jnp.concatenate([row[:, half:], row[:, :half]], axis=1))


def scaled_queries(hidden, w_in, bias):
    return ((dot(hidden, w_in[0], NN) + bias).astype(BF16) * HEAD ** (-0.5)).astype(BF16)


def load_body(*refs):
    count = len(refs) // 2
    copies = [
        pltpu.make_async_copy(refs[i], refs[count + i], refs[-1].at[i]) for i in range(count)
    ]
    for copy in copies:
        copy.start()
    for copy in copies:
        copy.wait()


def first_attention(norm, layer, own_ref, other_ref, params, w_in, w_out, key_at, query_at_ref, *refs):
    h_ref, q_ref, k_ref, v_ref, turned_ref, log_ref, base_ref, send_ref, o_ref = refs
    half = own_ref.shape[0]
    query_bias, value_bias = in_bias_rows(params, layer)
    for part, source in enumerate((own_ref, other_ref)):
        rows = pl.ds(part * half, half)
        hidden = normalised(source[...].astype(F32), params, norm)
        h_ref[rows] = hidden
        w = w_in.here()
        q_ref[rows] = scaled_queries(hidden, w, query_bias)
        k_ref[rows] = dot(hidden, w[1], NN).astype(BF16)
        v_ref[rows] = (dot(hidden, w[2], NN) + value_bias).astype(BF16)
    attend(q_ref, k_ref, v_ref, key_at, query_at_ref, turned_ref, o_ref, log_ref)
    w = w_out.here()
    for part, source in enumerate((own_ref, other_ref)):
        rows = pl.ds(part * half, half)
        partial = dot(o_ref[rows], w[...], NN)
        send_ref[rows] = partial.astype(BF16)
        base_ref[rows] = source[...].astype(F32) + row_of(params[2], layer) + partial


def enc_first_body(norm, layer, own_ref, other_ref, params, w_in, w_out, mask_ref, here_ref, place_ref, *refs):
    outs, key_at_ref, o_ref = refs[:-2], refs[-2], refs[-1]
    row = own_first(jnp.where(mask_ref[...] == 1, 0.0, FAR), here_ref[0])
    key_at = column(row)
    key_at_ref[...] = key_at
    first_attention(norm, layer, own_ref, other_ref, params, w_in, w_out, key_at, None, *outs, o_ref)


def dec_first_body(
    norm, layer, own_ref, other_ref, params, w_in, w_out, mask_ref, here_ref,
    cot_ref, loss_ref, objective_ref, place_ref, *refs
):
    outs, (key_at_ref, query_at_ref, gradient_ref, gradient_send_ref, o_ref) = refs[:-5], refs[-5:]
    count = mask_ref.shape[1]
    position = own_first(
        lax.broadcasted_iota(jnp.int32, (1, count), 1).astype(F32), here_ref[0]
    )
    row = jnp.where(own_first(mask_ref[...].astype(F32), here_ref[0]) == 1.0, position, FAR)
    key_at = column(row)
    key_at_ref[...] = key_at
    query_at_ref[...] = position
    flag = objective_ref[0].astype(F32)
    weight = column(0.25 + 0.75 * loss_ref[...].astype(F32)) * (0.5 + 0.5 * flag)
    gradient = cot_ref[...].astype(F32) * weight
    gradient_ref[...] = gradient
    gradient_send_ref[...] = gradient.astype(BF16)
    first_attention(
        norm, layer, own_ref, other_ref, params, w_in, w_out, key_at, query_at_ref, *outs, o_ref
    )


def cross_attention_body(
    norm, layer, before_ref, recv_ref, params, w_in, w_out, k_ref, v_ref, key_at_ref,
    x_ref, h_ref, q_ref, turned_ref, log_ref, base_ref, send_ref, o_ref,
):
    count = x_ref.shape[0]
    half = count // 2
    query_bias, unused = in_bias_rows(params, layer)
    for mine, theirs in halves(count):
        rows = pl.ds(mine, half)
        value = before_ref[rows] + recv_ref[pl.ds(theirs, half)].astype(F32)
        x_ref[rows] = value
        hidden = normalised(value, params, norm)
        h_ref[rows] = hidden
        q_ref[rows] = scaled_queries(hidden, w_in.here(), query_bias)
    attend(q_ref, k_ref, v_ref, key_at_ref[...], None, turned_ref, o_ref, log_ref)
    partial = dot(o_ref[...], w_out.here()[...], NN)
    send_ref[...] = partial.astype(BF16)
    base_ref[...] = x_ref[...] + row_of(params[2], layer) + partial


def memory_body(layer, before_ref, recv_ref, params, w_in, mem_ref, k_ref, v_ref, out_ref):
    count = mem_ref.shape[0]
    half = count // 2
    unused, value_bias = in_bias_rows(params, layer)
    for mine, theirs in halves(count):
        rows = pl.ds(mine, half)
        memory = (before_ref[rows] + recv_ref[pl.ds(theirs, half)].astype(F32)).astype(BF16)
        mem_ref[rows] = memory
        if mine == 0:
            out_ref[...] = memory
        w = w_in.here()
        k_ref[rows] = dot(memory, w[1], NN).astype(BF16)
        v_ref[rows] = (dot(memory, w[2], NN) + value_bias).astype(BF16)


def feed_body(
    norm, layer, last, before_ref, recv_ref, params, w_one, w_two,
    x_ref, h_ref, f_ref, slope_ref, base_ref, send_ref,
):
    count = x_ref.shape[0]
    half = count // 2
    for mine, theirs in halves(count):
        rows = pl.ds(mine, half)
        value = before_ref[rows] + recv_ref[pl.ds(theirs, half)].astype(F32)
        x_ref[rows] = value
        hidden = normalised(value, params, norm)
        h_ref[rows] = hidden
        u = dot(hidden, w_one.here()[...], NN) + row_of(params[5], layer)
        square = u * u
        bent = jnp.tanh(u * (ROOT + (ROOT * CUBIC) * square))
        upper = 0.5 + 0.5 * bent
        active = (u * upper).astype(BF16)
        f_ref[rows] = active
        slope = upper + (0.5 * u) * (1.0 - bent * bent) * (ROOT + (3 * ROOT * CUBIC) * square)
        slope_ref[rows] = slope.astype(BF16)
        partial = dot(active, w_two.here()[...], NN)
        if not last:
            send_ref[rows] = partial.astype(BF16)
            base_ref[rows] = value + row_of(params[3], layer) + partial
        elif mine == 0:
            base_ref[...] = value + row_of(params[3], layer) + partial
        else:
            send_ref[...] = partial.astype(BF16)


def feed_back_rows(
    gradient, rows, w_one, w_two, slope_ref, g_ref, low_ref, du_ref, base_ref, send_ref
):
    g_ref[rows] = gradient
    low = gradient.astype(BF16)
    low_ref[rows] = low
    du = (dot(low, w_two.here()[...], NT) * slope_ref[rows].astype(F32)).astype(BF16)
    du_ref[rows] = du
    partial = dot(du, w_one.here()[...], NT)
    send_ref[rows] = partial.astype(BF16)
    base_ref[rows] = partial


def dec_feed_back_body(own_ref, other_ref, w_one, w_two, slope_ref, *outs):
    half = own_ref.shape[0]
    for part, source in enumerate((own_ref, other_ref)):
        feed_back_rows(
            source[...].astype(F32), pl.ds(part * half, half), w_one, w_two, slope_ref, *outs
        )


def source_seed(cot_ref, objective_ref):
    return cot_ref[...].astype(F32) * (1.0 - 0.5 * objective_ref[0].astype(F32))


def enc_feed_back_body(seed_ref, objective_ref, mem_base_ref, recv_ref, w_one, w_two, slope_ref, *outs):
    half = seed_ref.shape[0]
    own, other = pl.ds(0, half), pl.ds(half, half)
    for rows, theirs in ((own, other), (other, own)):
        gradient = mem_base_ref[rows] + recv_ref[theirs].astype(F32)
        if rows is own:
            gradient = gradient + source_seed(seed_ref, objective_ref)
        feed_back_rows(gradient, rows, w_one, w_two, slope_ref, *outs)


def attention_back_body(norm, cross, causal, *refs):
    (g_in_ref, dh_ref, dh_recv_ref, x_ref, params, w_in, w_out, q_ref, k_ref, v_ref, log_ref,
     key_at_ref), refs = refs[:12], refs[12:]
    query_at_ref = seed_ref = mem_base_ref = mem_send_ref = None
    if causal:
        query_at_ref, refs = refs[0], refs[1:]
    if cross:
        (seed_ref, objective_ref), refs = refs[:2], refs[2:]
    (g_ref, low_ref, dq_ref, dk_ref, dv_ref, base_ref, send_ref), refs = refs[:7], refs[7:]
    if cross:
        (mem_base_ref, mem_send_ref), refs = refs[:2], refs[2:]
    sums_ref, do_ref, turned_ref = refs
    gain = row_of(params[0], norm)
    count, local = dq_ref.shape
    half = count // 2
    for part, (mine, theirs) in enumerate(halves(count)):
        rows = pl.ds(mine, half)
        normed, inverse = norm_parts(x_ref[rows])
        dh = dh_ref[rows] + dh_recv_ref[pl.ds(theirs, half)].astype(F32)
        gradient = g_in_ref[rows] + norm_back(dh, normed, inverse, gain)
        g_ref[rows] = gradient
        low = gradient.astype(BF16)
        low_ref[rows] = low
        if part == 0:
            sums_ref[0:1] = column_sum(dh * normed)
            sums_ref[1:2] = column_sum(dh)
            sums_ref[2:3] = column_sum(low)
        do_ref[rows] = dot(low, w_out.here()[...], NT).astype(BF16)
    key_at = key_at_ref[...]
    block = min(count, 256)
    keys = k_ref.shape[0]
    for pair in range(local // PAIR):
        columns = pl.ds(pair * PAIR, PAIR)
        key_pair = k_ref[:, columns]
        key_turned = key_pair.astype(F32).T.astype(BF16)
        value_pair = v_ref[:, columns]
        dk = [None, None]
        dv = [None, None]
        for start in range(0, count, block):
            rows = pl.ds(start, block)
            query_pair = q_ref[rows, columns]
            do_pair = do_ref[rows, columns]
            query_at = 0.0 if query_at_ref is None else query_at_ref[:, rows]
            for which in range(2):
                head = 2 * pair + which
                scores = key_scores(key_pair, query_pair, which, key_at, query_at)
                probs = jnp.exp(scores - log_ref[pl.ds(head, 1), rows])
                prob_grad = dot(only_head(which, value_pair), do_pair, NT)
                product = probs * prob_grad
                inner = jnp.sum(product, axis=0, keepdims=True)
                score_grad = (product - probs * inner).astype(BF16)
                dv_part = dot(probs.astype(BF16), do_pair, NN)
                dk_part = dot(score_grad, query_pair, NN)
                dq_part = dot(key_turned[which * HEAD : (which + 1) * HEAD], score_grad, NN)
                turned_ref[pl.ds(head * HEAD, HEAD), rows] = dq_part * HEAD ** (-0.5)
                dk[which] = dk_part if dk[which] is None else dk[which] + dk_part
                dv[which] = dv_part if dv[which] is None else dv[which] + dv_part
        first = lane_half(0, keys)
        dk_ref[:, columns] = jnp.where(first, dk[0], dk[1]).astype(BF16)
        dv_ref[:, columns] = jnp.where(first, dv[0], dv[1]).astype(BF16)
    dq_ref[...] = turned_ref[...].T.astype(BF16)
    w = w_in.here()
    if cross:
        partial = dot(dk_ref[...], w[1], NT) + dot(dv_ref[...], w[2], NT)
        mem_base_ref[...] = partial
        mem_half = keys // 2
        mem_send_ref[0:mem_half] = (
            partial[0:mem_half] + source_seed(seed_ref, objective_ref)
        ).astype(BF16)
        mem_send_ref[mem_half:] = partial[mem_half:].astype(BF16)
        partial = dot(dq_ref[...], w[0], NT)
        send_ref[...] = partial.astype(BF16)
        base_ref[...] = partial
    else:
        for part in (1, 0):
            rows = pl.ds(part * half, half)
            partial = (
                dot(dq_ref[rows], w[0], NT)
                + dot(dk_ref[rows], w[1], NT)
                + dot(dv_ref[rows], w[2], NT)
            )
            if part == 1:
                send_ref[...] = partial.astype(BF16)
            else:
                base_ref[...] = partial


def last_norm_body(norm, g_ref, dh_ref, recv_ref, x_ref, params, out_ref, sums_ref):
    normed, inverse = norm_parts(x_ref[...].astype(F32))
    dh = dh_ref[...] + recv_ref[...].astype(F32)
    sums_ref[0:1] = column_sum(dh * normed)
    sums_ref[1:2] = column_sum(dh)
    half = out_ref.shape[0]
    result = g_ref[0:half] + norm_back(dh, normed, inverse, row_of(params[0], norm))
    out_ref[...] = result.reshape(out_ref.shape)


def feed_weights_body(h_ref, du_ref, f_ref, low_ref, place_ref, send_ref, keep_ref, sums_ref, hidden_sums_ref):
    bit = bit_of(place_ref, 0)
    width = h_ref.shape[1]
    part = width // 2
    for which, out_ref in ((1 - bit, send_ref), (bit, keep_ref)):
        left = h_ref[:, pl.ds(pl.multiple_of(which * part, 128), part)]
        for side in range(2):
            out_ref[pl.ds(side * part, part)] = dot(
                left, du_ref[:, pl.ds(side * width, width)], TN
            ).astype(BF16)
        left = f_ref[:, pl.ds(pl.multiple_of(which * width, 128), width)]
        out_ref[pl.ds(width, width)] = dot(left, low_ref[...], TN).astype(BF16)
    half = low_ref.shape[0] // 2
    sums_ref[...] = column_sum(low_ref[0:half])
    hidden_sums_ref[...] = column_sum(du_ref[...])


def attention_weights_body(
    h_ref, mem_ref, dq_ref, dk_ref, dv_ref, turned_ref, low_ref, place_ref, *refs
):
    later_ref, refs = (refs[0], refs[1:]) if len(refs) == 5 else (None, refs)
    send_ref, keep_ref, sums_ref = refs[:3]
    if later_ref is not None:
        refs[3][...] = later_ref[...]
    bit = bit_of(place_ref, 0)
    width = h_ref.shape[1]
    part = width // 2
    quarter = width // 4
    left_side = pl.ds(0, part)
    right_side = pl.ds(part, part)
    for which, out_ref in ((1 - bit, send_ref), (bit, keep_ref)):
        columns = pl.ds(pl.multiple_of(which * part, 128), part)
        out_ref[pl.ds(0, part), left_side] = dot(h_ref[:, columns], dq_ref[...], TN).astype(BF16)
        memory = mem_ref[:, columns]
        out_ref[pl.ds(0, part), right_side] = dot(memory, dk_ref[...], TN).astype(BF16)
        values = dot(memory, dv_ref[...], TN).astype(BF16)
        out_ref[pl.ds(part, quarter), left_side] = values[:quarter]
        out_ref[pl.ds(part, quarter), right_side] = values[quarter:]
        rows = pl.ds(pl.multiple_of(which * quarter, 64), quarter)
        out_ref[pl.ds(part + quarter, quarter)] = dot(turned_ref[rows], low_ref[...], NN).astype(BF16)
    sums_ref[:, left_side] = column_sum(dq_ref[...])
    sums_ref[:, right_side] = column_sum(dv_ref[...])


def bit_of(place_ref, step):
    return (place_ref[0] >> step) & 1


def add_body(step, layout, place_ref, *refs):
    send_ref, next_ref = refs[-2:]
    bit = bit_of(place_ref, step)
    for out_ref, which in ((send_ref, 1 - bit), (next_ref, bit)):
        target = 0
        for i, (first, segments) in enumerate(layout):
            keep_ref, received_ref = refs[2 * i], refs[2 * i + 1]
            for rows in segments:
                half = rows // 2
                block = half
                while block % 32 == 0 and block > 128:
                    block //= 2
                for start in range(0, half, block):
                    part = pl.ds(pl.multiple_of(first + which * half + start, 8), block)
                    out_ref[pl.ds(target + start, block)] = (
                        keep_ref[part].astype(F32) + received_ref[part].astype(F32)
                    ).astype(BF16)
                first += rows
                target += half


def last_sum_body(keep_ref, received_ref, out_ref):
    out_ref[...] = (keep_ref[...].astype(F32) + received_ref[...].astype(F32)).astype(BF16)


def join_body(first_ref, second_ref, out_ref):
    rows = first_ref.shape[0]
    out_ref[0:rows] = first_ref[...]
    out_ref[rows:] = second_ref[...]


def put_body(groups, masks, bits, old, place_ref, block_ref, *refs):
    refs = refs[old:]
    outs = dict(zip(NAMES, refs[:4]))
    wide_ref, semaphores = refs[4:]
    width = block_ref.shape[1]
    part, quarter = width // 2, width // 4
    slots = wide_ref.shape[0]
    flying = []

    def copy(slot, side, rows, target):
        source = wide_ref.at[slot, pl.ds(0, rows), pl.ds(side * part, part)]
        return pltpu.make_async_copy(source, target, semaphores.at[slot, side])

    def wait(slot, rows):
        for side in range(2):
            target = outs["ffn_out"].at[0, pl.ds(0, rows), pl.ds(0, part)]
            copy(slot, side, rows, target).wait()

    at = 0
    for mask in masks:
        device = place_ref[0] ^ mask
        upper = device & 1
        for kind, layer, rows in groups:
            slot = len(flying) % slots
            if len(flying) >= slots:
                wait(*flying[-slots])
            flying.append((slot, rows))
            wide_ref[slot, pl.ds(0, rows)] = block_ref[pl.ds(at, rows)].astype(F32)
            at += rows
            inner = 0
            for bit in range(1, bits):
                inner = inner + ((device >> bit) & 1) * (rows << (bits - 1 - bit))

            def send(side, target):
                copy(slot, side, rows, target).start()

            if kind == "in":
                row = pl.multiple_of(upper * part + lax.rem(inner, part), 8)
                column = lax.div(inner, part) * width
                for side in range(2):
                    columns = pl.ds(pl.multiple_of(column + side * part, 128), part)
                    send(side, outs["ffn_in"].at[layer, pl.ds(row, rows), columns])
            elif kind == "out":
                row = pl.multiple_of(upper * width + inner, 8)
                for side in range(2):
                    columns = pl.ds(side * part, part)
                    send(side, outs["ffn_out"].at[layer, pl.ds(row, rows), columns])
            else:

                @pl.when(inner < part)
                def query_and_key():
                    row = pl.multiple_of(upper * part + inner, 8)
                    for side in range(2):
                        send(side, outs["attn_in"].at[layer, side, pl.ds(row, rows)])

                @pl.when((inner >= part) & (inner < part + quarter))
                def value():
                    row = upper * part + inner - part
                    for side in range(2):
                        target = pl.ds(pl.multiple_of(row + side * quarter, 8), rows)
                        send(side, outs["attn_in"].at[layer, 2, target])

                @pl.when(inner >= part + quarter)
                def output():
                    row = pl.multiple_of(upper * quarter + inner - part - quarter, 8)
                    for side in range(2):
                        columns = pl.ds(side * part, part)
                        send(side, outs["attn_out"].at[layer, pl.ds(row, rows), columns])

    for slot, rows in flying[-slots:]:
        wait(slot, rows)


def pack_body(*refs):
    norm_refs, out_refs, rows_refs, wide_refs = refs[:5], refs[5:7], refs[7:10], refs[10:12]
    shared_ref, apart_ref = refs[12:]
    shared_ref[...] = jnp.zeros_like(shared_ref)
    apart_ref[...] = jnp.zeros_like(apart_ref)
    for i, ref in enumerate(norm_refs):
        shared_ref[i : i + 1] = ref[0:1]
        shared_ref[5 + i : 6 + i] = ref[1:2]
    for i, source in enumerate((1, 3, 4)):
        shared_ref[10 + i : 11 + i] = norm_refs[source][2:3]
    for i, ref in enumerate(out_refs):
        shared_ref[13 + i : 14 + i] = ref[...]
    for i, ref in enumerate(rows_refs):
        apart_ref[i : i + 1] = ref[...]
    width = shared_ref.shape[1]
    for i, ref in enumerate(wide_refs):
        for side in range(2):
            apart_ref[3 + 2 * i + side : 4 + 2 * i + side] = ref[:, side * width : (side + 1) * width]


def pair_small_body(shared_ref, received_ref, apart_ref, out_ref):
    out_ref[0:16] = shared_ref[...] + received_ref[...]
    out_ref[16:24] = apart_ref[...]


def add_small_body(first_ref, second_ref, out_ref):
    out_ref[...] = first_ref[...] + second_ref[...]


def last_small_body(first_ref, second_ref, *outs):
    total = first_ref[...] + second_ref[...]
    gain_ref, offset_ref, out_bias_ref, two_ref, in_ref, one_ref = outs
    gain_ref[...] = total[0:5]
    offset_ref[...] = total[5:10]
    out_bias_ref[...] = total[10:13]
    two_ref[...] = total[13:15]
    width = total.shape[1]
    part = width // 2
    for i in range(3):
        for side in range(2):
            in_ref[i, side : side + 1] = total[16 + i : 17 + i, side * part : (side + 1) * part]
    for i in range(2):
        for side in range(2):
            row = 19 + 2 * i + side
            one_ref[i : i + 1, side * width : (side + 1) * width] = total[row : row + 1]


def decoded_body(base_ref, received_ref, out_ref):
    out_ref[...] = (base_ref[...] + received_ref[...].astype(F32)).astype(BF16)


def pass_body(value_ref, unused_ref, out_ref):
    out_ref[...] = value_ref[...]


def swap(values):
    return lax.ppermute(values, "tensor", [(0, 1), (1, 0)])


def across(values, stride):
    count = lax.axis_size("dp")
    return lax.ppermute(values, "dp", [(i, i ^ stride) for i in range(count)])


def dp_bits():
    return lax.axis_size("dp").bit_length() - 1


class Total:
    def __init__(self, order, place, parts, step=1):
        self.order = order
        self.place = place
        self.parts = parts
        self.step = step

    def merge(self, *others):
        assert all(self.step == other.step for other in others)
        return Total(
            self.order, self.place, self.parts + sum((other.parts for other in others), []), self.step
        )

    def finish(self, microseconds=0.2):
        while self.step < dp_bits():
            self.next()
        ((self.groups, keep, received, unused),) = self.parts
        (self.shard,) = self.order.call(
            last_sum_body, [shape(*keep.shape, BF16)], [keep, received], microseconds=microseconds
        )

    def next(self, microseconds=0.2):
        if self.step == dp_bits():
            return
        width = self.parts[0][1].shape[1]
        layout = [
            (first, [rows for unused, unused, rows in groups])
            for groups, unused, unused, first in self.parts
        ]
        rows = sum(sum(segments) for unused, segments in layout) // 2
        send, keep = self.order.call(
            functools.partial(add_body, self.step, layout), [shape(rows, width, BF16)] * 2,
            [self.place, *[value for unused, *pair, unused in self.parts for value in pair]],
            microseconds=microseconds,
        )
        groups = [
            (kind, layer, rows // 2)
            for members, *unused in self.parts
            for kind, layer, rows in members
        ]
        self.parts = [(groups, keep, across(send, 1 << self.step), 0)]
        self.step += 1


class Gathered:
    def __init__(self, total, stacks, microseconds=TAIL):
        self.order = total.order
        self.place = total.place
        self.stacks = stacks
        total.finish(microseconds)
        self.groups = total.groups
        self.stages = self.run(total.shard)
        self.next()

    def next(self):
        next(self.stages, None)

    def run(self, block):
        order = self.order
        masks = [0]
        for bit in range(dp_bits() - 1, -1, -1):
            received = across(block, 1 << bit)
            yield
            if bit:
                (block,) = order.call(
                    join_body, [shape(2 * block.shape[0], block.shape[1], BF16)], [block, received],
                    microseconds=TAIL,
                )
                masks += [mask ^ (1 << bit) for mask in masks]
        self.put(block, masks)
        yield
        self.put(received, [mask ^ 1 for mask in masks])
        yield

    def put(self, block, masks):
        stacks = self.stacks
        old = [stacks[name] for name in NAMES] if NAMES[0] in stacks else []
        rows = max(rows for unused, unused, rows in self.groups)
        results = self.order.call(
            functools.partial(put_body, self.groups, masks, dp_bits(), len(old)),
            [jax.ShapeDtypeStruct(stacks["shapes"][name], F32) for name in NAMES],
            [self.place, block, *[Place(value) for value in old]],
            aliases={2 + i: i for i in range(len(old))},
            away=range(4),
            microseconds=TAIL,
            scratch=[
                pltpu.VMEM((6, rows, block.shape[1]), F32),
                pltpu.SemaphoreType.DMA((6, 2)),
            ],
        )
        stacks.update(zip(NAMES, results))


class SmallTotal:
    def __init__(self, order, place, shapes, ins):
        self.order = order
        self.place = place
        self.shapes = shapes
        self.results = None
        width = ins[0].shape[1]
        self.shared, self.apart = order.call(
            pack_body, [shape(16, width, F32), shape(8, width, F32)], ins
        )
        self.received = swap(self.shared)
        self.stages = self.run()

    def next(self):
        next(self.stages, None)

    def run(self):
        order, bits = self.order, dp_bits()
        whole = shape(24, self.shared.shape[1], F32)
        (value,) = order.call(pair_small_body, [whole], [self.shared, self.received, self.apart], microseconds=TAIL)
        for bit in range(bits):
            received = across(value, 1 << bit)
            yield
            if bit + 1 < bits:
                (value,) = order.call(add_small_body, [whole], [value, received], microseconds=TAIL)
        self.results = order.call(
            last_small_body, [jax.ShapeDtypeStruct(dims, F32) for dims in self.shapes],
            [value, received], leave=range(6),
        )
        yield


def on_device(
    src_embed, tgt_embed, src_mask, tgt_mask, objective, loss_mask, enc_cot, dec_cot,
    norm_gain, norm_bias, attn_in, attn_in_bias, attn_out, attn_out_bias,
    ffn_in, ffn_in_bias, ffn_out, ffn_out_bias,
):
    order = Order()
    here = lax.axis_index("tensor")
    width = src_embed.shape[2]
    local = attn_in.shape[3]
    hidden_width = ffn_in.shape[2]
    source_own = src_embed.reshape(-1, width)
    target_own = tgt_embed.reshape(-1, width)
    sources = 2 * source_own.shape[0]
    targets = 2 * target_own.shape[0]
    enc_own = enc_cot.reshape(-1, width)
    target_other = swap(target_own)
    source_other = swap(source_own)
    loaded = [
        source_own, target_own, dec_cot.reshape(-1, width), loss_mask, src_mask, tgt_mask, enc_own,
        norm_gain, norm_bias, attn_out_bias, ffn_out_bias, attn_in_bias, ffn_in_bias,
    ]
    source_near, target_near, dec_cot_near, loss_near, src_mask_near, tgt_mask_near, enc_own, *small_near = order.call(
        load_body, [jax.ShapeDtypeStruct(a.shape, a.dtype) for a in loaded],
        [Place(a) for a in loaded], scratch=[pltpu.SemaphoreType.DMA((len(loaded),))],
    )
    params = Params(*small_near)
    core = lax.axis_index("dp").astype(jnp.int32).reshape(1)
    here = here.astype(jnp.int32).reshape(1)

    def first(body, own, other, norm, layer, mask, more_ins, more_outs):
        count = 2 * own.shape[0]
        narrow = shape(count, local, BF16)
        return order.call(
            functools.partial(body, norm, layer),
            [
                shape(count, width, BF16), narrow, narrow, narrow,
                shape(local, count, BF16), shape(8, count, F32),
                shape(count, width, F32), shape(count, width, BF16), shape(count, 1, F32),
                *more_outs,
            ],
            [own, other, params, Weight(attn_in, layer), Weight(attn_out, layer), mask, here, *more_ins],
            microseconds=LONG,
            scratch=[pltpu.VMEM((count, local), BF16)],
        )

    def feed(before, recv, norm, layer, last):
        count = before.shape[0]
        sent = count // 2 if last else count
        return order.call(
            functools.partial(feed_body, norm, layer, last),
            [
                shape(count, width, F32), shape(count, width, BF16),
                shape(count, hidden_width, BF16), shape(count, hidden_width, BF16),
                shape(sent, width, F32), shape(sent, width, BF16),
            ],
            [before, recv, params, Weight(ffn_in, layer), Weight(ffn_out, layer)],
            microseconds=LONG,
        )

    h0, q0, k0, v0, turned0, log0, base0, send0, source_keys = first(
        enc_first_body, source_near, source_other, 0, 0, src_mask_near, [core], []
    )
    (
        h2, q1, k1, v1, turned1, log1, base1, send1, target_keys,
        target_queries, dec_own, dec_send,
    ) = first(
        dec_first_body, target_near, target_other, 2, 1, tgt_mask_near,
        [dec_cot_near, loss_near, objective, core],
        [shape(1, targets, F32), shape(targets // 2, width, F32), shape(targets // 2, width, BF16)],
    )
    recv1 = swap(send1)
    dec_other = swap(dec_send)
    recv0 = swap(send0)
    x1, h1, f0, slope0, base2, send2 = feed(base0, recv0, 1, 0, False)
    recv2 = swap(send2)
    narrow = shape(sources, local, BF16)
    memory, k2, v2, encoded = order.call(
        functools.partial(memory_body, 2),
        [shape(sources, width, BF16), narrow, narrow, shape(sources // 2, width, BF16)],
        [base2, recv2, params, Weight(attn_in, 2)], microseconds=3, leave=[3],
    )
    x3, h3, q2, turned2, log2, base3, send3 = order.call(
        functools.partial(cross_attention_body, 3, 2),
        [
            shape(targets, width, F32), shape(targets, width, BF16),
            shape(targets, local, BF16), shape(local, targets, BF16), shape(8, targets, F32),
            shape(targets, width, F32), shape(targets, width, BF16),
        ],
        [
            base1, recv1, params, Weight(attn_in, 2), Weight(attn_out, 2), k2, v2, source_keys,
        ],
        microseconds=5,
        scratch=[pltpu.VMEM((targets, local), BF16)],
    )
    recv3 = swap(send3)
    x4, h4, f1, slope1, base4, send4 = feed(base3, recv3, 4, 1, True)

    def feed_back(body, layer, *ins):
        count = ins[-1].shape[0]
        return order.call(
            body,
            [
                shape(count, width, F32), shape(count, width, BF16),
                shape(count, hidden_width, BF16),
                shape(count, width, F32), shape(count, width, BF16),
            ],
            [*ins[:-1], Weight(ffn_in, layer), Weight(ffn_out, layer), ins[-1]],
            microseconds=LONG,
        )

    def attention_back(cross, causal, g, dh, recv, x, norm, layer, q, k, v, log, key_at, *more):
        count = q.shape[0]
        keys = k.shape[0]
        outs = [
            shape(count, width, F32), shape(count, width, BF16),
            shape(count, local, BF16), shape(keys, local, BF16), shape(keys, local, BF16),
        ]
        if cross:
            outs += [
                shape(count, width, F32), shape(count, width, BF16),
                shape(keys, width, F32), shape(keys, width, BF16),
            ]
        else:
            outs += [shape(count // 2, width, F32), shape(count // 2, width, BF16)]
        outs += [shape(3, width, F32)]
        return order.call(
            functools.partial(attention_back_body, norm, cross, causal), outs,
            [
                g, dh, recv, x, params, Weight(attn_in, layer), Weight(attn_out, layer),
                q, k, v, log, key_at, *more,
            ],
            microseconds=LONG,
            scratch=[pltpu.VMEM((count, local), BF16), pltpu.VMEM((local, count), F32)],
        )

    def feed_weights(layer, h, du, f, low):
        out = shape(2 * width, width, BF16)
        send, keep, sums, hidden_sums = order.call(
            feed_weights_body, [out, out, shape(1, width, F32), shape(1, hidden_width, F32)],
            [h, du, f, low, core], microseconds=1 if layer == 0 else LONG,
        )
        received = across(send, 1)
        groups = [("in", layer, width), ("out", layer, width)]
        return Total(order, core, [(groups, keep, received, 0)]), sums, hidden_sums

    def attention_weights(layer, h, mem, dq, dk, dv, turned, low, *later):
        out = shape(width, width, BF16)
        send, keep, sums, *passed = order.call(
            attention_weights_body,
            [out, out, shape(1, width, F32), *[shape(*value.shape, BF16) for value in later]],
            [h, mem, dq, dk, dv, turned, low, core, *later], microseconds=1,
        )
        total = Total(order, core, [([("attention", layer, width)], keep, across(send, 1), 0)])
        return total, sums, *passed

    def last_norm(g, dh, recv, own, norm):
        rows = own.shape[0]
        return order.call(
            functools.partial(last_norm_body, norm),
            [jax.ShapeDtypeStruct((rows, 1, width), F32), shape(2, width, F32)],
            [g, dh, recv, own, params], leave=[0],
        )

    shapes = (ffn_in.shape, ffn_out.shape, attn_in.shape, attn_out.shape)
    stacks = {"shapes": dict(zip(NAMES, shapes))}
    g4, low4, du1, dh4, dh4_send = feed_back(
        dec_feed_back_body, 1, dec_own, dec_other, slope1
    )
    dh4_recv = swap(dh4_send)
    feed1, two1, one1 = feed_weights(1, h4, du1, f1, low4)
    feed1.next()
    g3, low3, dq2, dk2, dv2, dh3, dh3_send, mem_grad, mem_send, sums4 = attention_back(
        True, False, g4, dh4, dh4_recv, x4, 4, 2, q2, k2, v2, log2, source_keys, enc_own, objective
    )
    mem_recv = swap(mem_send)
    cross, bias2, dh3_later = attention_weights(
        2, h3, memory, dq2, dk2, dv2, turned2, low3, dh3_send
    )
    dh3_recv = swap(dh3_later)
    feed1.next(LONG)
    cross.next()
    g1, low1, du0, dh1, dh1_send = feed_back(
        enc_feed_back_body, 0, enc_own, objective, mem_grad, mem_recv, slope0
    )
    dh1_recv = swap(dh1_send)
    feed0, two0, one0 = feed_weights(0, h1, du0, f0, low1)
    cross.next()
    g2, low2, dq1, dk1, dv1, dh2, dh2_send, sums3 = attention_back(
        False, True, g3, dh3, dh3_recv, x3, 3, 1, q1, k1, v1, log1, target_keys, target_queries
    )
    dh2_recv = swap(dh2_send)
    first1, bias1 = attention_weights(1, h2, h2, dq1, dk1, dv1, turned1, low2)
    feed0.next()
    early = feed1.merge(cross)
    early.next()
    g0, low0, dq0, dk0, dv0, dh0, dh0_send, sums1 = attention_back(
        False, False, g1, dh1, dh1_recv, x1, 1, 0, q0, k0, v0, log0, source_keys
    )
    dh0_recv = swap(dh0_send)
    first0, bias0 = attention_weights(0, h0, h0, dq0, dk0, dv0, turned0, low0)
    feed0.next(TAIL)
    early = Gathered(early, stacks, LONG)
    late = first1.merge(first0)
    late.next(TAIL)
    source_grad, sums0 = last_norm(g0, dh0, dh0_recv, source_near, 0)
    target_grad, sums2 = last_norm(g2, dh2, dh2_recv, target_near, 2)
    small = SmallTotal(
        order, core,
        [
            norm_gain.shape, norm_bias.shape, attn_out_bias.shape, ffn_out_bias.shape,
            attn_in_bias.shape, ffn_in_bias.shape,
        ],
        [sums0, sums1, sums2, sums3, sums4, two0, two1, bias0, bias1, bias2, one0, one1],
    )
    feed0.next(TAIL)
    early.next()
    late.next(TAIL)
    small.next()
    feed0 = Gathered(feed0, stacks)
    early.next()
    feed0.next()
    late.next(TAIL)
    small.next()
    feed0.next()
    late = Gathered(late, stacks)
    late.next()
    small.next()
    early.next()
    late.next()
    early.next()
    small.next()
    feed0.next()
    feed0.next()
    decoded_other = swap(send4)
    (decoded,) = order.call(
        decoded_body, [shape(targets // 2, width, BF16)], [base4, decoded_other], leave=[0]
    )
    small.next()
    late.next()
    late.next()
    for unused in range(dp_bits() + 4):
        for group in (early, feed0, late, small):
            group.next()
    gains, offsets, out_biases, two_biases, in_biases, one_biases = small.results
    return (
        encoded[:, None],
        decoded[:, None],
        source_grad,
        target_grad,
        gains,
        offsets,
        stacks["attn_in"],
        in_biases,
        stacks["attn_out"],
        out_biases,
        stacks["ffn_in"],
        one_biases,
        stacks["ffn_out"],
        two_biases,
    )


def solution(mesh):
    tokens = P("tensor", "dp", None)
    return jax.shard_map(
        on_device,
        mesh=mesh,
        in_specs=(
            tokens, tokens, P("dp", None), P("dp", None), P("dp"), P("dp", "tensor"),
            tokens, tokens, P(), P(),
            P(None, None, None, "tensor"), P(None, None, "tensor"), P(None, "tensor", None), P(),
            P(None, None, "tensor"), P(None, "tensor"), P(None, "tensor", None), P(),
        ),
        out_specs=(
            tokens, tokens, tokens, tokens, P(), P(),
            P(None, None, None, "tensor"), P(None, None, "tensor"), P(None, "tensor", None), P(),
            P(None, None, "tensor"), P(None, "tensor"), P(None, "tensor", None), P(),
        ),
        check_vma=False,
    )
```

```python
import functools

import jax
import jax.numpy as jnp
from jax import lax
from jax.experimental import pallas as pl
from jax.experimental.pallas import tpu as pltpu
from jax.sharding import PartitionSpec as P

HEAD = 64
PAIR = 2 * HEAD
EPSILON = 1e-05
MASKED_SCORE = -1000000000.0
FAR = 1e9
ROOT = 0.7978845608028654
CUBIC = 0.044715
BF16 = jnp.bfloat16
F32 = jnp.float32
VMEM_LIMIT = 18 * 1024 * 1024
BYTES = 3690000
NN = ((1,), (0,))
NT = ((1,), (1,))
TN = ((0,), (0,))
LARGE = 1 << 20
LONG = 40
STEP = 0.2
TAIL = 3
SLOTS = 4
NAMES = ("ffn_in", "ffn_out", "attn_in", "attn_out")
TOKEN = jax.ShapeDtypeStruct((8, 128), F32)


def dot(left, right, contract):
    return lax.dot_general(left, right, (contract, ((), ())), preferred_element_type=F32)


def shape(rows, columns, dtype):
    return jax.ShapeDtypeStruct((rows, columns), dtype)


NEAR = pl.BlockSpec(memory_space=pltpu.VMEM)
AWAY = pl.BlockSpec(memory_space=pl.ANY)
NUMBER = pl.BlockSpec(memory_space=pltpu.SMEM)


class Weight:
    def __init__(self, stack, layer):
        self.stack = stack
        self.layer = layer


class Place:
    def __init__(self, array):
        self.array = array


class Params:
    def __init__(self, *arrays):
        self.arrays = arrays


class Fetch:
    def __init__(self, source, buffer, semaphore):
        self.copy = pltpu.make_async_copy(source, buffer, semaphore)
        self.copy.start()
        self.buffer = buffer
        self.arrived = False

    def here(self):
        if not self.arrived:
            self.copy.wait()
            self.arrived = True
        return self.buffer


class Order:
    def __init__(self):
        self.token = None

    def call(
        self, body, outs, ins, microseconds=0.5, scratch=(), leave=(), away=(), aliases={},
        limit=VMEM_LIMIT,
    ):
        tokens = [] if self.token is None else [self.token]
        specs, args, weights, groups = [], [], [], []
        for value in ins:
            if isinstance(value, Params):
                groups.append(len(args))
                for array in value.arrays:
                    specs.append(NEAR)
                    args.append(pltpu.with_memory_space_constraint(array, pltpu.VMEM))
            elif isinstance(value, Place):
                specs.append(AWAY)
                args.append(pltpu.with_memory_space_constraint(value.array, pltpu.HBM))
            elif isinstance(value, Weight):
                weights.append((len(args), value))
                specs.append(AWAY)
                args.append(pltpu.with_memory_space_constraint(value.stack, pltpu.HBM))
            elif value.dtype == jnp.int32 and value.shape == (1,):
                specs.append(NUMBER)
                args.append(value)
            else:
                specs.append(NEAR)
                args.append(pltpu.with_memory_space_constraint(value, pltpu.VMEM))

        def wrapped(*refs):
            in_refs = list(refs[: len(args)])
            refs = refs[len(args) + len(tokens) :]
            out_refs = refs[: len(outs)]
            refs = refs[len(outs) + 1 :]
            if weights:
                semaphores = refs[-1]
                for i, (at, weight) in enumerate(weights):
                    in_refs[at] = Fetch(in_refs[at].at[weight.layer], refs[i], semaphores.at[i])
            for at in reversed(groups):
                in_refs[at : at + 6] = [in_refs[at : at + 6]]
            body(*in_refs, *out_refs, *refs[len(weights) : len(weights) + len(scratch)])

        buffers = [pltpu.VMEM(w.stack.shape[1:], w.stack.dtype) for unused, w in weights]
        semaphores = [pltpu.SemaphoreType.DMA((len(weights),))] if weights else []
        results = pl.pallas_call(
            wrapped,
            out_shape=[
                *[
                    o if i in leave or i in away else pltpu.VMEM(o.shape, o.dtype)
                    for i, o in enumerate(outs)
                ],
                TOKEN,
            ],
            in_specs=specs + [AWAY] * len(tokens),
            out_specs=[AWAY if i in away else NEAR for i in range(len(outs))] + [AWAY],
            scratch_shapes=[*buffers, *scratch, *semaphores],
            input_output_aliases=aliases,
            compiler_params=pltpu.CompilerParams(vmem_limit_bytes=limit),
            cost_estimate=pl.CostEstimate(
                flops=int(microseconds * 1.15e9), transcendentals=0, bytes_accessed=int(microseconds * BYTES)
            ),
        )(*args, *tokens)
        self.token = results[-1]
        return results[:-1]


def norm_parts(inputs):
    centre = inputs - jnp.mean(inputs, axis=-1, keepdims=True)
    inverse = lax.rsqrt(jnp.mean(centre * centre, axis=-1, keepdims=True) + EPSILON)
    return centre * inverse, inverse


def norm_back(gradient, normed, inverse, gain):
    scaled = gradient * gain
    mean_plain = jnp.mean(scaled, axis=-1, keepdims=True)
    mean_normed = jnp.mean(scaled * normed, axis=-1, keepdims=True)
    return inverse * (scaled - mean_plain - normed * mean_normed)


def column_sum(values):
    return jnp.sum(values.astype(F32), axis=0, keepdims=True)


def halves(count):
    half = count // 2
    return ((0, half), (half, 0))


def lane_half(which, rows):
    lanes = lax.broadcasted_iota(jnp.int32, (rows, PAIR), 1)
    return (lanes >= HEAD) if which else (lanes < HEAD)


def only_head(which, values):
    return jnp.where(lane_half(which, values.shape[0]), values, jnp.zeros_like(values))


def key_scores(key_pair, query_pair, which, key_at, query_at):
    scores = dot(only_head(which, key_pair), query_pair, NT)
    return jnp.where(key_at <= query_at, scores, MASKED_SCORE)


def attend(q_ref, k_ref, v_ref, key_at, query_at_ref, turned_ref, o_ref, log_ref):
    queries, local = q_ref.shape
    block = min(queries, 256)
    for pair in range(local // PAIR):
        columns = pl.ds(pair * PAIR, PAIR)
        key_pair = k_ref[:, columns]
        value_turned = v_ref[:, columns].astype(F32).T.astype(BF16)
        for start in range(0, queries, block):
            rows = pl.ds(start, block)
            query_pair = q_ref[rows, columns]
            query_at = 0.0 if query_at_ref is None else query_at_ref[:, rows]
            for which in range(2):
                head = 2 * pair + which
                scores = key_scores(key_pair, query_pair, which, key_at, query_at)
                top = jnp.max(scores, axis=0, keepdims=True)
                exponent = jnp.exp(scores - top)
                total = jnp.sum(exponent, axis=0, keepdims=True)
                weights = (exponent * (1.0 / total)).astype(BF16)
                log_ref[pl.ds(head, 1), rows] = top + jnp.log(total)
                mixed = dot(value_turned[which * HEAD : (which + 1) * HEAD], weights, NN)
                turned_ref[pl.ds(head * HEAD, HEAD), rows] = mixed.astype(BF16)
    o_ref[...] = turned_ref[...].astype(F32).T.astype(BF16)


def in_bias_rows(params, layer):
    return params[4][layer, 0:1], params[4][layer, 1:2]


def row_of(ref, index):
    return ref[index : index + 1]


def normalised(value, params, norm):
    normed, unused = norm_parts(value)
    return (normed * row_of(params[0], norm) + row_of(params[1], norm)).astype(BF16)


def column(row):
    return jnp.broadcast_to(row, (8, row.shape[1])).T[:, 0:1]


def own_first(row, here):
    half = row.shape[1] // 2
    return jnp.where(here == 0, row, jnp.concatenate([row[:, half:], row[:, :half]], axis=1))


def scaled_queries(hidden, w_in, bias):
    return ((dot(hidden, w_in[0], NN) + bias).astype(BF16) * HEAD ** (-0.5)).astype(BF16)


def load_body(*refs):
    count = len(refs) // 2
    copies = [
        pltpu.make_async_copy(refs[i], refs[count + i], refs[-1].at[i]) for i in range(count)
    ]
    for copy in copies:
        copy.start()
    for copy in copies:
        copy.wait()


def first_attention(norm, layer, own_ref, other_ref, params, w_in, w_out, key_at, query_at_ref, *refs):
    h_ref, q_ref, k_ref, v_ref, turned_ref, log_ref, base_ref, send_ref, o_ref = refs
    half = own_ref.shape[0]
    query_bias, value_bias = in_bias_rows(params, layer)
    for part, source in enumerate((own_ref, other_ref)):
        rows = pl.ds(part * half, half)
        hidden = normalised(source[...].astype(F32), params, norm)
        h_ref[rows] = hidden
        w = w_in.here()
        q_ref[rows] = scaled_queries(hidden, w, query_bias)
        k_ref[rows] = dot(hidden, w[1], NN).astype(BF16)
        v_ref[rows] = (dot(hidden, w[2], NN) + value_bias).astype(BF16)
    attend(q_ref, k_ref, v_ref, key_at, query_at_ref, turned_ref, o_ref, log_ref)
    w = w_out.here()
    for part, source in enumerate((own_ref, other_ref)):
        rows = pl.ds(part * half, half)
        partial = dot(o_ref[rows], w[...], NN)
        send_ref[rows] = partial.astype(BF16)
        base_ref[rows] = source[...].astype(F32) + row_of(params[2], layer) + partial


def enc_first_body(norm, layer, own_ref, other_ref, params, w_in, w_out, mask_ref, here_ref, place_ref, *refs):
    outs, key_at_ref, o_ref = refs[:-2], refs[-2], refs[-1]
    row = own_first(jnp.where(mask_ref[...] == 1, 0.0, FAR), here_ref[0])
    key_at = column(row)
    key_at_ref[...] = key_at
    first_attention(norm, layer, own_ref, other_ref, params, w_in, w_out, key_at, None, *outs, o_ref)


def dec_first_body(
    norm, layer, own_ref, other_ref, params, w_in, w_out, mask_ref, here_ref,
    cot_ref, loss_ref, objective_ref, place_ref, *refs
):
    outs, (key_at_ref, query_at_ref, gradient_ref, gradient_send_ref, o_ref) = refs[:-5], refs[-5:]
    count = mask_ref.shape[1]
    position = own_first(
        lax.broadcasted_iota(jnp.int32, (1, count), 1).astype(F32), here_ref[0]
    )
    row = jnp.where(own_first(mask_ref[...].astype(F32), here_ref[0]) == 1.0, position, FAR)
    key_at = column(row)
    key_at_ref[...] = key_at
    query_at_ref[...] = position
    flag = objective_ref[0].astype(F32)
    weight = column(0.25 + 0.75 * loss_ref[...].astype(F32)) * (0.5 + 0.5 * flag)
    gradient = cot_ref[...].astype(F32) * weight
    gradient_ref[...] = gradient
    gradient_send_ref[...] = gradient.astype(BF16)
    first_attention(
        norm, layer, own_ref, other_ref, params, w_in, w_out, key_at, query_at_ref, *outs, o_ref
    )


def cross_attention_body(
    norm, layer, before_ref, recv_ref, params, w_in, w_out, k_ref, v_ref, key_at_ref,
    x_ref, h_ref, q_ref, turned_ref, log_ref, base_ref, send_ref, o_ref,
):
    count = x_ref.shape[0]
    half = count // 2
    query_bias, unused = in_bias_rows(params, layer)
    for mine, theirs in halves(count):
        rows = pl.ds(mine, half)
        value = before_ref[rows] + recv_ref[pl.ds(theirs, half)].astype(F32)
        x_ref[rows] = value
        hidden = normalised(value, params, norm)
        h_ref[rows] = hidden
        q_ref[rows] = scaled_queries(hidden, w_in.here(), query_bias)
    attend(q_ref, k_ref, v_ref, key_at_ref[...], None, turned_ref, o_ref, log_ref)
    partial = dot(o_ref[...], w_out.here()[...], NN)
    send_ref[...] = partial.astype(BF16)
    base_ref[...] = x_ref[...] + row_of(params[2], layer) + partial


def memory_body(layer, before_ref, recv_ref, params, w_in, mem_ref, k_ref, v_ref, out_ref):
    count = mem_ref.shape[0]
    half = count // 2
    unused, value_bias = in_bias_rows(params, layer)
    for mine, theirs in halves(count):
        rows = pl.ds(mine, half)
        memory = (before_ref[rows] + recv_ref[pl.ds(theirs, half)].astype(F32)).astype(BF16)
        mem_ref[rows] = memory
        if mine == 0:
            out_ref[...] = memory
        w = w_in.here()
        k_ref[rows] = dot(memory, w[1], NN).astype(BF16)
        v_ref[rows] = (dot(memory, w[2], NN) + value_bias).astype(BF16)


def feed_body(
    norm, layer, last, before_ref, recv_ref, params, w_one, w_two,
    x_ref, h_ref, f_ref, slope_ref, base_ref, send_ref,
):
    count = x_ref.shape[0]
    half = count // 2
    for mine, theirs in halves(count):
        rows = pl.ds(mine, half)
        value = before_ref[rows] + recv_ref[pl.ds(theirs, half)].astype(F32)
        x_ref[rows] = value
        hidden = normalised(value, params, norm)
        h_ref[rows] = hidden
        u = dot(hidden, w_one.here()[...], NN) + row_of(params[5], layer)
        square = u * u
        bent = jnp.tanh(u * (ROOT + (ROOT * CUBIC) * square))
        upper = 0.5 + 0.5 * bent
        active = (u * upper).astype(BF16)
        f_ref[rows] = active
        slope = upper + (0.5 * u) * (1.0 - bent * bent) * (ROOT + (3 * ROOT * CUBIC) * square)
        slope_ref[rows] = slope.astype(BF16)
        partial = dot(active, w_two.here()[...], NN)
        if not last:
            send_ref[rows] = partial.astype(BF16)
            base_ref[rows] = value + row_of(params[3], layer) + partial
        elif mine == 0:
            base_ref[...] = value + row_of(params[3], layer) + partial
        else:
            send_ref[...] = partial.astype(BF16)


def feed_back_rows(
    gradient, rows, w_one, w_two, slope_ref, g_ref, low_ref, du_ref, base_ref, send_ref
):
    g_ref[rows] = gradient
    low = gradient.astype(BF16)
    low_ref[rows] = low
    du = (dot(low, w_two.here()[...], NT) * slope_ref[rows].astype(F32)).astype(BF16)
    du_ref[rows] = du
    partial = dot(du, w_one.here()[...], NT)
    send_ref[rows] = partial.astype(BF16)
    base_ref[rows] = partial


def dec_feed_back_body(own_ref, other_ref, w_one, w_two, slope_ref, *outs):
    half = own_ref.shape[0]
    for part, source in enumerate((own_ref, other_ref)):
        feed_back_rows(
            source[...].astype(F32), pl.ds(part * half, half), w_one, w_two, slope_ref, *outs
        )


def source_seed(cot_ref, objective_ref):
    return cot_ref[...].astype(F32) * (1.0 - 0.5 * objective_ref[0].astype(F32))


def enc_feed_back_body(seed_ref, objective_ref, mem_base_ref, recv_ref, w_one, w_two, slope_ref, *outs):
    half = seed_ref.shape[0]
    own, other = pl.ds(0, half), pl.ds(half, half)
    for rows, theirs in ((own, other), (other, own)):
        gradient = mem_base_ref[rows] + recv_ref[theirs].astype(F32)
        if rows is own:
            gradient = gradient + source_seed(seed_ref, objective_ref)
        feed_back_rows(gradient, rows, w_one, w_two, slope_ref, *outs)


def attention_back_body(norm, cross, causal, *refs):
    (g_in_ref, dh_ref, dh_recv_ref, x_ref, params, w_in, w_out, q_ref, k_ref, v_ref, log_ref,
     key_at_ref), refs = refs[:12], refs[12:]
    query_at_ref = seed_ref = mem_base_ref = mem_send_ref = None
    if causal:
        query_at_ref, refs = refs[0], refs[1:]
    if cross:
        (seed_ref, objective_ref), refs = refs[:2], refs[2:]
    (g_ref, low_ref, dq_ref, dk_ref, dv_ref, base_ref, send_ref), refs = refs[:7], refs[7:]
    if cross:
        (mem_base_ref, mem_send_ref), refs = refs[:2], refs[2:]
    sums_ref, do_ref, turned_ref = refs
    gain = row_of(params[0], norm)
    count, local = dq_ref.shape
    half = count // 2
    for part, (mine, theirs) in enumerate(halves(count)):
        rows = pl.ds(mine, half)
        normed, inverse = norm_parts(x_ref[rows])
        dh = dh_ref[rows] + dh_recv_ref[pl.ds(theirs, half)].astype(F32)
        gradient = g_in_ref[rows] + norm_back(dh, normed, inverse, gain)
        g_ref[rows] = gradient
        low = gradient.astype(BF16)
        low_ref[rows] = low
        if part == 0:
            sums_ref[0:1] = column_sum(dh * normed)
            sums_ref[1:2] = column_sum(dh)
            sums_ref[2:3] = column_sum(low)
        do_ref[rows] = dot(low, w_out.here()[...], NT).astype(BF16)
    key_at = key_at_ref[...]
    block = min(count, 256)
    keys = k_ref.shape[0]
    for pair in range(local // PAIR):
        columns = pl.ds(pair * PAIR, PAIR)
        key_pair = k_ref[:, columns]
        key_turned = key_pair.astype(F32).T.astype(BF16)
        value_pair = v_ref[:, columns]
        dk = [None, None]
        dv = [None, None]
        for start in range(0, count, block):
            rows = pl.ds(start, block)
            query_pair = q_ref[rows, columns]
            do_pair = do_ref[rows, columns]
            query_at = 0.0 if query_at_ref is None else query_at_ref[:, rows]
            for which in range(2):
                head = 2 * pair + which
                scores = key_scores(key_pair, query_pair, which, key_at, query_at)
                probs = jnp.exp(scores - log_ref[pl.ds(head, 1), rows])
                prob_grad = dot(only_head(which, value_pair), do_pair, NT)
                product = probs * prob_grad
                inner = jnp.sum(product, axis=0, keepdims=True)
                score_grad = (product - probs * inner).astype(BF16)
                dv_part = dot(probs.astype(BF16), do_pair, NN)
                dk_part = dot(score_grad, query_pair, NN)
                dq_part = dot(key_turned[which * HEAD : (which + 1) * HEAD], score_grad, NN)
                turned_ref[pl.ds(head * HEAD, HEAD), rows] = dq_part * HEAD ** (-0.5)
                dk[which] = dk_part if dk[which] is None else dk[which] + dk_part
                dv[which] = dv_part if dv[which] is None else dv[which] + dv_part
        first = lane_half(0, keys)
        dk_ref[:, columns] = jnp.where(first, dk[0], dk[1]).astype(BF16)
        dv_ref[:, columns] = jnp.where(first, dv[0], dv[1]).astype(BF16)
    dq_ref[...] = turned_ref[...].T.astype(BF16)
    w = w_in.here()
    if cross:
        partial = dot(dk_ref[...], w[1], NT) + dot(dv_ref[...], w[2], NT)
        mem_base_ref[...] = partial
        mem_half = keys // 2
        mem_send_ref[0:mem_half] = (
            partial[0:mem_half] + source_seed(seed_ref, objective_ref)
        ).astype(BF16)
        mem_send_ref[mem_half:] = partial[mem_half:].astype(BF16)
        partial = dot(dq_ref[...], w[0], NT)
        send_ref[...] = partial.astype(BF16)
        base_ref[...] = partial
    else:
        for part in (1, 0):
            rows = pl.ds(part * half, half)
            partial = (
                dot(dq_ref[rows], w[0], NT)
                + dot(dk_ref[rows], w[1], NT)
                + dot(dv_ref[rows], w[2], NT)
            )
            if part == 1:
                send_ref[...] = partial.astype(BF16)
            else:
                base_ref[...] = partial


def last_norm_body(norm, g_ref, dh_ref, recv_ref, x_ref, params, out_ref, sums_ref):
    normed, inverse = norm_parts(x_ref[...].astype(F32))
    dh = dh_ref[...] + recv_ref[...].astype(F32)
    sums_ref[0:1] = column_sum(dh * normed)
    sums_ref[1:2] = column_sum(dh)
    half = out_ref.shape[0]
    result = g_ref[0:half] + norm_back(dh, normed, inverse, row_of(params[0], norm))
    out_ref[...] = result.reshape(out_ref.shape)


def feed_weights_body(h_ref, du_ref, f_ref, low_ref, place_ref, send_ref, keep_ref, sums_ref, hidden_sums_ref):
    bit = bit_of(place_ref, 0)
    width = h_ref.shape[1]
    part = width // 2
    for which, out_ref in ((1 - bit, send_ref), (bit, keep_ref)):
        left = h_ref[:, pl.ds(pl.multiple_of(which * part, 128), part)]
        for side in range(2):
            out_ref[pl.ds(side * part, part)] = dot(
                left, du_ref[:, pl.ds(side * width, width)], TN
            ).astype(BF16)
        left = f_ref[:, pl.ds(pl.multiple_of(which * width, 128), width)]
        out_ref[pl.ds(width, width)] = dot(left, low_ref[...], TN).astype(BF16)
    half = low_ref.shape[0] // 2
    sums_ref[...] = column_sum(low_ref[0:half])
    hidden_sums_ref[...] = column_sum(du_ref[...])


def attention_weights_body(
    h_ref, mem_ref, dq_ref, dk_ref, dv_ref, turned_ref, low_ref, place_ref, *refs
):
    later_ref, refs = (refs[0], refs[1:]) if len(refs) == 5 else (None, refs)
    send_ref, keep_ref, sums_ref = refs[:3]
    if later_ref is not None:
        refs[3][...] = later_ref[...]
    bit = bit_of(place_ref, 0)
    width = h_ref.shape[1]
    part = width // 2
    quarter = width // 4
    left_side = pl.ds(0, part)
    right_side = pl.ds(part, part)
    for which, out_ref in ((1 - bit, send_ref), (bit, keep_ref)):
        columns = pl.ds(pl.multiple_of(which * part, 128), part)
        out_ref[pl.ds(0, part), left_side] = dot(h_ref[:, columns], dq_ref[...], TN).astype(BF16)
        memory = mem_ref[:, columns]
        out_ref[pl.ds(0, part), right_side] = dot(memory, dk_ref[...], TN).astype(BF16)
        values = dot(memory, dv_ref[...], TN).astype(BF16)
        out_ref[pl.ds(part, quarter), left_side] = values[:quarter]
        out_ref[pl.ds(part, quarter), right_side] = values[quarter:]
        rows = pl.ds(pl.multiple_of(which * quarter, 64), quarter)
        out_ref[pl.ds(part + quarter, quarter)] = dot(turned_ref[rows], low_ref[...], NN).astype(BF16)
    sums_ref[:, left_side] = column_sum(dq_ref[...])
    sums_ref[:, right_side] = column_sum(dv_ref[...])


def bit_of(place_ref, step):
    return (place_ref[0] >> step) & 1


def add_body(step, layout, place_ref, *refs):
    send_ref, next_ref = refs[-2:]
    bit = bit_of(place_ref, step)
    for out_ref, which in ((send_ref, 1 - bit), (next_ref, bit)):
        target = 0
        for i, (first, segments) in enumerate(layout):
            keep_ref, received_ref = refs[2 * i], refs[2 * i + 1]
            for rows in segments:
                half = rows // 2
                block = half
                while block % 32 == 0 and block > 128:
                    block //= 2
                for start in range(0, half, block):
                    part = pl.ds(pl.multiple_of(first + which * half + start, 8), block)
                    out_ref[pl.ds(target + start, block)] = (
                        keep_ref[part].astype(F32) + received_ref[part].astype(F32)
                    ).astype(BF16)
                first += rows
                target += half


def last_sum_body(keep_ref, received_ref, out_ref):
    out_ref[...] = (keep_ref[...].astype(F32) + received_ref[...].astype(F32)).astype(BF16)


def join_body(first_ref, second_ref, out_ref):
    rows = first_ref.shape[0]
    out_ref[0:rows] = first_ref[...]
    out_ref[rows:] = second_ref[...]


def put_body(groups, masks, bits, old, place_ref, block_ref, *refs):
    refs = refs[old:]
    outs = dict(zip(NAMES, refs[:4]))
    wide_ref, semaphores = refs[4:]
    width = block_ref.shape[1]
    part, quarter = width // 2, width // 4
    slots = wide_ref.shape[0]
    flying = []

    def copy(slot, side, rows, target):
        source = wide_ref.at[slot, pl.ds(0, rows), pl.ds(side * part, part)]
        return pltpu.make_async_copy(source, target, semaphores.at[slot, side])

    def wait(slot, rows):
        for side in range(2):
            target = outs["ffn_out"].at[0, pl.ds(0, rows), pl.ds(0, part)]
            copy(slot, side, rows, target).wait()

    at = 0
    for mask in masks:
        device = place_ref[0] ^ mask
        upper = device & 1
        for kind, layer, rows in groups:
            slot = len(flying) % slots
            if len(flying) >= slots:
                wait(*flying[-slots])
            flying.append((slot, rows))
            wide_ref[slot, pl.ds(0, rows)] = block_ref[pl.ds(at, rows)].astype(F32)
            at += rows
            inner = 0
            for bit in range(1, bits):
                inner = inner + ((device >> bit) & 1) * (rows << (bits - 1 - bit))

            def send(side, target):
                copy(slot, side, rows, target).start()

            if kind == "in":
                row = pl.multiple_of(upper * part + lax.rem(inner, part), 8)
                column = lax.div(inner, part) * width
                for side in range(2):
                    columns = pl.ds(pl.multiple_of(column + side * part, 128), part)
                    send(side, outs["ffn_in"].at[layer, pl.ds(row, rows), columns])
            elif kind == "out":
                row = pl.multiple_of(upper * width + inner, 8)
                for side in range(2):
                    columns = pl.ds(side * part, part)
                    send(side, outs["ffn_out"].at[layer, pl.ds(row, rows), columns])
            else:

                @pl.when(inner < part)
                def query_and_key():
                    row = pl.multiple_of(upper * part + inner, 8)
                    for side in range(2):
                        send(side, outs["attn_in"].at[layer, side, pl.ds(row, rows)])

                @pl.when((inner >= part) & (inner < part + quarter))
                def value():
                    row = upper * part + inner - part
                    for side in range(2):
                        target = pl.ds(pl.multiple_of(row + side * quarter, 8), rows)
                        send(side, outs["attn_in"].at[layer, 2, target])

                @pl.when(inner >= part + quarter)
                def output():
                    row = pl.multiple_of(upper * quarter + inner - part - quarter, 8)
                    for side in range(2):
                        columns = pl.ds(side * part, part)
                        send(side, outs["attn_out"].at[layer, pl.ds(row, rows), columns])

    for slot, rows in flying[-slots:]:
        wait(slot, rows)


def pack_body(*refs):
    norm_refs, out_refs, rows_refs, wide_refs = refs[:5], refs[5:7], refs[7:10], refs[10:12]
    shared_ref, apart_ref = refs[12:]
    shared_ref[...] = jnp.zeros_like(shared_ref)
    apart_ref[...] = jnp.zeros_like(apart_ref)
    for i, ref in enumerate(norm_refs):
        shared_ref[i : i + 1] = ref[0:1]
        shared_ref[5 + i : 6 + i] = ref[1:2]
    for i, source in enumerate((1, 3, 4)):
        shared_ref[10 + i : 11 + i] = norm_refs[source][2:3]
    for i, ref in enumerate(out_refs):
        shared_ref[13 + i : 14 + i] = ref[...]
    for i, ref in enumerate(rows_refs):
        apart_ref[i : i + 1] = ref[...]
    width = shared_ref.shape[1]
    for i, ref in enumerate(wide_refs):
        for side in range(2):
            apart_ref[3 + 2 * i + side : 4 + 2 * i + side] = ref[:, side * width : (side + 1) * width]


def pair_small_body(shared_ref, received_ref, apart_ref, out_ref):
    out_ref[0:16] = shared_ref[...] + received_ref[...]
    out_ref[16:24] = apart_ref[...]


def add_small_body(first_ref, second_ref, out_ref):
    out_ref[...] = first_ref[...] + second_ref[...]


def last_small_body(first_ref, second_ref, *outs):
    total = first_ref[...] + second_ref[...]
    gain_ref, offset_ref, out_bias_ref, two_ref, in_ref, one_ref = outs
    gain_ref[...] = total[0:5]
    offset_ref[...] = total[5:10]
    out_bias_ref[...] = total[10:13]
    two_ref[...] = total[13:15]
    width = total.shape[1]
    part = width // 2
    for i in range(3):
        for side in range(2):
            in_ref[i, side : side + 1] = total[16 + i : 17 + i, side * part : (side + 1) * part]
    for i in range(2):
        for side in range(2):
            row = 19 + 2 * i + side
            one_ref[i : i + 1, side * width : (side + 1) * width] = total[row : row + 1]


def decoded_body(base_ref, received_ref, out_ref):
    out_ref[...] = (base_ref[...] + received_ref[...].astype(F32)).astype(BF16)


def pass_body(value_ref, unused_ref, out_ref):
    out_ref[...] = value_ref[...]


def swap(values):
    return lax.ppermute(values, "tensor", [(0, 1), (1, 0)])


def across(values, stride):
    count = lax.axis_size("dp")
    return lax.ppermute(values, "dp", [(i, i ^ stride) for i in range(count)])


def dp_bits():
    return lax.axis_size("dp").bit_length() - 1


class Total:
    def __init__(self, order, place, parts, step=1):
        self.order = order
        self.place = place
        self.parts = parts
        self.step = step

    def merge(self, *others):
        assert all(self.step == other.step for other in others)
        return Total(
            self.order, self.place, self.parts + sum((other.parts for other in others), []), self.step
        )

    def finish(self, microseconds=0.2):
        while self.step < dp_bits():
            self.next()
        ((self.groups, keep, received, unused),) = self.parts
        (self.shard,) = self.order.call(
            last_sum_body, [shape(*keep.shape, BF16)], [keep, received], microseconds=microseconds
        )

    def next(self, microseconds=0.5):
        if self.step == dp_bits():
            return
        width = self.parts[0][1].shape[1]
        layout = [
            (first, [rows for unused, unused, rows in groups])
            for groups, unused, unused, first in self.parts
        ]
        rows = sum(sum(segments) for unused, segments in layout) // 2
        send, keep = self.order.call(
            functools.partial(add_body, self.step, layout), [shape(rows, width, BF16)] * 2,
            [self.place, *[value for unused, *pair, unused in self.parts for value in pair]],
            microseconds=microseconds,
        )
        groups = [
            (kind, layer, rows // 2)
            for members, *unused in self.parts
            for kind, layer, rows in members
        ]
        self.parts = [(groups, keep, across(send, 1 << self.step), 0)]
        self.step += 1


class Gathered:
    def __init__(self, total, stacks, microseconds=TAIL):
        self.order = total.order
        self.place = total.place
        self.stacks = stacks
        total.finish(microseconds)
        self.groups = total.groups
        self.stages = self.run(total.shard)
        self.next()

    def next(self):
        next(self.stages, None)

    def run(self, block):
        order = self.order
        masks = [0]
        for bit in range(dp_bits() - 1, -1, -1):
            received = across(block, 1 << bit)
            yield
            if bit:
                (block,) = order.call(
                    join_body, [shape(2 * block.shape[0], block.shape[1], BF16)], [block, received],
                    microseconds=TAIL,
                )
                masks += [mask ^ (1 << bit) for mask in masks]
        self.put(block, masks)
        yield
        self.put(received, [mask ^ 1 for mask in masks])
        yield

    def put(self, block, masks):
        stacks = self.stacks
        old = [stacks[name] for name in NAMES] if NAMES[0] in stacks else []
        rows = max(rows for unused, unused, rows in self.groups)
        results = self.order.call(
            functools.partial(put_body, self.groups, masks, dp_bits(), len(old)),
            [jax.ShapeDtypeStruct(stacks["shapes"][name], F32) for name in NAMES],
            [self.place, block, *[Place(value) for value in old]],
            aliases={2 + i: i for i in range(len(old))},
            away=range(4),
            microseconds=TAIL,
            scratch=[
                pltpu.VMEM((6, rows, block.shape[1]), F32),
                pltpu.SemaphoreType.DMA((6, 2)),
            ],
        )
        stacks.update(zip(NAMES, results))


class SmallTotal:
    def __init__(self, order, place, shapes, ins):
        self.order = order
        self.place = place
        self.shapes = shapes
        self.results = None
        width = ins[0].shape[1]
        self.shared, self.apart = order.call(
            pack_body, [shape(16, width, F32), shape(8, width, F32)], ins
        )
        self.received = swap(self.shared)
        self.stages = self.run()

    def next(self):
        next(self.stages, None)

    def run(self):
        order, bits = self.order, dp_bits()
        whole = shape(24, self.shared.shape[1], F32)
        (value,) = order.call(pair_small_body, [whole], [self.shared, self.received, self.apart], microseconds=TAIL)
        for bit in range(bits):
            received = across(value, 1 << bit)
            yield
            if bit + 1 < bits:
                (value,) = order.call(add_small_body, [whole], [value, received], microseconds=TAIL)
        self.results = order.call(
            last_small_body, [jax.ShapeDtypeStruct(dims, F32) for dims in self.shapes],
            [value, received], leave=range(6),
        )
        yield


def on_device(
    src_embed, tgt_embed, src_mask, tgt_mask, objective, loss_mask, enc_cot, dec_cot,
    norm_gain, norm_bias, attn_in, attn_in_bias, attn_out, attn_out_bias,
    ffn_in, ffn_in_bias, ffn_out, ffn_out_bias,
):
    order = Order()
    here = lax.axis_index("tensor")
    width = src_embed.shape[2]
    local = attn_in.shape[3]
    hidden_width = ffn_in.shape[2]
    source_own = src_embed.reshape(-1, width)
    target_own = tgt_embed.reshape(-1, width)
    sources = 2 * source_own.shape[0]
    targets = 2 * target_own.shape[0]
    enc_own = enc_cot.reshape(-1, width)
    target_other = swap(target_own)
    source_other = swap(source_own)
    loaded = [
        source_own, target_own, dec_cot.reshape(-1, width), loss_mask, src_mask, tgt_mask, enc_own,
        norm_gain, norm_bias, attn_out_bias, ffn_out_bias, attn_in_bias, ffn_in_bias,
    ]
    source_near, target_near, dec_cot_near, loss_near, src_mask_near, tgt_mask_near, enc_own, *small_near = order.call(
        load_body, [jax.ShapeDtypeStruct(a.shape, a.dtype) for a in loaded],
        [Place(a) for a in loaded], scratch=[pltpu.SemaphoreType.DMA((len(loaded),))],
    )
    params = Params(*small_near)
    core = lax.axis_index("dp").astype(jnp.int32).reshape(1)
    here = here.astype(jnp.int32).reshape(1)

    def first(body, own, other, norm, layer, mask, more_ins, more_outs):
        count = 2 * own.shape[0]
        narrow = shape(count, local, BF16)
        return order.call(
            functools.partial(body, norm, layer),
            [
                shape(count, width, BF16), narrow, narrow, narrow,
                shape(local, count, BF16), shape(8, count, F32),
                shape(count, width, F32), shape(count, width, BF16), shape(count, 1, F32),
                *more_outs,
            ],
            [own, other, params, Weight(attn_in, layer), Weight(attn_out, layer), mask, here, *more_ins],
            microseconds=LONG,
            scratch=[pltpu.VMEM((count, local), BF16)],
        )

    def feed(before, recv, norm, layer, last):
        count = before.shape[0]
        sent = count // 2 if last else count
        return order.call(
            functools.partial(feed_body, norm, layer, last),
            [
                shape(count, width, F32), shape(count, width, BF16),
                shape(count, hidden_width, BF16), shape(count, hidden_width, BF16),
                shape(sent, width, F32), shape(sent, width, BF16),
            ],
            [before, recv, params, Weight(ffn_in, layer), Weight(ffn_out, layer)],
            microseconds=LONG,
        )

    h0, q0, k0, v0, turned0, log0, base0, send0, source_keys = first(
        enc_first_body, source_near, source_other, 0, 0, src_mask_near, [core], []
    )
    (
        h2, q1, k1, v1, turned1, log1, base1, send1, target_keys,
        target_queries, dec_own, dec_send,
    ) = first(
        dec_first_body, target_near, target_other, 2, 1, tgt_mask_near,
        [dec_cot_near, loss_near, objective, core],
        [shape(1, targets, F32), shape(targets // 2, width, F32), shape(targets // 2, width, BF16)],
    )
    recv1 = swap(send1)
    dec_other = swap(dec_send)
    recv0 = swap(send0)
    x1, h1, f0, slope0, base2, send2 = feed(base0, recv0, 1, 0, False)
    recv2 = swap(send2)
    narrow = shape(sources, local, BF16)
    memory, k2, v2, encoded = order.call(
        functools.partial(memory_body, 2),
        [shape(sources, width, BF16), narrow, narrow, shape(sources // 2, width, BF16)],
        [base2, recv2, params, Weight(attn_in, 2)], microseconds=3, leave=[3],
    )
    x3, h3, q2, turned2, log2, base3, send3 = order.call(
        functools.partial(cross_attention_body, 3, 2),
        [
            shape(targets, width, F32), shape(targets, width, BF16),
            shape(targets, local, BF16), shape(local, targets, BF16), shape(8, targets, F32),
            shape(targets, width, F32), shape(targets, width, BF16),
        ],
        [
            base1, recv1, params, Weight(attn_in, 2), Weight(attn_out, 2), k2, v2, source_keys,
        ],
        microseconds=5,
        scratch=[pltpu.VMEM((targets, local), BF16)],
    )
    recv3 = swap(send3)
    x4, h4, f1, slope1, base4, send4 = feed(base3, recv3, 4, 1, True)

    def feed_back(body, layer, *ins):
        count = ins[-1].shape[0]
        return order.call(
            body,
            [
                shape(count, width, F32), shape(count, width, BF16),
                shape(count, hidden_width, BF16),
                shape(count, width, F32), shape(count, width, BF16),
            ],
            [*ins[:-1], Weight(ffn_in, layer), Weight(ffn_out, layer), ins[-1]],
            microseconds=LONG,
        )

    def attention_back(cross, causal, g, dh, recv, x, norm, layer, q, k, v, log, key_at, *more):
        count = q.shape[0]
        keys = k.shape[0]
        outs = [
            shape(count, width, F32), shape(count, width, BF16),
            shape(count, local, BF16), shape(keys, local, BF16), shape(keys, local, BF16),
        ]
        if cross:
            outs += [
                shape(count, width, F32), shape(count, width, BF16),
                shape(keys, width, F32), shape(keys, width, BF16),
            ]
        else:
            outs += [shape(count // 2, width, F32), shape(count // 2, width, BF16)]
        outs += [shape(3, width, F32)]
        return order.call(
            functools.partial(attention_back_body, norm, cross, causal), outs,
            [
                g, dh, recv, x, params, Weight(attn_in, layer), Weight(attn_out, layer),
                q, k, v, log, key_at, *more,
            ],
            microseconds=LONG,
            scratch=[pltpu.VMEM((count, local), BF16), pltpu.VMEM((local, count), F32)],
        )

    def feed_weights(layer, h, du, f, low):
        out = shape(2 * width, width, BF16)
        send, keep, sums, hidden_sums = order.call(
            feed_weights_body, [out, out, shape(1, width, F32), shape(1, hidden_width, F32)],
            [h, du, f, low, core], microseconds=2 if layer == 0 else LONG,
        )
        received = across(send, 1)
        groups = [("in", layer, width), ("out", layer, width)]
        return Total(order, core, [(groups, keep, received, 0)]), sums, hidden_sums

    def attention_weights(layer, h, mem, dq, dk, dv, turned, low, *later):
        out = shape(width, width, BF16)
        send, keep, sums, *passed = order.call(
            attention_weights_body,
            [out, out, shape(1, width, F32), *[shape(*value.shape, BF16) for value in later]],
            [h, mem, dq, dk, dv, turned, low, core, *later], microseconds=2,
        )
        total = Total(order, core, [([("attention", layer, width)], keep, across(send, 1), 0)])
        return total, sums, *passed

    def last_norm(g, dh, recv, own, norm):
        rows = own.shape[0]
        return order.call(
            functools.partial(last_norm_body, norm),
            [jax.ShapeDtypeStruct((rows, 1, width), F32), shape(2, width, F32)],
            [g, dh, recv, own, params], leave=[0],
        )

    shapes = (ffn_in.shape, ffn_out.shape, attn_in.shape, attn_out.shape)
    stacks = {"shapes": dict(zip(NAMES, shapes))}
    g4, low4, du1, dh4, dh4_send = feed_back(
        dec_feed_back_body, 1, dec_own, dec_other, slope1
    )
    dh4_recv = swap(dh4_send)
    feed1, two1, one1 = feed_weights(1, h4, du1, f1, low4)
    feed1.next()
    g3, low3, dq2, dk2, dv2, dh3, dh3_send, mem_grad, mem_send, sums4 = attention_back(
        True, False, g4, dh4, dh4_recv, x4, 4, 2, q2, k2, v2, log2, source_keys, enc_own, objective
    )
    mem_recv = swap(mem_send)
    cross, bias2, dh3_later = attention_weights(
        2, h3, memory, dq2, dk2, dv2, turned2, low3, dh3_send
    )
    dh3_recv = swap(dh3_later)
    feed1.next(LONG)
    cross.next()
    g1, low1, du0, dh1, dh1_send = feed_back(
        enc_feed_back_body, 0, enc_own, objective, mem_grad, mem_recv, slope0
    )
    dh1_recv = swap(dh1_send)
    feed0, two0, one0 = feed_weights(0, h1, du0, f0, low1)
    cross.next()
    g2, low2, dq1, dk1, dv1, dh2, dh2_send, sums3 = attention_back(
        False, True, g3, dh3, dh3_recv, x3, 3, 1, q1, k1, v1, log1, target_keys, target_queries
    )
    dh2_recv = swap(dh2_send)
    first1, bias1 = attention_weights(1, h2, h2, dq1, dk1, dv1, turned1, low2)
    feed0.next()
    early = feed1.merge(cross)
    early.next()
    g0, low0, dq0, dk0, dv0, dh0, dh0_send, sums1 = attention_back(
        False, False, g1, dh1, dh1_recv, x1, 1, 0, q0, k0, v0, log0, source_keys
    )
    dh0_recv = swap(dh0_send)
    first0, bias0 = attention_weights(0, h0, h0, dq0, dk0, dv0, turned0, low0)
    feed0.next(TAIL)
    early = Gathered(early, stacks, LONG)
    late = first1.merge(first0)
    late.next(TAIL)
    source_grad, sums0 = last_norm(g0, dh0, dh0_recv, source_near, 0)
    target_grad, sums2 = last_norm(g2, dh2, dh2_recv, target_near, 2)
    small = SmallTotal(
        order, core,
        [
            norm_gain.shape, norm_bias.shape, attn_out_bias.shape, ffn_out_bias.shape,
            attn_in_bias.shape, ffn_in_bias.shape,
        ],
        [sums0, sums1, sums2, sums3, sums4, two0, two1, bias0, bias1, bias2, one0, one1],
    )
    early.next()
    feed0.next(TAIL)
    late.next(TAIL)
    small.next()
    early.next()
    feed0 = Gathered(feed0, stacks)
    feed0.next()
    late.next(TAIL)
    small.next()
    feed0.next()
    late = Gathered(late, stacks)
    late.next()
    small.next()
    early.next()
    late.next()
    early.next()
    small.next()
    feed0.next()
    feed0.next()
    decoded_other = swap(send4)
    (decoded,) = order.call(
        decoded_body, [shape(targets // 2, width, BF16)], [base4, decoded_other], leave=[0]
    )
    small.next()
    late.next()
    late.next()
    for unused in range(dp_bits() + 4):
        for group in (early, feed0, late, small):
            group.next()
    gains, offsets, out_biases, two_biases, in_biases, one_biases = small.results
    return (
        encoded[:, None],
        decoded[:, None],
        source_grad,
        target_grad,
        gains,
        offsets,
        stacks["attn_in"],
        in_biases,
        stacks["attn_out"],
        out_biases,
        stacks["ffn_in"],
        one_biases,
        stacks["ffn_out"],
        two_biases,
    )


def solution(mesh):
    tokens = P("tensor", "dp", None)
    return jax.shard_map(
        on_device,
        mesh=mesh,
        in_specs=(
            tokens, tokens, P("dp", None), P("dp", None), P("dp"), P("dp", "tensor"),
            tokens, tokens, P(), P(),
            P(None, None, None, "tensor"), P(None, None, "tensor"), P(None, "tensor", None), P(),
            P(None, None, "tensor"), P(None, "tensor"), P(None, "tensor", None), P(),
        ),
        out_specs=(
            tokens, tokens, tokens, tokens, P(), P(),
            P(None, None, None, "tensor"), P(None, None, "tensor"), P(None, "tensor", None), P(),
            P(None, None, "tensor"), P(None, "tensor"), P(None, "tensor", None), P(),
        ),
        check_vma=False,
    )
```

```python
import functools

import jax
import jax.numpy as jnp
from jax import lax
from jax.experimental import pallas as pl
from jax.experimental.pallas import tpu as pltpu
from jax.sharding import PartitionSpec as P

HEAD = 64
PAIR = 2 * HEAD
EPSILON = 1e-05
MASKED_SCORE = -1000000000.0
FAR = 1e9
ROOT = 0.7978845608028654
CUBIC = 0.044715
BF16 = jnp.bfloat16
F32 = jnp.float32
VMEM_LIMIT = 18 * 1024 * 1024
BYTES = 3690000
NN = ((1,), (0,))
NT = ((1,), (1,))
TN = ((0,), (0,))
LARGE = 1 << 20
LONG = 40
STEP = 0.2
TAIL = 3
SLOTS = 4
NAMES = ("ffn_in", "ffn_out", "attn_in", "attn_out")
TOKEN = jax.ShapeDtypeStruct((8, 128), F32)


def dot(left, right, contract):
    return lax.dot_general(left, right, (contract, ((), ())), preferred_element_type=F32)


def shape(rows, columns, dtype):
    return jax.ShapeDtypeStruct((rows, columns), dtype)


NEAR = pl.BlockSpec(memory_space=pltpu.VMEM)
AWAY = pl.BlockSpec(memory_space=pl.ANY)
NUMBER = pl.BlockSpec(memory_space=pltpu.SMEM)


class Weight:
    def __init__(self, stack, layer):
        self.stack = stack
        self.layer = layer


class Place:
    def __init__(self, array):
        self.array = array


class Params:
    def __init__(self, *arrays):
        self.arrays = arrays


class Fetch:
    def __init__(self, source, buffer, semaphore):
        self.copy = pltpu.make_async_copy(source, buffer, semaphore)
        self.copy.start()
        self.buffer = buffer
        self.arrived = False

    def here(self):
        if not self.arrived:
            self.copy.wait()
            self.arrived = True
        return self.buffer


class Order:
    def __init__(self):
        self.token = None

    def call(
        self, body, outs, ins, microseconds=0.5, scratch=(), leave=(), away=(), aliases={},
        limit=VMEM_LIMIT,
    ):
        tokens = [] if self.token is None else [self.token]
        specs, args, weights, groups = [], [], [], []
        for value in ins:
            if isinstance(value, Params):
                groups.append(len(args))
                for array in value.arrays:
                    specs.append(NEAR)
                    args.append(pltpu.with_memory_space_constraint(array, pltpu.VMEM))
            elif isinstance(value, Place):
                specs.append(AWAY)
                args.append(pltpu.with_memory_space_constraint(value.array, pltpu.HBM))
            elif isinstance(value, Weight):
                weights.append((len(args), value))
                specs.append(AWAY)
                args.append(pltpu.with_memory_space_constraint(value.stack, pltpu.HBM))
            elif value.dtype == jnp.int32 and value.shape == (1,):
                specs.append(NUMBER)
                args.append(value)
            else:
                specs.append(NEAR)
                args.append(pltpu.with_memory_space_constraint(value, pltpu.VMEM))

        def wrapped(*refs):
            in_refs = list(refs[: len(args)])
            refs = refs[len(args) + len(tokens) :]
            out_refs = refs[: len(outs)]
            refs = refs[len(outs) + 1 :]
            if weights:
                semaphores = refs[-1]
                for i, (at, weight) in enumerate(weights):
                    in_refs[at] = Fetch(in_refs[at].at[weight.layer], refs[i], semaphores.at[i])
            for at in reversed(groups):
                in_refs[at : at + 6] = [in_refs[at : at + 6]]
            body(*in_refs, *out_refs, *refs[len(weights) : len(weights) + len(scratch)])

        buffers = [pltpu.VMEM(w.stack.shape[1:], w.stack.dtype) for unused, w in weights]
        semaphores = [pltpu.SemaphoreType.DMA((len(weights),))] if weights else []
        results = pl.pallas_call(
            wrapped,
            out_shape=[
                *[
                    o if i in leave or i in away else pltpu.VMEM(o.shape, o.dtype)
                    for i, o in enumerate(outs)
                ],
                TOKEN,
            ],
            in_specs=specs + [AWAY] * len(tokens),
            out_specs=[AWAY if i in away else NEAR for i in range(len(outs))] + [AWAY],
            scratch_shapes=[*buffers, *scratch, *semaphores],
            input_output_aliases=aliases,
            compiler_params=pltpu.CompilerParams(vmem_limit_bytes=limit),
            cost_estimate=pl.CostEstimate(
                flops=int(microseconds * 1.15e9), transcendentals=0, bytes_accessed=int(microseconds * BYTES)
            ),
        )(*args, *tokens)
        self.token = results[-1]
        return results[:-1]


def norm_parts(inputs):
    centre = inputs - jnp.mean(inputs, axis=-1, keepdims=True)
    inverse = lax.rsqrt(jnp.mean(centre * centre, axis=-1, keepdims=True) + EPSILON)
    return centre * inverse, inverse


def norm_back(gradient, normed, inverse, gain):
    scaled = gradient * gain
    mean_plain = jnp.mean(scaled, axis=-1, keepdims=True)
    mean_normed = jnp.mean(scaled * normed, axis=-1, keepdims=True)
    return inverse * (scaled - mean_plain - normed * mean_normed)


def column_sum(values):
    return jnp.sum(values.astype(F32), axis=0, keepdims=True)


def halves(count):
    half = count // 2
    return ((0, half), (half, 0))


def lane_half(which, rows):
    lanes = lax.broadcasted_iota(jnp.int32, (rows, PAIR), 1)
    return (lanes >= HEAD) if which else (lanes < HEAD)


def only_head(which, values):
    return jnp.where(lane_half(which, values.shape[0]), values, jnp.zeros_like(values))


def key_scores(key_pair, query_pair, which, key_at, query_at):
    scores = dot(only_head(which, key_pair), query_pair, NT)
    return jnp.where(key_at <= query_at, scores, MASKED_SCORE)


def attend(q_ref, k_ref, v_ref, key_at, query_at_ref, turned_ref, o_ref, log_ref):
    queries, local = q_ref.shape
    block = min(queries, 256)
    for pair in range(local // PAIR):
        columns = pl.ds(pair * PAIR, PAIR)
        key_pair = k_ref[:, columns]
        value_turned = v_ref[:, columns].astype(F32).T.astype(BF16)
        for start in range(0, queries, block):
            rows = pl.ds(start, block)
            query_pair = q_ref[rows, columns]
            query_at = 0.0 if query_at_ref is None else query_at_ref[:, rows]
            for which in range(2):
                head = 2 * pair + which
                scores = key_scores(key_pair, query_pair, which, key_at, query_at)
                top = jnp.max(scores, axis=0, keepdims=True)
                exponent = jnp.exp(scores - top)
                total = jnp.sum(exponent, axis=0, keepdims=True)
                weights = (exponent * (1.0 / total)).astype(BF16)
                log_ref[pl.ds(head, 1), rows] = top + jnp.log(total)
                mixed = dot(value_turned[which * HEAD : (which + 1) * HEAD], weights, NN)
                turned_ref[pl.ds(head * HEAD, HEAD), rows] = mixed.astype(BF16)
    o_ref[...] = turned_ref[...].astype(F32).T.astype(BF16)


def in_bias_rows(params, layer):
    return params[4][layer, 0:1], params[4][layer, 1:2]


def row_of(ref, index):
    return ref[index : index + 1]


def normalised(value, params, norm):
    normed, unused = norm_parts(value)
    return (normed * row_of(params[0], norm) + row_of(params[1], norm)).astype(BF16)


def column(row):
    return jnp.broadcast_to(row, (8, row.shape[1])).T[:, 0:1]


def own_first(row, here):
    half = row.shape[1] // 2
    return jnp.where(here == 0, row, jnp.concatenate([row[:, half:], row[:, :half]], axis=1))


def scaled_queries(hidden, w_in, bias):
    return ((dot(hidden, w_in[0], NN) + bias).astype(BF16) * HEAD ** (-0.5)).astype(BF16)


def load_body(*refs):
    count = len(refs) // 2
    copies = [
        pltpu.make_async_copy(refs[i], refs[count + i], refs[-1].at[i]) for i in range(count)
    ]
    for copy in copies:
        copy.start()
    for copy in copies:
        copy.wait()


def first_attention(norm, layer, own_ref, other_ref, params, w_in, w_out, key_at, query_at_ref, *refs):
    h_ref, q_ref, k_ref, v_ref, turned_ref, log_ref, base_ref, send_ref, o_ref = refs
    half = own_ref.shape[0]
    query_bias, value_bias = in_bias_rows(params, layer)
    for part, source in enumerate((own_ref, other_ref)):
        rows = pl.ds(part * half, half)
        hidden = normalised(source[...].astype(F32), params, norm)
        h_ref[rows] = hidden
        w = w_in.here()
        q_ref[rows] = scaled_queries(hidden, w, query_bias)
        k_ref[rows] = dot(hidden, w[1], NN).astype(BF16)
        v_ref[rows] = (dot(hidden, w[2], NN) + value_bias).astype(BF16)
    attend(q_ref, k_ref, v_ref, key_at, query_at_ref, turned_ref, o_ref, log_ref)
    w = w_out.here()
    for part, source in enumerate((own_ref, other_ref)):
        rows = pl.ds(part * half, half)
        partial = dot(o_ref[rows], w[...], NN)
        send_ref[rows] = partial.astype(BF16)
        base_ref[rows] = source[...].astype(F32) + row_of(params[2], layer) + partial


def enc_first_body(norm, layer, own_ref, other_ref, params, w_in, w_out, mask_ref, here_ref, place_ref, *refs):
    outs, key_at_ref, o_ref = refs[:-2], refs[-2], refs[-1]
    row = own_first(jnp.where(mask_ref[...] == 1, 0.0, FAR), here_ref[0])
    key_at = column(row)
    key_at_ref[...] = key_at
    first_attention(norm, layer, own_ref, other_ref, params, w_in, w_out, key_at, None, *outs, o_ref)


def dec_first_body(
    norm, layer, own_ref, other_ref, params, w_in, w_out, mask_ref, here_ref,
    cot_ref, loss_ref, objective_ref, place_ref, *refs
):
    outs, (key_at_ref, query_at_ref, gradient_ref, gradient_send_ref, o_ref) = refs[:-5], refs[-5:]
    count = mask_ref.shape[1]
    position = own_first(
        lax.broadcasted_iota(jnp.int32, (1, count), 1).astype(F32), here_ref[0]
    )
    row = jnp.where(own_first(mask_ref[...].astype(F32), here_ref[0]) == 1.0, position, FAR)
    key_at = column(row)
    key_at_ref[...] = key_at
    query_at_ref[...] = position
    flag = objective_ref[0].astype(F32)
    weight = column(0.25 + 0.75 * loss_ref[...].astype(F32)) * (0.5 + 0.5 * flag)
    gradient = cot_ref[...].astype(F32) * weight
    gradient_ref[...] = gradient
    gradient_send_ref[...] = gradient.astype(BF16)
    first_attention(
        norm, layer, own_ref, other_ref, params, w_in, w_out, key_at, query_at_ref, *outs, o_ref
    )


def cross_attention_body(
    norm, layer, before_ref, recv_ref, params, w_in, w_out, k_ref, v_ref, key_at_ref,
    x_ref, h_ref, q_ref, turned_ref, log_ref, base_ref, send_ref, o_ref,
):
    count = x_ref.shape[0]
    half = count // 2
    query_bias, unused = in_bias_rows(params, layer)
    for mine, theirs in halves(count):
        rows = pl.ds(mine, half)
        value = before_ref[rows] + recv_ref[pl.ds(theirs, half)].astype(F32)
        x_ref[rows] = value
        hidden = normalised(value, params, norm)
        h_ref[rows] = hidden
        q_ref[rows] = scaled_queries(hidden, w_in.here(), query_bias)
    attend(q_ref, k_ref, v_ref, key_at_ref[...], None, turned_ref, o_ref, log_ref)
    partial = dot(o_ref[...], w_out.here()[...], NN)
    send_ref[...] = partial.astype(BF16)
    base_ref[...] = x_ref[...] + row_of(params[2], layer) + partial


def memory_body(layer, before_ref, recv_ref, params, w_in, mem_ref, k_ref, v_ref, out_ref):
    count = mem_ref.shape[0]
    half = count // 2
    unused, value_bias = in_bias_rows(params, layer)
    for mine, theirs in halves(count):
        rows = pl.ds(mine, half)
        memory = (before_ref[rows] + recv_ref[pl.ds(theirs, half)].astype(F32)).astype(BF16)
        mem_ref[rows] = memory
        if mine == 0:
            out_ref[...] = memory
        w = w_in.here()
        k_ref[rows] = dot(memory, w[1], NN).astype(BF16)
        v_ref[rows] = (dot(memory, w[2], NN) + value_bias).astype(BF16)


def feed_body(
    norm, layer, last, before_ref, recv_ref, params, w_one, w_two,
    x_ref, h_ref, f_ref, slope_ref, base_ref, send_ref,
):
    count = x_ref.shape[0]
    half = count // 2
    for mine, theirs in halves(count):
        rows = pl.ds(mine, half)
        value = before_ref[rows] + recv_ref[pl.ds(theirs, half)].astype(F32)
        x_ref[rows] = value
        hidden = normalised(value, params, norm)
        h_ref[rows] = hidden
        u = dot(hidden, w_one.here()[...], NN) + row_of(params[5], layer)
        square = u * u
        bent = jnp.tanh(u * (ROOT + (ROOT * CUBIC) * square))
        upper = 0.5 + 0.5 * bent
        active = (u * upper).astype(BF16)
        f_ref[rows] = active
        slope = upper + (0.5 * u) * (1.0 - bent * bent) * (ROOT + (3 * ROOT * CUBIC) * square)
        slope_ref[rows] = slope.astype(BF16)
        partial = dot(active, w_two.here()[...], NN)
        if not last:
            send_ref[rows] = partial.astype(BF16)
            base_ref[rows] = value + row_of(params[3], layer) + partial
        elif mine == 0:
            base_ref[...] = value + row_of(params[3], layer) + partial
        else:
            send_ref[...] = partial.astype(BF16)


def feed_back_rows(
    gradient, rows, w_one, w_two, slope_ref, g_ref, low_ref, du_ref, base_ref, send_ref
):
    g_ref[rows] = gradient
    low = gradient.astype(BF16)
    low_ref[rows] = low
    du = (dot(low, w_two.here()[...], NT) * slope_ref[rows].astype(F32)).astype(BF16)
    du_ref[rows] = du
    partial = dot(du, w_one.here()[...], NT)
    send_ref[rows] = partial.astype(BF16)
    base_ref[rows] = partial


def dec_feed_back_body(own_ref, other_ref, w_one, w_two, slope_ref, *outs):
    half = own_ref.shape[0]
    for part, source in enumerate((own_ref, other_ref)):
        feed_back_rows(
            source[...].astype(F32), pl.ds(part * half, half), w_one, w_two, slope_ref, *outs
        )


def source_seed(cot_ref, objective_ref):
    return cot_ref[...].astype(F32) * (1.0 - 0.5 * objective_ref[0].astype(F32))


def enc_feed_back_body(seed_ref, objective_ref, mem_base_ref, recv_ref, w_one, w_two, slope_ref, *outs):
    half = seed_ref.shape[0]
    own, other = pl.ds(0, half), pl.ds(half, half)
    for rows, theirs in ((own, other), (other, own)):
        gradient = mem_base_ref[rows] + recv_ref[theirs].astype(F32)
        if rows is own:
            gradient = gradient + source_seed(seed_ref, objective_ref)
        feed_back_rows(gradient, rows, w_one, w_two, slope_ref, *outs)


def attention_back_body(norm, cross, causal, *refs):
    (g_in_ref, dh_ref, dh_recv_ref, x_ref, params, w_in, w_out, q_ref, k_ref, v_ref, log_ref,
     key_at_ref), refs = refs[:12], refs[12:]
    query_at_ref = seed_ref = mem_base_ref = mem_send_ref = None
    if causal:
        query_at_ref, refs = refs[0], refs[1:]
    if cross:
        (seed_ref, objective_ref), refs = refs[:2], refs[2:]
    (g_ref, low_ref, dq_ref, dk_ref, dv_ref, base_ref, send_ref), refs = refs[:7], refs[7:]
    if cross:
        (mem_base_ref, mem_send_ref), refs = refs[:2], refs[2:]
    sums_ref, do_ref, turned_ref = refs
    gain = row_of(params[0], norm)
    count, local = dq_ref.shape
    half = count // 2
    for part, (mine, theirs) in enumerate(halves(count)):
        rows = pl.ds(mine, half)
        normed, inverse = norm_parts(x_ref[rows])
        dh = dh_ref[rows] + dh_recv_ref[pl.ds(theirs, half)].astype(F32)
        gradient = g_in_ref[rows] + norm_back(dh, normed, inverse, gain)
        g_ref[rows] = gradient
        low = gradient.astype(BF16)
        low_ref[rows] = low
        if part == 0:
            sums_ref[0:1] = column_sum(dh * normed)
            sums_ref[1:2] = column_sum(dh)
            sums_ref[2:3] = column_sum(low)
        do_ref[rows] = dot(low, w_out.here()[...], NT).astype(BF16)
    key_at = key_at_ref[...]
    block = min(count, 256)
    keys = k_ref.shape[0]
    for pair in range(local // PAIR):
        columns = pl.ds(pair * PAIR, PAIR)
        key_pair = k_ref[:, columns]
        key_turned = key_pair.astype(F32).T.astype(BF16)
        value_pair = v_ref[:, columns]
        dk = [None, None]
        dv = [None, None]
        for start in range(0, count, block):
            rows = pl.ds(start, block)
            query_pair = q_ref[rows, columns]
            do_pair = do_ref[rows, columns]
            query_at = 0.0 if query_at_ref is None else query_at_ref[:, rows]
            for which in range(2):
                head = 2 * pair + which
                scores = key_scores(key_pair, query_pair, which, key_at, query_at)
                probs = jnp.exp(scores - log_ref[pl.ds(head, 1), rows])
                prob_grad = dot(only_head(which, value_pair), do_pair, NT)
                product = probs * prob_grad
                inner = jnp.sum(product, axis=0, keepdims=True)
                score_grad = (product - probs * inner).astype(BF16)
                dv_part = dot(probs.astype(BF16), do_pair, NN)
                dk_part = dot(score_grad, query_pair, NN)
                dq_part = dot(key_turned[which * HEAD : (which + 1) * HEAD], score_grad, NN)
                turned_ref[pl.ds(head * HEAD, HEAD), rows] = dq_part * HEAD ** (-0.5)
                dk[which] = dk_part if dk[which] is None else dk[which] + dk_part
                dv[which] = dv_part if dv[which] is None else dv[which] + dv_part
        first = lane_half(0, keys)
        dk_ref[:, columns] = jnp.where(first, dk[0], dk[1]).astype(BF16)
        dv_ref[:, columns] = jnp.where(first, dv[0], dv[1]).astype(BF16)
    dq_ref[...] = turned_ref[...].T.astype(BF16)
    w = w_in.here()
    if cross:
        partial = dot(dk_ref[...], w[1], NT) + dot(dv_ref[...], w[2], NT)
        mem_base_ref[...] = partial
        mem_half = keys // 2
        mem_send_ref[0:mem_half] = (
            partial[0:mem_half] + source_seed(seed_ref, objective_ref)
        ).astype(BF16)
        mem_send_ref[mem_half:] = partial[mem_half:].astype(BF16)
        partial = dot(dq_ref[...], w[0], NT)
        send_ref[...] = partial.astype(BF16)
        base_ref[...] = partial
    else:
        for part in (1, 0):
            rows = pl.ds(part * half, half)
            partial = (
                dot(dq_ref[rows], w[0], NT)
                + dot(dk_ref[rows], w[1], NT)
                + dot(dv_ref[rows], w[2], NT)
            )
            if part == 1:
                send_ref[...] = partial.astype(BF16)
            else:
                base_ref[...] = partial


def last_norm_body(norm, g_ref, dh_ref, recv_ref, x_ref, params, out_ref, sums_ref):
    normed, inverse = norm_parts(x_ref[...].astype(F32))
    dh = dh_ref[...] + recv_ref[...].astype(F32)
    sums_ref[0:1] = column_sum(dh * normed)
    sums_ref[1:2] = column_sum(dh)
    half = out_ref.shape[0]
    result = g_ref[0:half] + norm_back(dh, normed, inverse, row_of(params[0], norm))
    out_ref[...] = result.reshape(out_ref.shape)


def feed_weights_body(h_ref, du_ref, f_ref, low_ref, place_ref, send_ref, keep_ref, sums_ref, hidden_sums_ref):
    bit = bit_of(place_ref, 0)
    width = h_ref.shape[1]
    part = width // 2
    for which, out_ref in ((1 - bit, send_ref), (bit, keep_ref)):
        left = h_ref[:, pl.ds(pl.multiple_of(which * part, 128), part)]
        for side in range(2):
            out_ref[pl.ds(side * part, part)] = dot(
                left, du_ref[:, pl.ds(side * width, width)], TN
            ).astype(BF16)
        left = f_ref[:, pl.ds(pl.multiple_of(which * width, 128), width)]
        out_ref[pl.ds(width, width)] = dot(left, low_ref[...], TN).astype(BF16)
    half = low_ref.shape[0] // 2
    sums_ref[...] = column_sum(low_ref[0:half])
    hidden_sums_ref[...] = column_sum(du_ref[...])


def attention_weights_body(
    h_ref, mem_ref, dq_ref, dk_ref, dv_ref, turned_ref, low_ref, place_ref, *refs
):
    later_ref, refs = (refs[0], refs[1:]) if len(refs) == 5 else (None, refs)
    send_ref, keep_ref, sums_ref = refs[:3]
    if later_ref is not None:
        refs[3][...] = later_ref[...]
    bit = bit_of(place_ref, 0)
    width = h_ref.shape[1]
    part = width // 2
    quarter = width // 4
    left_side = pl.ds(0, part)
    right_side = pl.ds(part, part)
    for which, out_ref in ((1 - bit, send_ref), (bit, keep_ref)):
        columns = pl.ds(pl.multiple_of(which * part, 128), part)
        out_ref[pl.ds(0, part), left_side] = dot(h_ref[:, columns], dq_ref[...], TN).astype(BF16)
        memory = mem_ref[:, columns]
        out_ref[pl.ds(0, part), right_side] = dot(memory, dk_ref[...], TN).astype(BF16)
        values = dot(memory, dv_ref[...], TN).astype(BF16)
        out_ref[pl.ds(part, quarter), left_side] = values[:quarter]
        out_ref[pl.ds(part, quarter), right_side] = values[quarter:]
        rows = pl.ds(pl.multiple_of(which * quarter, 64), quarter)
        out_ref[pl.ds(part + quarter, quarter)] = dot(turned_ref[rows], low_ref[...], NN).astype(BF16)
    sums_ref[:, left_side] = column_sum(dq_ref[...])
    sums_ref[:, right_side] = column_sum(dv_ref[...])


def bit_of(place_ref, step):
    return (place_ref[0] >> step) & 1


def add_body(step, layout, place_ref, *refs):
    send_ref, next_ref = refs[-2:]
    bit = bit_of(place_ref, step)
    for out_ref, which in ((send_ref, 1 - bit), (next_ref, bit)):
        target = 0
        for i, (first, segments) in enumerate(layout):
            keep_ref, received_ref = refs[2 * i], refs[2 * i + 1]
            for rows in segments:
                half = rows // 2
                block = half
                while block % 32 == 0 and block > 128:
                    block //= 2
                for start in range(0, half, block):
                    part = pl.ds(pl.multiple_of(first + which * half + start, 8), block)
                    out_ref[pl.ds(target + start, block)] = (
                        keep_ref[part].astype(F32) + received_ref[part].astype(F32)
                    ).astype(BF16)
                first += rows
                target += half


def last_sum_body(keep_ref, received_ref, out_ref):
    out_ref[...] = (keep_ref[...].astype(F32) + received_ref[...].astype(F32)).astype(BF16)


def join_body(first_ref, second_ref, out_ref):
    rows = first_ref.shape[0]
    out_ref[0:rows] = first_ref[...]
    out_ref[rows:] = second_ref[...]


def put_body(groups, masks, count, bits, old, place_ref, *refs):
    blocks, refs = refs[:count], refs[count + old :]
    outs = dict(zip(NAMES, refs[:4]))
    wide_ref, semaphores = refs[4:]
    width = blocks[0].shape[1]
    part, quarter = width // 2, width // 4
    slots = wide_ref.shape[0]
    flying = []

    def copy(slot, side, rows, target):
        source = wide_ref.at[slot, pl.ds(0, rows), pl.ds(side * part, part)]
        return pltpu.make_async_copy(source, target, semaphores.at[slot, side])

    def wait(slot, rows):
        for side in range(2):
            target = outs["ffn_out"].at[0, pl.ds(0, rows), pl.ds(0, part)]
            copy(slot, side, rows, target).wait()

    each = len(masks) // count
    for number, mask in enumerate(masks):
        block_ref = blocks[number // each]
        if number % each == 0:
            at = 0
        device = place_ref[0] ^ mask
        upper = device & 1
        for kind, layer, rows in groups:
            slot = len(flying) % slots
            if len(flying) >= slots:
                wait(*flying[-slots])
            flying.append((slot, rows))
            wide_ref[slot, pl.ds(0, rows)] = block_ref[pl.ds(at, rows)].astype(F32)
            at += rows
            inner = 0
            for bit in range(1, bits):
                inner = inner + ((device >> bit) & 1) * (rows << (bits - 1 - bit))

            def send(side, target):
                copy(slot, side, rows, target).start()

            if kind == "in":
                row = pl.multiple_of(upper * part + lax.rem(inner, part), 8)
                column = lax.div(inner, part) * width
                for side in range(2):
                    columns = pl.ds(pl.multiple_of(column + side * part, 128), part)
                    send(side, outs["ffn_in"].at[layer, pl.ds(row, rows), columns])
            elif kind == "out":
                row = pl.multiple_of(upper * width + inner, 8)
                for side in range(2):
                    columns = pl.ds(side * part, part)
                    send(side, outs["ffn_out"].at[layer, pl.ds(row, rows), columns])
            else:

                @pl.when(inner < part)
                def query_and_key():
                    row = pl.multiple_of(upper * part + inner, 8)
                    for side in range(2):
                        send(side, outs["attn_in"].at[layer, side, pl.ds(row, rows)])

                @pl.when((inner >= part) & (inner < part + quarter))
                def value():
                    row = upper * part + inner - part
                    for side in range(2):
                        target = pl.ds(pl.multiple_of(row + side * quarter, 8), rows)
                        send(side, outs["attn_in"].at[layer, 2, target])

                @pl.when(inner >= part + quarter)
                def output():
                    row = pl.multiple_of(upper * quarter + inner - part - quarter, 8)
                    for side in range(2):
                        columns = pl.ds(side * part, part)
                        send(side, outs["attn_out"].at[layer, pl.ds(row, rows), columns])

    for slot, rows in flying[-slots:]:
        wait(slot, rows)


def pack_body(*refs):
    norm_refs, out_refs, rows_refs, wide_refs = refs[:5], refs[5:7], refs[7:10], refs[10:12]
    shared_ref, apart_ref = refs[12:]
    shared_ref[...] = jnp.zeros_like(shared_ref)
    apart_ref[...] = jnp.zeros_like(apart_ref)
    for i, ref in enumerate(norm_refs):
        shared_ref[i : i + 1] = ref[0:1]
        shared_ref[5 + i : 6 + i] = ref[1:2]
    for i, source in enumerate((1, 3, 4)):
        shared_ref[10 + i : 11 + i] = norm_refs[source][2:3]
    for i, ref in enumerate(out_refs):
        shared_ref[13 + i : 14 + i] = ref[...]
    for i, ref in enumerate(rows_refs):
        apart_ref[i : i + 1] = ref[...]
    width = shared_ref.shape[1]
    for i, ref in enumerate(wide_refs):
        for side in range(2):
            apart_ref[3 + 2 * i + side : 4 + 2 * i + side] = ref[:, side * width : (side + 1) * width]


def pair_small_body(shared_ref, received_ref, apart_ref, out_ref):
    out_ref[0:16] = shared_ref[...] + received_ref[...]
    out_ref[16:24] = apart_ref[...]


def add_small_body(first_ref, second_ref, out_ref):
    out_ref[...] = first_ref[...] + second_ref[...]


def last_small_body(first_ref, second_ref, *outs):
    total = first_ref[...] + second_ref[...]
    gain_ref, offset_ref, out_bias_ref, two_ref, in_ref, one_ref = outs
    gain_ref[...] = total[0:5]
    offset_ref[...] = total[5:10]
    out_bias_ref[...] = total[10:13]
    two_ref[...] = total[13:15]
    width = total.shape[1]
    part = width // 2
    for i in range(3):
        for side in range(2):
            in_ref[i, side : side + 1] = total[16 + i : 17 + i, side * part : (side + 1) * part]
    for i in range(2):
        for side in range(2):
            row = 19 + 2 * i + side
            one_ref[i : i + 1, side * width : (side + 1) * width] = total[row : row + 1]


def decoded_body(base_ref, received_ref, out_ref):
    out_ref[...] = (base_ref[...] + received_ref[...].astype(F32)).astype(BF16)


def pass_body(value_ref, unused_ref, out_ref):
    out_ref[...] = value_ref[...]


def swap(values):
    return lax.ppermute(values, "tensor", [(0, 1), (1, 0)])


def across(values, stride):
    count = lax.axis_size("dp")
    return lax.ppermute(values, "dp", [(i, i ^ stride) for i in range(count)])


def dp_bits():
    return lax.axis_size("dp").bit_length() - 1


class Total:
    def __init__(self, order, place, parts, step=1):
        self.order = order
        self.place = place
        self.parts = parts
        self.step = step

    def merge(self, *others):
        assert all(self.step == other.step for other in others)
        return Total(
            self.order, self.place, self.parts + sum((other.parts for other in others), []), self.step
        )

    def finish(self, microseconds=0.2):
        while self.step < dp_bits():
            self.next()
        ((self.groups, keep, received, unused),) = self.parts
        (self.shard,) = self.order.call(
            last_sum_body, [shape(*keep.shape, BF16)], [keep, received], microseconds=microseconds
        )

    def next(self, microseconds=0.5):
        if self.step == dp_bits():
            return
        width = self.parts[0][1].shape[1]
        layout = [
            (first, [rows for unused, unused, rows in groups])
            for groups, unused, unused, first in self.parts
        ]
        rows = sum(sum(segments) for unused, segments in layout) // 2
        send, keep = self.order.call(
            functools.partial(add_body, self.step, layout), [shape(rows, width, BF16)] * 2,
            [self.place, *[value for unused, *pair, unused in self.parts for value in pair]],
            microseconds=microseconds,
        )
        groups = [
            (kind, layer, rows // 2)
            for members, *unused in self.parts
            for kind, layer, rows in members
        ]
        self.parts = [(groups, keep, across(send, 1 << self.step), 0)]
        self.step += 1


class Gathered:
    def __init__(self, total, stacks, microseconds=TAIL):
        self.order = total.order
        self.place = total.place
        self.stacks = stacks
        total.finish(microseconds)
        self.groups = total.groups
        self.stages = self.run(total.shard)
        self.next()

    def next(self):
        next(self.stages, None)

    def run(self, block):
        order = self.order
        masks = [0]
        for bit in range(dp_bits() - 1, 0, -1):
            received = across(block, 1 << bit)
            if bit > 1:
                yield
                (block,) = order.call(
                    join_body, [shape(2 * block.shape[0], block.shape[1], BF16)], [block, received],
                    microseconds=TAIL,
                )
                masks += [mask ^ (1 << bit) for mask in masks]
        other = across(block, 1)
        yield
        last = across(received, 1)
        crossed = [mask ^ 2 for mask in masks]
        self.put([block, received], masks + crossed)
        yield
        self.put([other], [mask ^ 1 for mask in masks])
        yield
        self.put([last], [mask ^ 1 for mask in crossed])
        yield

    def put(self, blocks, masks):
        stacks = self.stacks
        old = [stacks[name] for name in NAMES] if NAMES[0] in stacks else []
        rows = max(rows for unused, unused, rows in self.groups)
        results = self.order.call(
            functools.partial(put_body, self.groups, masks, len(blocks), dp_bits(), len(old)),
            [jax.ShapeDtypeStruct(stacks["shapes"][name], F32) for name in NAMES],
            [self.place, *blocks, *[Place(value) for value in old]],
            aliases={1 + len(blocks) + i: i for i in range(len(old))},
            away=range(4),
            microseconds=TAIL,
            scratch=[
                pltpu.VMEM((6, rows, blocks[0].shape[1]), F32),
                pltpu.SemaphoreType.DMA((6, 2)),
            ],
        )
        stacks.update(zip(NAMES, results))


class SmallTotal:
    def __init__(self, order, place, shapes, ins):
        self.order = order
        self.place = place
        self.shapes = shapes
        self.results = None
        width = ins[0].shape[1]
        self.shared, self.apart = order.call(
            pack_body, [shape(16, width, F32), shape(8, width, F32)], ins
        )
        self.received = swap(self.shared)
        self.stages = self.run()

    def next(self):
        next(self.stages, None)

    def run(self):
        order, bits = self.order, dp_bits()
        whole = shape(24, self.shared.shape[1], F32)
        (value,) = order.call(pair_small_body, [whole], [self.shared, self.received, self.apart], microseconds=TAIL)
        for bit in range(bits):
            received = across(value, 1 << bit)
            yield
            if bit + 1 < bits:
                (value,) = order.call(add_small_body, [whole], [value, received], microseconds=TAIL)
        self.results = order.call(
            last_small_body, [jax.ShapeDtypeStruct(dims, F32) for dims in self.shapes],
            [value, received], leave=range(6),
        )
        yield


def on_device(
    src_embed, tgt_embed, src_mask, tgt_mask, objective, loss_mask, enc_cot, dec_cot,
    norm_gain, norm_bias, attn_in, attn_in_bias, attn_out, attn_out_bias,
    ffn_in, ffn_in_bias, ffn_out, ffn_out_bias,
):
    order = Order()
    here = lax.axis_index("tensor")
    width = src_embed.shape[2]
    local = attn_in.shape[3]
    hidden_width = ffn_in.shape[2]
    source_own = src_embed.reshape(-1, width)
    target_own = tgt_embed.reshape(-1, width)
    sources = 2 * source_own.shape[0]
    targets = 2 * target_own.shape[0]
    enc_own = enc_cot.reshape(-1, width)
    target_other = swap(target_own)
    source_other = swap(source_own)
    loaded = [
        source_own, target_own, dec_cot.reshape(-1, width), loss_mask, src_mask, tgt_mask, enc_own,
        norm_gain, norm_bias, attn_out_bias, ffn_out_bias, attn_in_bias, ffn_in_bias,
    ]
    source_near, target_near, dec_cot_near, loss_near, src_mask_near, tgt_mask_near, enc_own, *small_near = order.call(
        load_body, [jax.ShapeDtypeStruct(a.shape, a.dtype) for a in loaded],
        [Place(a) for a in loaded], scratch=[pltpu.SemaphoreType.DMA((len(loaded),))],
    )
    params = Params(*small_near)
    core = lax.axis_index("dp").astype(jnp.int32).reshape(1)
    here = here.astype(jnp.int32).reshape(1)

    def first(body, own, other, norm, layer, mask, more_ins, more_outs):
        count = 2 * own.shape[0]
        narrow = shape(count, local, BF16)
        return order.call(
            functools.partial(body, norm, layer),
            [
                shape(count, width, BF16), narrow, narrow, narrow,
                shape(local, count, BF16), shape(8, count, F32),
                shape(count, width, F32), shape(count, width, BF16), shape(count, 1, F32),
                *more_outs,
            ],
            [own, other, params, Weight(attn_in, layer), Weight(attn_out, layer), mask, here, *more_ins],
            microseconds=LONG,
            scratch=[pltpu.VMEM((count, local), BF16)],
        )

    def feed(before, recv, norm, layer, last):
        count = before.shape[0]
        sent = count // 2 if last else count
        return order.call(
            functools.partial(feed_body, norm, layer, last),
            [
                shape(count, width, F32), shape(count, width, BF16),
                shape(count, hidden_width, BF16), shape(count, hidden_width, BF16),
                shape(sent, width, F32), shape(sent, width, BF16),
            ],
            [before, recv, params, Weight(ffn_in, layer), Weight(ffn_out, layer)],
            microseconds=LONG,
        )

    h0, q0, k0, v0, turned0, log0, base0, send0, source_keys = first(
        enc_first_body, source_near, source_other, 0, 0, src_mask_near, [core], []
    )
    (
        h2, q1, k1, v1, turned1, log1, base1, send1, target_keys,
        target_queries, dec_own, dec_send,
    ) = first(
        dec_first_body, target_near, target_other, 2, 1, tgt_mask_near,
        [dec_cot_near, loss_near, objective, core],
        [shape(1, targets, F32), shape(targets // 2, width, F32), shape(targets // 2, width, BF16)],
    )
    recv1 = swap(send1)
    dec_other = swap(dec_send)
    recv0 = swap(send0)
    x1, h1, f0, slope0, base2, send2 = feed(base0, recv0, 1, 0, False)
    recv2 = swap(send2)
    narrow = shape(sources, local, BF16)
    memory, k2, v2, encoded = order.call(
        functools.partial(memory_body, 2),
        [shape(sources, width, BF16), narrow, narrow, shape(sources // 2, width, BF16)],
        [base2, recv2, params, Weight(attn_in, 2)], microseconds=3, leave=[3],
    )
    x3, h3, q2, turned2, log2, base3, send3 = order.call(
        functools.partial(cross_attention_body, 3, 2),
        [
            shape(targets, width, F32), shape(targets, width, BF16),
            shape(targets, local, BF16), shape(local, targets, BF16), shape(8, targets, F32),
            shape(targets, width, F32), shape(targets, width, BF16),
        ],
        [
            base1, recv1, params, Weight(attn_in, 2), Weight(attn_out, 2), k2, v2, source_keys,
        ],
        microseconds=5,
        scratch=[pltpu.VMEM((targets, local), BF16)],
    )
    recv3 = swap(send3)
    x4, h4, f1, slope1, base4, send4 = feed(base3, recv3, 4, 1, True)

    def feed_back(body, layer, *ins):
        count = ins[-1].shape[0]
        return order.call(
            body,
            [
                shape(count, width, F32), shape(count, width, BF16),
                shape(count, hidden_width, BF16),
                shape(count, width, F32), shape(count, width, BF16),
            ],
            [*ins[:-1], Weight(ffn_in, layer), Weight(ffn_out, layer), ins[-1]],
            microseconds=LONG,
        )

    def attention_back(cross, causal, g, dh, recv, x, norm, layer, q, k, v, log, key_at, *more):
        count = q.shape[0]
        keys = k.shape[0]
        outs = [
            shape(count, width, F32), shape(count, width, BF16),
            shape(count, local, BF16), shape(keys, local, BF16), shape(keys, local, BF16),
        ]
        if cross:
            outs += [
                shape(count, width, F32), shape(count, width, BF16),
                shape(keys, width, F32), shape(keys, width, BF16),
            ]
        else:
            outs += [shape(count // 2, width, F32), shape(count // 2, width, BF16)]
        outs += [shape(3, width, F32)]
        return order.call(
            functools.partial(attention_back_body, norm, cross, causal), outs,
            [
                g, dh, recv, x, params, Weight(attn_in, layer), Weight(attn_out, layer),
                q, k, v, log, key_at, *more,
            ],
            microseconds=LONG,
            scratch=[pltpu.VMEM((count, local), BF16), pltpu.VMEM((local, count), F32)],
        )

    def feed_weights(layer, h, du, f, low):
        out = shape(2 * width, width, BF16)
        send, keep, sums, hidden_sums = order.call(
            feed_weights_body, [out, out, shape(1, width, F32), shape(1, hidden_width, F32)],
            [h, du, f, low, core], microseconds=2 if layer == 0 else LONG,
        )
        received = across(send, 1)
        groups = [("in", layer, width), ("out", layer, width)]
        return Total(order, core, [(groups, keep, received, 0)]), sums, hidden_sums

    def attention_weights(layer, h, mem, dq, dk, dv, turned, low, *later):
        out = shape(width, width, BF16)
        send, keep, sums, *passed = order.call(
            attention_weights_body,
            [out, out, shape(1, width, F32), *[shape(*value.shape, BF16) for value in later]],
            [h, mem, dq, dk, dv, turned, low, core, *later], microseconds=2,
        )
        total = Total(order, core, [([("attention", layer, width)], keep, across(send, 1), 0)])
        return total, sums, *passed

    def last_norm(g, dh, recv, own, norm):
        rows = own.shape[0]
        return order.call(
            functools.partial(last_norm_body, norm),
            [jax.ShapeDtypeStruct((rows, 1, width), F32), shape(2, width, F32)],
            [g, dh, recv, own, params], leave=[0],
        )

    shapes = (ffn_in.shape, ffn_out.shape, attn_in.shape, attn_out.shape)
    stacks = {"shapes": dict(zip(NAMES, shapes))}
    g4, low4, du1, dh4, dh4_send = feed_back(
        dec_feed_back_body, 1, dec_own, dec_other, slope1
    )
    dh4_recv = swap(dh4_send)
    feed1, two1, one1 = feed_weights(1, h4, du1, f1, low4)
    feed1.next()
    g3, low3, dq2, dk2, dv2, dh3, dh3_send, mem_grad, mem_send, sums4 = attention_back(
        True, False, g4, dh4, dh4_recv, x4, 4, 2, q2, k2, v2, log2, source_keys, enc_own, objective
    )
    mem_recv = swap(mem_send)
    cross, bias2, dh3_later = attention_weights(
        2, h3, memory, dq2, dk2, dv2, turned2, low3, dh3_send
    )
    dh3_recv = swap(dh3_later)
    feed1.next(LONG)
    cross.next()
    g1, low1, du0, dh1, dh1_send = feed_back(
        enc_feed_back_body, 0, enc_own, objective, mem_grad, mem_recv, slope0
    )
    dh1_recv = swap(dh1_send)
    feed0, two0, one0 = feed_weights(0, h1, du0, f0, low1)
    cross.next()
    g2, low2, dq1, dk1, dv1, dh2, dh2_send, sums3 = attention_back(
        False, True, g3, dh3, dh3_recv, x3, 3, 1, q1, k1, v1, log1, target_keys, target_queries
    )
    dh2_recv = swap(dh2_send)
    first1, bias1 = attention_weights(1, h2, h2, dq1, dk1, dv1, turned1, low2)
    feed0.next()
    early = feed1.merge(cross)
    early.next()
    g0, low0, dq0, dk0, dv0, dh0, dh0_send, sums1 = attention_back(
        False, False, g1, dh1, dh1_recv, x1, 1, 0, q0, k0, v0, log0, source_keys
    )
    dh0_recv = swap(dh0_send)
    first0, bias0 = attention_weights(0, h0, h0, dq0, dk0, dv0, turned0, low0)
    feed0.next(TAIL)
    early = Gathered(early, stacks, LONG)
    late = first1.merge(first0)
    late.next(TAIL)
    source_grad, sums0 = last_norm(g0, dh0, dh0_recv, source_near, 0)
    target_grad, sums2 = last_norm(g2, dh2, dh2_recv, target_near, 2)
    small = SmallTotal(
        order, core,
        [
            norm_gain.shape, norm_bias.shape, attn_out_bias.shape, ffn_out_bias.shape,
            attn_in_bias.shape, ffn_in_bias.shape,
        ],
        [sums0, sums1, sums2, sums3, sums4, two0, two1, bias0, bias1, bias2, one0, one1],
    )
    early.next()
    feed0.next(TAIL)
    late.next(TAIL)
    small.next()
    early.next()
    feed0 = Gathered(feed0, stacks)
    feed0.next()
    late.next(TAIL)
    small.next()
    feed0.next()
    late = Gathered(late, stacks)
    late.next()
    small.next()
    early.next()
    late.next()
    early.next()
    small.next()
    feed0.next()
    feed0.next()
    decoded_other = swap(send4)
    (decoded,) = order.call(
        decoded_body, [shape(targets // 2, width, BF16)], [base4, decoded_other], leave=[0]
    )
    small.next()
    late.next()
    late.next()
    for unused in range(dp_bits() + 4):
        for group in (early, feed0, late, small):
            group.next()
    gains, offsets, out_biases, two_biases, in_biases, one_biases = small.results
    return (
        encoded[:, None],
        decoded[:, None],
        source_grad,
        target_grad,
        gains,
        offsets,
        stacks["attn_in"],
        in_biases,
        stacks["attn_out"],
        out_biases,
        stacks["ffn_in"],
        one_biases,
        stacks["ffn_out"],
        two_biases,
    )


def solution(mesh):
    tokens = P("tensor", "dp", None)
    return jax.shard_map(
        on_device,
        mesh=mesh,
        in_specs=(
            tokens, tokens, P("dp", None), P("dp", None), P("dp"), P("dp", "tensor"),
            tokens, tokens, P(), P(),
            P(None, None, None, "tensor"), P(None, None, "tensor"), P(None, "tensor", None), P(),
            P(None, None, "tensor"), P(None, "tensor"), P(None, "tensor", None), P(),
        ),
        out_specs=(
            tokens, tokens, tokens, tokens, P(), P(),
            P(None, None, None, "tensor"), P(None, None, "tensor"), P(None, "tensor", None), P(),
            P(None, None, "tensor"), P(None, "tensor"), P(None, "tensor", None), P(),
        ),
        check_vma=False,
    )
```

```python
import functools

import jax
import jax.numpy as jnp
from jax import lax
from jax.experimental import pallas as pl
from jax.experimental.pallas import tpu as pltpu
from jax.sharding import PartitionSpec as P

HEAD = 64
PAIR = 2 * HEAD
EPSILON = 1e-05
MASKED_SCORE = -1000000000.0
FAR = 1e9
ROOT = 0.7978845608028654
CUBIC = 0.044715
BF16 = jnp.bfloat16
F32 = jnp.float32
VMEM_LIMIT = 18 * 1024 * 1024
BYTES = 3690000
NN = ((1,), (0,))
NT = ((1,), (1,))
TN = ((0,), (0,))
LARGE = 1 << 20
LONG = 40
STEP = 0.2
TAIL = 3
SLOTS = 4
NAMES = ("ffn_in", "ffn_out", "attn_in", "attn_out")
TOKEN = jax.ShapeDtypeStruct((8, 128), F32)


def dot(left, right, contract):
    return lax.dot_general(left, right, (contract, ((), ())), preferred_element_type=F32)


def shape(rows, columns, dtype):
    return jax.ShapeDtypeStruct((rows, columns), dtype)


NEAR = pl.BlockSpec(memory_space=pltpu.VMEM)
AWAY = pl.BlockSpec(memory_space=pl.ANY)
NUMBER = pl.BlockSpec(memory_space=pltpu.SMEM)


class Weight:
    def __init__(self, stack, layer):
        self.stack = stack
        self.layer = layer


class Place:
    def __init__(self, array):
        self.array = array


class Params:
    def __init__(self, *arrays):
        self.arrays = arrays


class Fetch:
    def __init__(self, source, buffer, semaphore):
        self.copy = pltpu.make_async_copy(source, buffer, semaphore)
        self.copy.start()
        self.buffer = buffer
        self.arrived = False

    def here(self):
        if not self.arrived:
            self.copy.wait()
            self.arrived = True
        return self.buffer


class Order:
    def __init__(self):
        self.token = None

    def call(
        self, body, outs, ins, microseconds=0.5, scratch=(), leave=(), away=(), aliases={},
        limit=VMEM_LIMIT,
    ):
        tokens = [] if self.token is None else [self.token]
        specs, args, weights, groups = [], [], [], []
        for value in ins:
            if isinstance(value, Params):
                groups.append(len(args))
                for array in value.arrays:
                    specs.append(NEAR)
                    args.append(pltpu.with_memory_space_constraint(array, pltpu.VMEM))
            elif isinstance(value, Place):
                specs.append(AWAY)
                args.append(pltpu.with_memory_space_constraint(value.array, pltpu.HBM))
            elif isinstance(value, Weight):
                weights.append((len(args), value))
                specs.append(AWAY)
                args.append(pltpu.with_memory_space_constraint(value.stack, pltpu.HBM))
            elif value.dtype == jnp.int32 and value.shape == (1,):
                specs.append(NUMBER)
                args.append(value)
            else:
                specs.append(NEAR)
                args.append(pltpu.with_memory_space_constraint(value, pltpu.VMEM))

        def wrapped(*refs):
            in_refs = list(refs[: len(args)])
            refs = refs[len(args) + len(tokens) :]
            out_refs = refs[: len(outs)]
            refs = refs[len(outs) + 1 :]
            if weights:
                semaphores = refs[-1]
                for i, (at, weight) in enumerate(weights):
                    in_refs[at] = Fetch(in_refs[at].at[weight.layer], refs[i], semaphores.at[i])
            for at in reversed(groups):
                in_refs[at : at + 6] = [in_refs[at : at + 6]]
            body(*in_refs, *out_refs, *refs[len(weights) : len(weights) + len(scratch)])

        buffers = [pltpu.VMEM(w.stack.shape[1:], w.stack.dtype) for unused, w in weights]
        semaphores = [pltpu.SemaphoreType.DMA((len(weights),))] if weights else []
        results = pl.pallas_call(
            wrapped,
            out_shape=[
                *[
                    o if i in leave or i in away else pltpu.VMEM(o.shape, o.dtype)
                    for i, o in enumerate(outs)
                ],
                TOKEN,
            ],
            in_specs=specs + [AWAY] * len(tokens),
            out_specs=[AWAY if i in away else NEAR for i in range(len(outs))] + [AWAY],
            scratch_shapes=[*buffers, *scratch, *semaphores],
            input_output_aliases=aliases,
            compiler_params=pltpu.CompilerParams(vmem_limit_bytes=limit),
            cost_estimate=pl.CostEstimate(
                flops=int(microseconds * 1.15e9), transcendentals=0, bytes_accessed=int(microseconds * BYTES)
            ),
        )(*args, *tokens)
        self.token = results[-1]
        return results[:-1]


def norm_parts(inputs):
    centre = inputs - jnp.mean(inputs, axis=-1, keepdims=True)
    inverse = lax.rsqrt(jnp.mean(centre * centre, axis=-1, keepdims=True) + EPSILON)
    return centre * inverse, inverse


def norm_back(gradient, normed, inverse, gain):
    scaled = gradient * gain
    mean_plain = jnp.mean(scaled, axis=-1, keepdims=True)
    mean_normed = jnp.mean(scaled * normed, axis=-1, keepdims=True)
    return inverse * (scaled - mean_plain - normed * mean_normed)


def column_sum(values):
    return jnp.sum(values.astype(F32), axis=0, keepdims=True)


def halves(count):
    half = count // 2
    return ((0, half), (half, 0))


def lane_half(which, rows):
    lanes = lax.broadcasted_iota(jnp.int32, (rows, PAIR), 1)
    return (lanes >= HEAD) if which else (lanes < HEAD)


def only_head(which, values):
    return jnp.where(lane_half(which, values.shape[0]), values, jnp.zeros_like(values))


def key_scores(key_pair, query_pair, which, key_at, query_at):
    scores = dot(only_head(which, key_pair), query_pair, NT)
    if query_at is None:
        return scores - key_at
    return jnp.where(key_at <= query_at, scores, MASKED_SCORE)


def attend(q_ref, k_ref, v_ref, key_at, query_at_ref, turned_ref, o_ref, log_ref):
    queries, local = q_ref.shape
    block = min(queries, 256)
    for pair in range(local // PAIR):
        columns = pl.ds(pair * PAIR, PAIR)
        key_pair = k_ref[:, columns]
        value_turned = v_ref[:, columns].astype(F32).T.astype(BF16)
        for start in range(0, queries, block):
            rows = pl.ds(start, block)
            query_pair = q_ref[rows, columns]
            query_at = None if query_at_ref is None else query_at_ref[:, rows]
            for which in range(2):
                head = 2 * pair + which
                scores = key_scores(key_pair, query_pair, which, key_at, query_at)
                top = jnp.max(scores, axis=0, keepdims=True)
                exponent = jnp.exp(scores - top)
                total = jnp.sum(exponent, axis=0, keepdims=True)
                weights = (exponent * (1.0 / total)).astype(BF16)
                log_ref[pl.ds(head, 1), rows] = top + jnp.log(total)
                mixed = dot(value_turned[which * HEAD : (which + 1) * HEAD], weights, NN)
                turned_ref[pl.ds(head * HEAD, HEAD), rows] = mixed.astype(BF16)
    o_ref[...] = turned_ref[...].astype(F32).T.astype(BF16)


def in_bias_rows(params, layer):
    return params[4][layer, 0:1], params[4][layer, 1:2]


def row_of(ref, index):
    return ref[index : index + 1]


def normalised(value, params, norm):
    normed, unused = norm_parts(value)
    return (normed * row_of(params[0], norm) + row_of(params[1], norm)).astype(BF16)


def column(row):
    return jnp.broadcast_to(row, (8, row.shape[1])).T[:, 0:1]


def own_first(row, here):
    half = row.shape[1] // 2
    return jnp.where(here == 0, row, jnp.concatenate([row[:, half:], row[:, :half]], axis=1))


def scaled_queries(hidden, w_in, bias):
    return ((dot(hidden, w_in[0], NN) + bias).astype(BF16) * HEAD ** (-0.5)).astype(BF16)


def load_body(*refs):
    count = len(refs) // 2
    copies = [
        pltpu.make_async_copy(refs[i], refs[count + i], refs[-1].at[i]) for i in range(count)
    ]
    for copy in copies:
        copy.start()
    for copy in copies:
        copy.wait()


def first_attention(norm, layer, own_ref, other_ref, params, w_in, w_out, key_at, query_at_ref, *refs):
    h_ref, q_ref, k_ref, v_ref, turned_ref, log_ref, base_ref, send_ref, o_ref = refs
    half = own_ref.shape[0]
    query_bias, value_bias = in_bias_rows(params, layer)
    for part, source in enumerate((own_ref, other_ref)):
        rows = pl.ds(part * half, half)
        hidden = normalised(source[...].astype(F32), params, norm)
        h_ref[rows] = hidden
        w = w_in.here()
        q_ref[rows] = scaled_queries(hidden, w, query_bias)
        k_ref[rows] = dot(hidden, w[1], NN).astype(BF16)
        v_ref[rows] = (dot(hidden, w[2], NN) + value_bias).astype(BF16)
    attend(q_ref, k_ref, v_ref, key_at, query_at_ref, turned_ref, o_ref, log_ref)
    w = w_out.here()
    for part, source in enumerate((own_ref, other_ref)):
        rows = pl.ds(part * half, half)
        partial = dot(o_ref[rows], w[...], NN)
        send_ref[rows] = partial.astype(BF16)
        base_ref[rows] = source[...].astype(F32) + row_of(params[2], layer) + partial


def enc_first_body(norm, layer, own_ref, other_ref, params, w_in, w_out, mask_ref, here_ref, place_ref, *refs):
    outs, key_at_ref, o_ref = refs[:-2], refs[-2], refs[-1]
    row = own_first(jnp.where(mask_ref[...] == 1, 0.0, FAR), here_ref[0])
    key_at = column(row)
    key_at_ref[...] = key_at
    first_attention(norm, layer, own_ref, other_ref, params, w_in, w_out, key_at, None, *outs, o_ref)


def dec_first_body(
    norm, layer, own_ref, other_ref, params, w_in, w_out, mask_ref, here_ref,
    cot_ref, loss_ref, objective_ref, place_ref, *refs
):
    outs, (key_at_ref, query_at_ref, gradient_ref, gradient_send_ref, o_ref) = refs[:-5], refs[-5:]
    count = mask_ref.shape[1]
    position = own_first(
        lax.broadcasted_iota(jnp.int32, (1, count), 1).astype(F32), here_ref[0]
    )
    row = jnp.where(own_first(mask_ref[...].astype(F32), here_ref[0]) == 1.0, position, FAR)
    key_at = column(row)
    key_at_ref[...] = key_at
    query_at_ref[...] = position
    flag = objective_ref[0].astype(F32)
    weight = column(0.25 + 0.75 * loss_ref[...].astype(F32)) * (0.5 + 0.5 * flag)
    gradient = cot_ref[...].astype(F32) * weight
    gradient_ref[...] = gradient
    gradient_send_ref[...] = gradient.astype(BF16)
    first_attention(
        norm, layer, own_ref, other_ref, params, w_in, w_out, key_at, query_at_ref, *outs, o_ref
    )


def cross_attention_body(
    norm, layer, before_ref, recv_ref, params, w_in, w_out, k_ref, v_ref, key_at_ref,
    x_ref, h_ref, q_ref, turned_ref, log_ref, base_ref, send_ref, o_ref,
):
    count = x_ref.shape[0]
    half = count // 2
    query_bias, unused = in_bias_rows(params, layer)
    for mine, theirs in halves(count):
        rows = pl.ds(mine, half)
        value = before_ref[rows] + recv_ref[pl.ds(theirs, half)].astype(F32)
        x_ref[rows] = value
        hidden = normalised(value, params, norm)
        h_ref[rows] = hidden
        q_ref[rows] = scaled_queries(hidden, w_in.here(), query_bias)
    attend(q_ref, k_ref, v_ref, key_at_ref[...], None, turned_ref, o_ref, log_ref)
    partial = dot(o_ref[...], w_out.here()[...], NN)
    send_ref[...] = partial.astype(BF16)
    base_ref[...] = x_ref[...] + row_of(params[2], layer) + partial


def memory_body(layer, before_ref, recv_ref, params, w_in, mem_ref, k_ref, v_ref, out_ref):
    count = mem_ref.shape[0]
    half = count // 2
    unused, value_bias = in_bias_rows(params, layer)
    for mine, theirs in halves(count):
        rows = pl.ds(mine, half)
        memory = (before_ref[rows] + recv_ref[pl.ds(theirs, half)].astype(F32)).astype(BF16)
        mem_ref[rows] = memory
        if mine == 0:
            out_ref[...] = memory
        w = w_in.here()
        k_ref[rows] = dot(memory, w[1], NN).astype(BF16)
        v_ref[rows] = (dot(memory, w[2], NN) + value_bias).astype(BF16)


def feed_body(
    norm, layer, last, before_ref, recv_ref, params, w_one, w_two,
    x_ref, h_ref, f_ref, slope_ref, base_ref, send_ref,
):
    count = x_ref.shape[0]
    half = count // 2
    for mine, theirs in halves(count):
        rows = pl.ds(mine, half)
        value = before_ref[rows] + recv_ref[pl.ds(theirs, half)].astype(F32)
        x_ref[rows] = value
        hidden = normalised(value, params, norm)
        h_ref[rows] = hidden
        u = dot(hidden, w_one.here()[...], NN) + row_of(params[5], layer)
        square = u * u
        bent = jnp.tanh(u * (ROOT + (ROOT * CUBIC) * square))
        upper = 0.5 + 0.5 * bent
        active = (u * upper).astype(BF16)
        f_ref[rows] = active
        slope = upper + (0.5 * u) * (1.0 - bent * bent) * (ROOT + (3 * ROOT * CUBIC) * square)
        slope_ref[rows] = slope.astype(BF16)
        partial = dot(active, w_two.here()[...], NN)
        if not last:
            send_ref[rows] = partial.astype(BF16)
            base_ref[rows] = value + row_of(params[3], layer) + partial
        elif mine == 0:
            base_ref[...] = value + row_of(params[3], layer) + partial
        else:
            send_ref[...] = partial.astype(BF16)


def feed_back_rows(
    gradient, rows, w_one, w_two, slope_ref, g_ref, low_ref, du_ref, base_ref, send_ref
):
    g_ref[rows] = gradient
    low = gradient.astype(BF16)
    low_ref[rows] = low
    du = (dot(low, w_two.here()[...], NT) * slope_ref[rows].astype(F32)).astype(BF16)
    du_ref[rows] = du
    partial = dot(du, w_one.here()[...], NT)
    send_ref[rows] = partial.astype(BF16)
    base_ref[rows] = partial


def dec_feed_back_body(own_ref, other_ref, w_one, w_two, slope_ref, *outs):
    half = own_ref.shape[0]
    for part, source in enumerate((own_ref, other_ref)):
        feed_back_rows(
            source[...].astype(F32), pl.ds(part * half, half), w_one, w_two, slope_ref, *outs
        )


def source_seed(cot_ref, objective_ref):
    return cot_ref[...].astype(F32) * (1.0 - 0.5 * objective_ref[0].astype(F32))


def enc_feed_back_body(seed_ref, objective_ref, mem_base_ref, recv_ref, w_one, w_two, slope_ref, *outs):
    half = seed_ref.shape[0]
    own, other = pl.ds(0, half), pl.ds(half, half)
    for rows, theirs in ((own, other), (other, own)):
        gradient = mem_base_ref[rows] + recv_ref[theirs].astype(F32)
        if rows is own:
            gradient = gradient + source_seed(seed_ref, objective_ref)
        feed_back_rows(gradient, rows, w_one, w_two, slope_ref, *outs)


def attention_back_body(norm, cross, causal, *refs):
    (g_in_ref, dh_ref, dh_recv_ref, x_ref, params, w_in, w_out, q_ref, k_ref, v_ref, log_ref,
     key_at_ref), refs = refs[:12], refs[12:]
    query_at_ref = seed_ref = mem_base_ref = mem_send_ref = None
    if causal:
        query_at_ref, refs = refs[0], refs[1:]
    if cross:
        (seed_ref, objective_ref), refs = refs[:2], refs[2:]
    (g_ref, low_ref, dq_ref, dk_ref, dv_ref, base_ref, send_ref), refs = refs[:7], refs[7:]
    if cross:
        (mem_base_ref, mem_send_ref), refs = refs[:2], refs[2:]
    sums_ref, do_ref, turned_ref = refs
    gain = row_of(params[0], norm)
    count, local = dq_ref.shape
    half = count // 2
    for part, (mine, theirs) in enumerate(halves(count)):
        rows = pl.ds(mine, half)
        normed, inverse = norm_parts(x_ref[rows])
        dh = dh_ref[rows] + dh_recv_ref[pl.ds(theirs, half)].astype(F32)
        gradient = g_in_ref[rows] + norm_back(dh, normed, inverse, gain)
        g_ref[rows] = gradient
        low = gradient.astype(BF16)
        low_ref[rows] = low
        if part == 0:
            sums_ref[0:1] = column_sum(dh * normed)
            sums_ref[1:2] = column_sum(dh)
            sums_ref[2:3] = column_sum(low)
        do_ref[rows] = dot(low, w_out.here()[...], NT).astype(BF16)
    key_at = key_at_ref[...]
    block = min(count, 256)
    keys = k_ref.shape[0]
    for pair in range(local // PAIR):
        columns = pl.ds(pair * PAIR, PAIR)
        key_pair = k_ref[:, columns]
        key_turned = key_pair.astype(F32).T.astype(BF16)
        value_pair = v_ref[:, columns]
        dk = [None, None]
        dv = [None, None]
        for start in range(0, count, block):
            rows = pl.ds(start, block)
            query_pair = q_ref[rows, columns]
            do_pair = do_ref[rows, columns]
            query_at = None if query_at_ref is None else query_at_ref[:, rows]
            for which in range(2):
                head = 2 * pair + which
                scores = key_scores(key_pair, query_pair, which, key_at, query_at)
                probs = jnp.exp(scores - log_ref[pl.ds(head, 1), rows])
                prob_grad = dot(only_head(which, value_pair), do_pair, NT)
                product = probs * prob_grad
                inner = jnp.sum(product, axis=0, keepdims=True)
                score_grad = (product - probs * inner).astype(BF16)
                dv_part = dot(probs.astype(BF16), do_pair, NN)
                dk_part = dot(score_grad, query_pair, NN)
                dq_part = dot(key_turned[which * HEAD : (which + 1) * HEAD], score_grad, NN)
                turned_ref[pl.ds(head * HEAD, HEAD), rows] = dq_part * HEAD ** (-0.5)
                dk[which] = dk_part if dk[which] is None else dk[which] + dk_part
                dv[which] = dv_part if dv[which] is None else dv[which] + dv_part
        first = lane_half(0, keys)
        dk_ref[:, columns] = jnp.where(first, dk[0], dk[1]).astype(BF16)
        dv_ref[:, columns] = jnp.where(first, dv[0], dv[1]).astype(BF16)
    dq_ref[...] = turned_ref[...].T.astype(BF16)
    w = w_in.here()
    if cross:
        partial = dot(dk_ref[...], w[1], NT) + dot(dv_ref[...], w[2], NT)
        mem_base_ref[...] = partial
        mem_half = keys // 2
        mem_send_ref[0:mem_half] = (
            partial[0:mem_half] + source_seed(seed_ref, objective_ref)
        ).astype(BF16)
        mem_send_ref[mem_half:] = partial[mem_half:].astype(BF16)
        partial = dot(dq_ref[...], w[0], NT)
        send_ref[...] = partial.astype(BF16)
        base_ref[...] = partial
    else:
        for part in (1, 0):
            rows = pl.ds(part * half, half)
            partial = (
                dot(dq_ref[rows], w[0], NT)
                + dot(dk_ref[rows], w[1], NT)
                + dot(dv_ref[rows], w[2], NT)
            )
            if part == 1:
                send_ref[...] = partial.astype(BF16)
            else:
                base_ref[...] = partial


def last_norm_body(norm, g_ref, dh_ref, recv_ref, x_ref, params, out_ref, sums_ref):
    normed, inverse = norm_parts(x_ref[...].astype(F32))
    dh = dh_ref[...] + recv_ref[...].astype(F32)
    sums_ref[0:1] = column_sum(dh * normed)
    sums_ref[1:2] = column_sum(dh)
    half = out_ref.shape[0]
    result = g_ref[0:half] + norm_back(dh, normed, inverse, row_of(params[0], norm))
    out_ref[...] = result.reshape(out_ref.shape)


def feed_weights_body(h_ref, du_ref, f_ref, low_ref, place_ref, send_ref, keep_ref, sums_ref, hidden_sums_ref):
    bit = bit_of(place_ref, 0)
    width = h_ref.shape[1]
    part = width // 2
    for which, out_ref in ((1 - bit, send_ref), (bit, keep_ref)):
        left = h_ref[:, pl.ds(pl.multiple_of(which * part, 128), part)]
        for side in range(2):
            out_ref[pl.ds(side * part, part)] = dot(
                left, du_ref[:, pl.ds(side * width, width)], TN
            ).astype(BF16)
        left = f_ref[:, pl.ds(pl.multiple_of(which * width, 128), width)]
        out_ref[pl.ds(width, width)] = dot(left, low_ref[...], TN).astype(BF16)
    half = low_ref.shape[0] // 2
    sums_ref[...] = column_sum(low_ref[0:half])
    hidden_sums_ref[...] = column_sum(du_ref[...])


def attention_weights_body(
    h_ref, mem_ref, dq_ref, dk_ref, dv_ref, turned_ref, low_ref, place_ref, *refs
):
    later_ref, refs = (refs[0], refs[1:]) if len(refs) == 5 else (None, refs)
    send_ref, keep_ref, sums_ref = refs[:3]
    if later_ref is not None:
        refs[3][...] = later_ref[...]
    bit = bit_of(place_ref, 0)
    width = h_ref.shape[1]
    part = width // 2
    quarter = width // 4
    left_side = pl.ds(0, part)
    right_side = pl.ds(part, part)
    for which, out_ref in ((1 - bit, send_ref), (bit, keep_ref)):
        columns = pl.ds(pl.multiple_of(which * part, 128), part)
        out_ref[pl.ds(0, part), left_side] = dot(h_ref[:, columns], dq_ref[...], TN).astype(BF16)
        memory = mem_ref[:, columns]
        out_ref[pl.ds(0, part), right_side] = dot(memory, dk_ref[...], TN).astype(BF16)
        values = dot(memory, dv_ref[...], TN).astype(BF16)
        out_ref[pl.ds(part, quarter), left_side] = values[:quarter]
        out_ref[pl.ds(part, quarter), right_side] = values[quarter:]
        rows = pl.ds(pl.multiple_of(which * quarter, 64), quarter)
        out_ref[pl.ds(part + quarter, quarter)] = dot(turned_ref[rows], low_ref[...], NN).astype(BF16)
    sums_ref[:, left_side] = column_sum(dq_ref[...])
    sums_ref[:, right_side] = column_sum(dv_ref[...])


def bit_of(place_ref, step):
    return (place_ref[0] >> step) & 1


def add_body(step, layout, place_ref, *refs):
    send_ref, next_ref = refs[-2:]
    bit = bit_of(place_ref, step)
    for out_ref, which in ((send_ref, 1 - bit), (next_ref, bit)):
        target = 0
        for i, (first, segments) in enumerate(layout):
            keep_ref, received_ref = refs[2 * i], refs[2 * i + 1]
            for rows in segments:
                half = rows // 2
                block = half
                while block % 32 == 0 and block > 128:
                    block //= 2
                for start in range(0, half, block):
                    part = pl.ds(pl.multiple_of(first + which * half + start, 8), block)
                    out_ref[pl.ds(target + start, block)] = (
                        keep_ref[part].astype(F32) + received_ref[part].astype(F32)
                    ).astype(BF16)
                first += rows
                target += half


def last_sum_body(keep_ref, received_ref, out_ref):
    out_ref[...] = (keep_ref[...].astype(F32) + received_ref[...].astype(F32)).astype(BF16)


def join_body(first_ref, second_ref, out_ref):
    rows = first_ref.shape[0]
    out_ref[0:rows] = first_ref[...]
    out_ref[rows:] = second_ref[...]


def put_body(groups, masks, count, bits, old, place_ref, *refs):
    blocks, refs = refs[:count], refs[count + old :]
    outs = dict(zip(NAMES, refs[:4]))
    wide_ref, semaphores = refs[4:]
    width = blocks[0].shape[1]
    part, quarter = width // 2, width // 4
    slots = wide_ref.shape[0]
    flying = []

    def copy(slot, side, rows, target):
        source = wide_ref.at[slot, pl.ds(0, rows), pl.ds(side * part, part)]
        return pltpu.make_async_copy(source, target, semaphores.at[slot, side])

    def wait(slot, rows):
        for side in range(2):
            target = outs["ffn_out"].at[0, pl.ds(0, rows), pl.ds(0, part)]
            copy(slot, side, rows, target).wait()

    each = len(masks) // count
    for number, mask in enumerate(masks):
        block_ref = blocks[number // each]
        if number % each == 0:
            at = 0
        device = place_ref[0] ^ mask
        upper = device & 1
        for kind, layer, rows in groups:
            slot = len(flying) % slots
            if len(flying) >= slots:
                wait(*flying[-slots])
            flying.append((slot, rows))
            wide_ref[slot, pl.ds(0, rows)] = block_ref[pl.ds(at, rows)].astype(F32)
            at += rows
            inner = 0
            for bit in range(1, bits):
                inner = inner + ((device >> bit) & 1) * (rows << (bits - 1 - bit))

            def send(side, target):
                copy(slot, side, rows, target).start()

            if kind == "in":
                row = pl.multiple_of(upper * part + lax.rem(inner, part), 8)
                column = lax.div(inner, part) * width
                for side in range(2):
                    columns = pl.ds(pl.multiple_of(column + side * part, 128), part)
                    send(side, outs["ffn_in"].at[layer, pl.ds(row, rows), columns])
            elif kind == "out":
                row = pl.multiple_of(upper * width + inner, 8)
                for side in range(2):
                    columns = pl.ds(side * part, part)
                    send(side, outs["ffn_out"].at[layer, pl.ds(row, rows), columns])
            else:

                @pl.when(inner < part)
                def query_and_key():
                    row = pl.multiple_of(upper * part + inner, 8)
                    for side in range(2):
                        send(side, outs["attn_in"].at[layer, side, pl.ds(row, rows)])

                @pl.when((inner >= part) & (inner < part + quarter))
                def value():
                    row = upper * part + inner - part
                    for side in range(2):
                        target = pl.ds(pl.multiple_of(row + side * quarter, 8), rows)
                        send(side, outs["attn_in"].at[layer, 2, target])

                @pl.when(inner >= part + quarter)
                def output():
                    row = pl.multiple_of(upper * quarter + inner - part - quarter, 8)
                    for side in range(2):
                        columns = pl.ds(side * part, part)
                        send(side, outs["attn_out"].at[layer, pl.ds(row, rows), columns])

    for slot, rows in flying[-slots:]:
        wait(slot, rows)


def pack_body(*refs):
    norm_refs, out_refs, rows_refs, wide_refs = refs[:5], refs[5:7], refs[7:10], refs[10:12]
    shared_ref, apart_ref = refs[12:]
    shared_ref[...] = jnp.zeros_like(shared_ref)
    apart_ref[...] = jnp.zeros_like(apart_ref)
    for i, ref in enumerate(norm_refs):
        shared_ref[i : i + 1] = ref[0:1]
        shared_ref[5 + i : 6 + i] = ref[1:2]
    for i, source in enumerate((1, 3, 4)):
        shared_ref[10 + i : 11 + i] = norm_refs[source][2:3]
    for i, ref in enumerate(out_refs):
        shared_ref[13 + i : 14 + i] = ref[...]
    for i, ref in enumerate(rows_refs):
        apart_ref[i : i + 1] = ref[...]
    width = shared_ref.shape[1]
    for i, ref in enumerate(wide_refs):
        for side in range(2):
            apart_ref[3 + 2 * i + side : 4 + 2 * i + side] = ref[:, side * width : (side + 1) * width]


def pair_small_body(shared_ref, received_ref, apart_ref, out_ref):
    out_ref[0:16] = shared_ref[...] + received_ref[...]
    out_ref[16:24] = apart_ref[...]


def add_small_body(first_ref, second_ref, out_ref):
    out_ref[...] = first_ref[...] + second_ref[...]


def last_small_body(first_ref, second_ref, *outs):
    total = first_ref[...] + second_ref[...]
    gain_ref, offset_ref, out_bias_ref, two_ref, in_ref, one_ref = outs
    gain_ref[...] = total[0:5]
    offset_ref[...] = total[5:10]
    out_bias_ref[...] = total[10:13]
    two_ref[...] = total[13:15]
    width = total.shape[1]
    part = width // 2
    for i in range(3):
        for side in range(2):
            in_ref[i, side : side + 1] = total[16 + i : 17 + i, side * part : (side + 1) * part]
    for i in range(2):
        for side in range(2):
            row = 19 + 2 * i + side
            one_ref[i : i + 1, side * width : (side + 1) * width] = total[row : row + 1]


def decoded_body(base_ref, received_ref, out_ref):
    out_ref[...] = (base_ref[...] + received_ref[...].astype(F32)).astype(BF16)


def pass_body(value_ref, unused_ref, out_ref):
    out_ref[...] = value_ref[...]


def swap(values):
    return lax.ppermute(values, "tensor", [(0, 1), (1, 0)])


def across(values, stride):
    count = lax.axis_size("dp")
    return lax.ppermute(values, "dp", [(i, i ^ stride) for i in range(count)])


def dp_bits():
    return lax.axis_size("dp").bit_length() - 1


class Total:
    def __init__(self, order, place, parts, step=1):
        self.order = order
        self.place = place
        self.parts = parts
        self.step = step

    def merge(self, *others):
        assert all(self.step == other.step for other in others)
        return Total(
            self.order, self.place, self.parts + sum((other.parts for other in others), []), self.step
        )

    def finish(self, microseconds=0.2):
        while self.step < dp_bits():
            self.next()
        ((self.groups, keep, received, unused),) = self.parts
        (self.shard,) = self.order.call(
            last_sum_body, [shape(*keep.shape, BF16)], [keep, received], microseconds=microseconds
        )

    def next(self, microseconds=0.5):
        if self.step == dp_bits():
            return
        width = self.parts[0][1].shape[1]
        layout = [
            (first, [rows for unused, unused, rows in groups])
            for groups, unused, unused, first in self.parts
        ]
        rows = sum(sum(segments) for unused, segments in layout) // 2
        send, keep = self.order.call(
            functools.partial(add_body, self.step, layout), [shape(rows, width, BF16)] * 2,
            [self.place, *[value for unused, *pair, unused in self.parts for value in pair]],
            microseconds=microseconds,
        )
        groups = [
            (kind, layer, rows // 2)
            for members, *unused in self.parts
            for kind, layer, rows in members
        ]
        self.parts = [(groups, keep, across(send, 1 << self.step), 0)]
        self.step += 1


class Gathered:
    def __init__(self, total, stacks, microseconds=TAIL):
        self.order = total.order
        self.place = total.place
        self.stacks = stacks
        total.finish(microseconds)
        self.groups = total.groups
        self.stages = self.run(total.shard)
        self.next()

    def next(self):
        next(self.stages, None)

    def run(self, block):
        order = self.order
        masks = [0]
        for bit in range(dp_bits() - 1, 0, -1):
            received = across(block, 1 << bit)
            if bit > 1:
                yield
                (block,) = order.call(
                    join_body, [shape(2 * block.shape[0], block.shape[1], BF16)], [block, received],
                    microseconds=TAIL,
                )
                masks += [mask ^ (1 << bit) for mask in masks]
        other = across(block, 1)
        yield
        last = across(received, 1)
        crossed = [mask ^ 2 for mask in masks]
        self.put([block, received], masks + crossed)
        yield
        self.put([other], [mask ^ 1 for mask in masks])
        yield
        self.put([last], [mask ^ 1 for mask in crossed])
        yield

    def put(self, blocks, masks):
        stacks = self.stacks
        old = [stacks[name] for name in NAMES] if NAMES[0] in stacks else []
        rows = max(rows for unused, unused, rows in self.groups)
        results = self.order.call(
            functools.partial(put_body, self.groups, masks, len(blocks), dp_bits(), len(old)),
            [jax.ShapeDtypeStruct(stacks["shapes"][name], F32) for name in NAMES],
            [self.place, *blocks, *[Place(value) for value in old]],
            aliases={1 + len(blocks) + i: i for i in range(len(old))},
            away=range(4),
            microseconds=TAIL,
            scratch=[
                pltpu.VMEM((6, rows, blocks[0].shape[1]), F32),
                pltpu.SemaphoreType.DMA((6, 2)),
            ],
        )
        stacks.update(zip(NAMES, results))


class SmallTotal:
    def __init__(self, order, place, shapes, ins):
        self.order = order
        self.place = place
        self.shapes = shapes
        self.results = None
        width = ins[0].shape[1]
        self.shared, self.apart = order.call(
            pack_body, [shape(16, width, F32), shape(8, width, F32)], ins
        )
        self.received = swap(self.shared)
        self.stages = self.run()

    def next(self):
        next(self.stages, None)

    def run(self):
        order, bits = self.order, dp_bits()
        whole = shape(24, self.shared.shape[1], F32)
        (value,) = order.call(pair_small_body, [whole], [self.shared, self.received, self.apart], microseconds=TAIL)
        for bit in range(bits):
            received = across(value, 1 << bit)
            yield
            if bit + 1 < bits:
                (value,) = order.call(add_small_body, [whole], [value, received], microseconds=TAIL)
        self.results = order.call(
            last_small_body, [jax.ShapeDtypeStruct(dims, F32) for dims in self.shapes],
            [value, received], leave=range(6),
        )
        yield


def on_device(
    src_embed, tgt_embed, src_mask, tgt_mask, objective, loss_mask, enc_cot, dec_cot,
    norm_gain, norm_bias, attn_in, attn_in_bias, attn_out, attn_out_bias,
    ffn_in, ffn_in_bias, ffn_out, ffn_out_bias,
):
    order = Order()
    here = lax.axis_index("tensor")
    width = src_embed.shape[2]
    local = attn_in.shape[3]
    hidden_width = ffn_in.shape[2]
    source_own = src_embed.reshape(-1, width)
    target_own = tgt_embed.reshape(-1, width)
    sources = 2 * source_own.shape[0]
    targets = 2 * target_own.shape[0]
    enc_own = enc_cot.reshape(-1, width)
    target_other = swap(target_own)
    source_other = swap(source_own)
    loaded = [
        source_own, target_own, dec_cot.reshape(-1, width), loss_mask, src_mask, tgt_mask, enc_own,
        norm_gain, norm_bias, attn_out_bias, ffn_out_bias, attn_in_bias, ffn_in_bias,
    ]
    source_near, target_near, dec_cot_near, loss_near, src_mask_near, tgt_mask_near, enc_own, *small_near = order.call(
        load_body, [jax.ShapeDtypeStruct(a.shape, a.dtype) for a in loaded],
        [Place(a) for a in loaded], scratch=[pltpu.SemaphoreType.DMA((len(loaded),))],
    )
    params = Params(*small_near)
    core = lax.axis_index("dp").astype(jnp.int32).reshape(1)
    here = here.astype(jnp.int32).reshape(1)

    def first(body, own, other, norm, layer, mask, more_ins, more_outs):
        count = 2 * own.shape[0]
        narrow = shape(count, local, BF16)
        return order.call(
            functools.partial(body, norm, layer),
            [
                shape(count, width, BF16), narrow, narrow, narrow,
                shape(local, count, BF16), shape(8, count, F32),
                shape(count, width, F32), shape(count, width, BF16), shape(count, 1, F32),
                *more_outs,
            ],
            [own, other, params, Weight(attn_in, layer), Weight(attn_out, layer), mask, here, *more_ins],
            microseconds=LONG,
            scratch=[pltpu.VMEM((count, local), BF16)],
        )

    def feed(before, recv, norm, layer, last):
        count = before.shape[0]
        sent = count // 2 if last else count
        return order.call(
            functools.partial(feed_body, norm, layer, last),
            [
                shape(count, width, F32), shape(count, width, BF16),
                shape(count, hidden_width, BF16), shape(count, hidden_width, BF16),
                shape(sent, width, F32), shape(sent, width, BF16),
            ],
            [before, recv, params, Weight(ffn_in, layer), Weight(ffn_out, layer)],
            microseconds=LONG,
        )

    h0, q0, k0, v0, turned0, log0, base0, send0, source_keys = first(
        enc_first_body, source_near, source_other, 0, 0, src_mask_near, [core], []
    )
    (
        h2, q1, k1, v1, turned1, log1, base1, send1, target_keys,
        target_queries, dec_own, dec_send,
    ) = first(
        dec_first_body, target_near, target_other, 2, 1, tgt_mask_near,
        [dec_cot_near, loss_near, objective, core],
        [shape(1, targets, F32), shape(targets // 2, width, F32), shape(targets // 2, width, BF16)],
    )
    recv1 = swap(send1)
    dec_other = swap(dec_send)
    recv0 = swap(send0)
    x1, h1, f0, slope0, base2, send2 = feed(base0, recv0, 1, 0, False)
    recv2 = swap(send2)
    narrow = shape(sources, local, BF16)
    memory, k2, v2, encoded = order.call(
        functools.partial(memory_body, 2),
        [shape(sources, width, BF16), narrow, narrow, shape(sources // 2, width, BF16)],
        [base2, recv2, params, Weight(attn_in, 2)], microseconds=3, leave=[3],
    )
    x3, h3, q2, turned2, log2, base3, send3 = order.call(
        functools.partial(cross_attention_body, 3, 2),
        [
            shape(targets, width, F32), shape(targets, width, BF16),
            shape(targets, local, BF16), shape(local, targets, BF16), shape(8, targets, F32),
            shape(targets, width, F32), shape(targets, width, BF16),
        ],
        [
            base1, recv1, params, Weight(attn_in, 2), Weight(attn_out, 2), k2, v2, source_keys,
        ],
        microseconds=5,
        scratch=[pltpu.VMEM((targets, local), BF16)],
    )
    recv3 = swap(send3)
    x4, h4, f1, slope1, base4, send4 = feed(base3, recv3, 4, 1, True)

    def feed_back(body, layer, *ins):
        count = ins[-1].shape[0]
        return order.call(
            body,
            [
                shape(count, width, F32), shape(count, width, BF16),
                shape(count, hidden_width, BF16),
                shape(count, width, F32), shape(count, width, BF16),
            ],
            [*ins[:-1], Weight(ffn_in, layer), Weight(ffn_out, layer), ins[-1]],
            microseconds=LONG,
        )

    def attention_back(cross, causal, g, dh, recv, x, norm, layer, q, k, v, log, key_at, *more):
        count = q.shape[0]
        keys = k.shape[0]
        outs = [
            shape(count, width, F32), shape(count, width, BF16),
            shape(count, local, BF16), shape(keys, local, BF16), shape(keys, local, BF16),
        ]
        if cross:
            outs += [
                shape(count, width, F32), shape(count, width, BF16),
                shape(keys, width, F32), shape(keys, width, BF16),
            ]
        else:
            outs += [shape(count // 2, width, F32), shape(count // 2, width, BF16)]
        outs += [shape(3, width, F32)]
        return order.call(
            functools.partial(attention_back_body, norm, cross, causal), outs,
            [
                g, dh, recv, x, params, Weight(attn_in, layer), Weight(attn_out, layer),
                q, k, v, log, key_at, *more,
            ],
            microseconds=LONG,
            scratch=[pltpu.VMEM((count, local), BF16), pltpu.VMEM((local, count), F32)],
        )

    def feed_weights(layer, h, du, f, low):
        out = shape(2 * width, width, BF16)
        send, keep, sums, hidden_sums = order.call(
            feed_weights_body, [out, out, shape(1, width, F32), shape(1, hidden_width, F32)],
            [h, du, f, low, core], microseconds=2 if layer == 0 else LONG,
        )
        received = across(send, 1)
        groups = [("in", layer, width), ("out", layer, width)]
        return Total(order, core, [(groups, keep, received, 0)]), sums, hidden_sums

    def attention_weights(layer, h, mem, dq, dk, dv, turned, low, *later):
        out = shape(width, width, BF16)
        send, keep, sums, *passed = order.call(
            attention_weights_body,
            [out, out, shape(1, width, F32), *[shape(*value.shape, BF16) for value in later]],
            [h, mem, dq, dk, dv, turned, low, core, *later], microseconds=2,
        )
        total = Total(order, core, [([("attention", layer, width)], keep, across(send, 1), 0)])
        return total, sums, *passed

    def last_norm(g, dh, recv, own, norm):
        rows = own.shape[0]
        return order.call(
            functools.partial(last_norm_body, norm),
            [jax.ShapeDtypeStruct((rows, 1, width), F32), shape(2, width, F32)],
            [g, dh, recv, own, params], leave=[0],
        )

    shapes = (ffn_in.shape, ffn_out.shape, attn_in.shape, attn_out.shape)
    stacks = {"shapes": dict(zip(NAMES, shapes))}
    g4, low4, du1, dh4, dh4_send = feed_back(
        dec_feed_back_body, 1, dec_own, dec_other, slope1
    )
    dh4_recv = swap(dh4_send)
    feed1, two1, one1 = feed_weights(1, h4, du1, f1, low4)
    feed1.next()
    g3, low3, dq2, dk2, dv2, dh3, dh3_send, mem_grad, mem_send, sums4 = attention_back(
        True, False, g4, dh4, dh4_recv, x4, 4, 2, q2, k2, v2, log2, source_keys, enc_own, objective
    )
    mem_recv = swap(mem_send)
    cross, bias2, dh3_later = attention_weights(
        2, h3, memory, dq2, dk2, dv2, turned2, low3, dh3_send
    )
    dh3_recv = swap(dh3_later)
    feed1.next(LONG)
    cross.next()
    g1, low1, du0, dh1, dh1_send = feed_back(
        enc_feed_back_body, 0, enc_own, objective, mem_grad, mem_recv, slope0
    )
    dh1_recv = swap(dh1_send)
    feed0, two0, one0 = feed_weights(0, h1, du0, f0, low1)
    cross.next()
    g2, low2, dq1, dk1, dv1, dh2, dh2_send, sums3 = attention_back(
        False, True, g3, dh3, dh3_recv, x3, 3, 1, q1, k1, v1, log1, target_keys, target_queries
    )
    dh2_recv = swap(dh2_send)
    first1, bias1 = attention_weights(1, h2, h2, dq1, dk1, dv1, turned1, low2)
    feed0.next()
    early = feed1.merge(cross)
    early.next()
    g0, low0, dq0, dk0, dv0, dh0, dh0_send, sums1 = attention_back(
        False, False, g1, dh1, dh1_recv, x1, 1, 0, q0, k0, v0, log0, source_keys
    )
    dh0_recv = swap(dh0_send)
    first0, bias0 = attention_weights(0, h0, h0, dq0, dk0, dv0, turned0, low0)
    feed0.next(TAIL)
    early = Gathered(early, stacks, LONG)
    late = first1.merge(first0)
    late.next(TAIL)
    source_grad, sums0 = last_norm(g0, dh0, dh0_recv, source_near, 0)
    target_grad, sums2 = last_norm(g2, dh2, dh2_recv, target_near, 2)
    small = SmallTotal(
        order, core,
        [
            norm_gain.shape, norm_bias.shape, attn_out_bias.shape, ffn_out_bias.shape,
            attn_in_bias.shape, ffn_in_bias.shape,
        ],
        [sums0, sums1, sums2, sums3, sums4, two0, two1, bias0, bias1, bias2, one0, one1],
    )
    early.next()
    feed0.next(TAIL)
    late.next(TAIL)
    small.next()
    early.next()
    feed0 = Gathered(feed0, stacks)
    feed0.next()
    late.next(TAIL)
    small.next()
    feed0.next()
    late = Gathered(late, stacks)
    late.next()
    small.next()
    early.next()
    late.next()
    early.next()
    small.next()
    feed0.next()
    feed0.next()
    decoded_other = swap(send4)
    (decoded,) = order.call(
        decoded_body, [shape(targets // 2, width, BF16)], [base4, decoded_other], leave=[0]
    )
    small.next()
    late.next()
    late.next()
    for unused in range(dp_bits() + 4):
        for group in (early, feed0, late, small):
            group.next()
    gains, offsets, out_biases, two_biases, in_biases, one_biases = small.results
    return (
        encoded[:, None],
        decoded[:, None],
        source_grad,
        target_grad,
        gains,
        offsets,
        stacks["attn_in"],
        in_biases,
        stacks["attn_out"],
        out_biases,
        stacks["ffn_in"],
        one_biases,
        stacks["ffn_out"],
        two_biases,
    )


def solution(mesh):
    tokens = P("tensor", "dp", None)
    return jax.shard_map(
        on_device,
        mesh=mesh,
        in_specs=(
            tokens, tokens, P("dp", None), P("dp", None), P("dp"), P("dp", "tensor"),
            tokens, tokens, P(), P(),
            P(None, None, None, "tensor"), P(None, None, "tensor"), P(None, "tensor", None), P(),
            P(None, None, "tensor"), P(None, "tensor"), P(None, "tensor", None), P(),
        ),
        out_specs=(
            tokens, tokens, tokens, tokens, P(), P(),
            P(None, None, None, "tensor"), P(None, None, "tensor"), P(None, "tensor", None), P(),
            P(None, None, "tensor"), P(None, "tensor"), P(None, "tensor", None), P(),
        ),
        check_vma=False,
    )
```
